128 devices in a mesh: state: 32 (over x, y, core), mem: 4 (over z).
Axes of the slice: x: 4, y: 4, z: 4, core: 2. Of those that a mesh axis runs over, the one named last changes fastest.
Arguments:
- ensemble: bfloat16 [80, 1048576], P('mem', 'state'), may hold values from -6 to 6
- weights: bfloat16 [8192, 12, 128], P('state'), may hold values from 0 to 0.14941406
- seg_obs: int32 [8192, 12], P('state'), may hold values from 0 to 65535, as said below
- observed: float32 [65536], replicated, may hold values from -180 to 180
- inv_var: float32 [65536], replicated, may hold values from 0.0001 to 0.001
Outputs:
- analysis: bfloat16 [80, 1048576], P('mem', 'state')
The draws below stay inside these ranges and needn't reach their ends.
Inputs may be any that keep to these rules, and one draw needn't show every extreme that they name: seg_obs names the observation that a slot's arc segment contributes to. Of the 3072 slots of the tiles of one index of state, exactly 96 name observations in each aligned block of 2048 observations; an observation may have any number of slots, or none.
All inputs are finite; a program needn't handle non-finite values.
Results may differ from the reference program's by a relative error of at most 0.0051.
Values may be sent and summed in bfloat16 or wider, within the bound.
A program may use at most 128 MiB of HBM per device.

```python
import math
import jax
import jax.numpy as jnp
from jax import lax

K = 80
TILE = 128
SPT = 12
ITERS = 14
TILES_DEV = 256
OBS_DEV = 2048
NTILES = 8192
NSTATE = 1048576
NOBS = 65536
ROUTE = 96
N_STATE = 32


def draw_seg_obs(key, part):
    slots_dev = TILES_DEV * SPT
    device_keys = jax.random.split(jax.random.fold_in(key, 7101), N_STATE)

    def one_device(device_key):
        order_key, place_key = jax.random.split(device_key)
        shuffled = jax.random.permutation(order_key, slots_dev).astype(jnp.int32)
        owner = shuffled // ROUTE
        within = jax.random.randint(place_key, (slots_dev,), 0, OBS_DEV).astype(jnp.int32)
        return owner * OBS_DEV + within
    every = jax.vmap(one_device)(device_keys)
    return every.reshape(N_STATE * TILES_DEV, SPT).astype(jnp.int32)


def draw_ensemble(key, part):
    offset_key, fluct_key = jax.random.split(jax.random.fold_in(key, 5303))
    offsets = 0.02 * jax.random.normal(offset_key, (K,), jnp.float32)
    fluctuation = jax.random.normal(fluct_key, (K, NSTATE), jnp.float32)
    members = jnp.clip(offsets[:, None] + fluctuation, -6.0, 6.0)
    return members.astype(jnp.bfloat16)


def block_levels(key, shape, shards, smallest, largest):
    loudness = 1.0
    for axis_at, blocks in shards:
        steps = jax.random.uniform(jax.random.fold_in(jax.random.fold_in(key, 6), axis_at), (blocks,), jnp.float32, smallest / len(shards), largest / len(shards))
        loudness = loudness * jnp.repeat(jnp.exp(steps), shape[axis_at] // blocks).reshape((-1,) + (1,) * (len(shape) - 1 - axis_at))
    return loudness


def gaussian(rng, dims, scale, limit, kind=jnp.bfloat16):
    return jnp.clip(scale * jax.random.normal(rng, dims, jnp.float32), -limit, limit).astype(kind)


def setup_inputs(seed: int = 0) -> dict:
    seeds = jax.random.split(jax.random.key(seed), 6)
    ensemble = draw_ensemble(jax.random.fold_in(seeds[5], 71), 0)
    weights = jnp.clip(0.14941406 * jax.random.uniform(seeds[1], (NTILES, SPT, TILE), jnp.float32) ** block_levels(seeds[1], (NTILES, SPT, TILE), ((0, 32),), -0.2, 0.2), 0.0, 0.14941406).astype(jnp.bfloat16)
    seg_obs = draw_seg_obs(jax.random.fold_in(seeds[5], 71), 0)
    observed = gaussian(seeds[3], (NOBS,), 30.0, 180.0, jnp.float32)
    inv_var = jnp.clip(jnp.exp(jax.random.uniform(seeds[4], (NOBS,), jnp.float32, math.log(0.0001), math.log(0.001))), 0.0001, 0.001)
    return dict(ensemble=ensemble, weights=weights, seg_obs=seg_obs, observed=observed, inv_var=inv_var)


def transform(gram, pull, members):
    identity = jnp.eye(members, dtype=jnp.float32)
    system = (members - 1.0) * identity + gram
    scaling = jnp.sqrt(jnp.sum(system * system))
    ynow = system / scaling
    znow = identity
    for step in range(ITERS):
        correct = 1.5 * identity - 0.5 * jnp.dot(znow, ynow, precision=lax.Precision.HIGHEST)
        ynow = jnp.dot(ynow, correct, precision=lax.Precision.HIGHEST)
        znow = jnp.dot(correct, znow, precision=lax.Precision.HIGHEST)
    root = znow / jnp.sqrt(scaling)
    shift = jnp.dot(root, jnp.dot(root, pull, precision=lax.Precision.HIGHEST), precision=lax.Precision.HIGHEST)
    mixed = shift[:, None] + math.sqrt(members - 1.0) * root
    mixed = mixed + (1.0 - lax.optimization_barrier(jnp.sum(mixed, axis=0, keepdims=True))) / members
    return mixed.astype(jnp.bfloat16)

def statistics(everyone, obs_here, var_here, members):
    mean_obs = lax.optimization_barrier(jnp.sum(everyone, axis=0)) / members
    anomaly = everyone - mean_obs
    weighted = anomaly * var_here
    gram = jnp.dot(weighted, anomaly.T, precision=lax.Precision.HIGHEST)
    pull = jnp.dot(weighted, obs_here - mean_obs, precision=lax.Precision.HIGHEST)
    return (gram, pull)

def reference(ensemble, weights, seg_obs, observed, inv_var):
    blocks = ensemble.reshape(K, NTILES, TILE).astype(jnp.float32)
    values = jnp.einsum('ktc,tjc->tjk', blocks, weights.astype(jnp.float32), precision=lax.Precision.HIGHEST)
    values = values.reshape(NTILES * SPT, K)
    summed = jax.ops.segment_sum(values, seg_obs.reshape(-1).astype(jnp.int32), num_segments=NOBS).T
    everyone = summed.astype(jnp.bfloat16).astype(jnp.float32)
    gram, pull = statistics(everyone, observed, inv_var, K)
    mixing = transform(gram, pull, K)
    result = jnp.dot(mixing.T, ensemble, preferred_element_type=jnp.float32)
    return result.astype(jnp.bfloat16)
```

```python
import functools
import math

import jax
import jax.numpy as jnp
from jax import lax
from jax.experimental import pallas as pl
from jax.experimental.pallas import tpu as pltpu
from jax.sharding import PartitionSpec as P

ITERS = 14
F32, BF16, I32 = jnp.float32, jnp.bfloat16, jnp.int32
MESH = pl.DeviceIdType.MESH
GT = 16
LANES = 128


def nt(a, b, precision=None):
    return lax.dot_general(
        a, b, (((1,), (1,)), ((), ())), precision=precision, preferred_element_type=F32
    )


def iota(shape, dim):
    return lax.broadcasted_iota(I32, shape, dim)


def onehot(mask):
    return jnp.where(mask, 1.0, 0.0)


def transform(total, members, yref, zref):
    hi = lax.Precision.HIGHEST
    total = jnp.concatenate([total, jnp.zeros((LANES - members, LANES), F32)], axis=0)
    down, across = iota((LANES, LANES), 0), iota((LANES, LANES), 1)
    gram = jnp.where(across < members, total, 0.0)
    identity = onehot(jnp.logical_and(down == across, down < members))
    system = (members - 1.0) * identity + gram
    scaling = jnp.sqrt(jnp.sum(jnp.sum(system * system, axis=1, keepdims=True), axis=0, keepdims=True))
    yref[...] = system / scaling
    zref[...] = identity

    def step(_, carry):
        y, z = yref[...], zref[...]
        c = 1.5 * identity - 0.5 * jnp.dot(z, y, precision=hi, preferred_element_type=F32)
        yref[...] = jnp.dot(y, c, precision=hi, preferred_element_type=F32)
        zref[...] = jnp.dot(c, z, precision=hi, preferred_element_type=F32)
        return carry

    lax.fori_loop(0, ITERS, step, 0)
    root = zref[...] / jnp.sqrt(scaling)
    once = jnp.dot(root, total, precision=hi, preferred_element_type=F32)
    twice = jnp.dot(root, once, precision=hi, preferred_element_type=F32)
    mixed = twice[:, members : members + 1] + math.sqrt(members - 1.0) * root
    mixed = mixed + (1.0 - jnp.sum(mixed, axis=0, keepdims=True)) / members
    return jnp.where(jnp.logical_and(down < members, across < members), mixed, 0.0)


def kernel(
    ns, nm, own, tiles, slots, share, route, nown,
    ens, wts, ids, obs, var,
    g16, g4, mix16, mix4,
    yref, zref, tab, rgt, e16, e4, wv, idv, ob, va, vs, lhs, sel, acc, pk, rx, acc2, hg, hf, an, wa, gr, rbuf, gs,
    lsem, bs, br, ps, pr, zs, zr, s1, r1, s2, r2,
):
    me = lax.axis_index("state")
    z = lax.axis_index("mem")
    groups = tiles // GT
    cells = tiles * LANES
    half = cells // 2
    his = share // LANES
    members = own * nm
    chunk = members // nown
    stride = ns // nown
    col = GT * GT

    loads = [
        pltpu.make_async_copy(ens.at[pl.ds(0, 16)], e16, lsem.at[0]),
        pltpu.make_async_copy(ens.at[pl.ds(16, own - 16)], e4, lsem.at[1]),
        pltpu.make_async_copy(wts, wv, lsem.at[2]),
        pltpu.make_async_copy(ids, idv, lsem.at[3]),
        pltpu.make_async_copy(obs.at[me], ob, lsem.at[4]),
        pltpu.make_async_copy(var.at[me], va, lsem.at[5]),
    ]
    for c in loads:
        c.start()

    def plane(d):
        return {"state": lax.rem(me + d, ns)}

    def along(d):
        return {"mem": lax.rem(z + d, nm)}

    barrier = pltpu.get_barrier_semaphore()
    for d in range(1, nm):
        pl.semaphore_signal(barrier, inc=1, device_id=along(d), device_id_type=MESH)

    def greet(d, carry):
        pl.semaphore_signal(barrier, inc=1, device_id=plane(d), device_id_type=MESH)
        return carry

    lax.fori_loop(1, ns, greet, 0)
    pl.semaphore_wait(barrier, nm - 1 + ns - 1)

    def bulk(src16, src4, slot, part, d, n):
        cut = pl.ds(part * half, half)
        return [
            pltpu.make_async_remote_copy(
                src16.at[:, cut], g16.at[slot, :, cut], bs.at[2 * n], br.at[2 * n],
                device_id=along(d), device_id_type=MESH),
            pltpu.make_async_remote_copy(
                src4.at[:, cut], g4.at[slot, :, cut], bs.at[2 * n + 1], br.at[2 * n + 1],
                device_id=along(d), device_id_type=MESH),
        ]

    up0 = bulk(e16, e4, 0, 0, 1, 0)
    dn1 = bulk(e16, e4, 1, 1, nm - 1, 1)
    up1 = bulk(e16, e4, 0, 1, 1, 2)
    dn0 = bulk(e16, e4, 1, 0, nm - 1, 3)
    fu = bulk(g16.at[0], g4.at[0], 2, 0, 1, 4)
    fd = bulk(g16.at[1], g4.at[1], 2, 1, nm - 1, 5)
    loads[0].wait()
    loads[1].wait()
    for c in up0 + dn1:
        c.start()

    loads[3].wait()
    raw = jnp.concatenate([idv[...], jnp.zeros((GT - slots, tiles), I32)], axis=0)
    tab[:tiles] = onehot(iota((tiles, col), 0) % GT == iota((tiles, col), 1) % GT).astype(BF16)
    spread = tab[:tiles]

    def regroup(part):
        part = part.astype(F32)
        tall = jnp.concatenate(
            [jnp.where(iota((GT, tiles), 1) // GT == g, part, 0.0) for g in range(groups)], axis=0
        ).astype(BF16)
        out = jnp.dot(tall, spread, preferred_element_type=F32).reshape(groups, GT, col)
        keep = iota((groups, GT, col), 1) == iota((groups, GT, col), 2) // GT
        return jnp.sum(jnp.where(keep, out, 0.0), axis=1)

    ident = (regroup(raw // 256) * 256.0 + regroup(raw % 256)).astype(I32)
    ident = jnp.where(iota((groups, col), 1) < slots * GT, ident, -1)
    owner = ident // share
    owner = jnp.where(ident < 0, -1, owner)
    place = ident % share
    p_hi = (place // LANES).astype(F32)
    p_lo = (place % LANES).astype(F32)

    ones = [onehot(iota((ns, col), 0) == owner[g : g + 1]) for g in range(groups)]
    tab[...] = onehot(iota((col, col), 0) < iota((col, col), 1)).astype(BF16)
    upper = tab[...]
    before = jnp.dot(
        jnp.concatenate([a.astype(BF16) for a in ones], axis=0), upper, preferred_element_type=F32
    )
    run = jnp.zeros((ns, 1), F32)
    for g in range(groups):
        rank = jnp.sum(ones[g] * (before[g * ns : (g + 1) * ns] + run), axis=0, keepdims=True)
        run = run + jnp.sum(ones[g], axis=1, keepdims=True)
        sel[:, g * col : (g + 1) * col] = onehot(
            iota((LANES, col), 0) == rank.astype(I32)
        ).astype(BF16)

    loads[2].wait()
    lane = iota((GT, col), 1) % GT
    row = iota((GT, col), 0)
    for g in range(groups):
        w = jnp.concatenate(
            [wv[:, g].reshape(slots * GT, LANES), jnp.zeros((col - slots * GT, LANES), BF16)], axis=0
        )
        a = e16[:, g * GT * LANES : (g + 1) * GT * LANES]
        b = e4[:, g * GT * LANES : (g + 1) * GT * LANES]
        b = jnp.concatenate([b, jnp.zeros((32 - own, GT * LANES), BF16)], axis=0)
        va16 = nt(jnp.concatenate([a[:, t * LANES : (t + 1) * LANES] for t in range(GT)], axis=0), w)
        va4 = nt(jnp.concatenate([b[:, t * LANES : (t + 1) * LANES] for t in range(GT)], axis=0), w)
        first = jnp.zeros((GT, col), F32)
        second = jnp.zeros((GT, col), F32)
        for t in range(GT):
            first = jnp.where(lane == t, va16[t * GT : (t + 1) * GT], first)
            second = jnp.where(lane == t, va4[t * GT : (t + 1) * GT], second)
        second = jnp.where(row == own - 16, p_hi[g : g + 1], second)
        second = jnp.where(row == own - 15, p_lo[g : g + 1], second)
        both = jnp.concatenate([first, second], axis=0)
        for o in range(ns):
            lhs[o * 32 : (o + 1) * 32, :] = jnp.where(owner[g : g + 1] == o, both, 0.0).astype(BF16)
        part = nt(lhs[...], sel[:, g * col : (g + 1) * col])
        if g == 0:
            acc[...] = part
        else:
            acc[...] += part
    for o in range(ns):
        pk[o] = acc[o * 32 : (o + 1) * 32, :].astype(BF16)

    def packet(d):
        return pltpu.make_async_remote_copy(
            pk.at[lax.rem(me + d, ns)], rx.at[me], ps.at[d], pr.at[d],
            device_id=plane(d), device_id_type=MESH)

    def arrival(d):
        return pltpu.make_async_remote_copy(
            pk.at[lax.rem(me + d, ns)], rx.at[lax.rem(me - d + ns, ns)], ps.at[d], pr.at[d],
            device_id=plane(d), device_id_type=MESH)

    def send(d, carry):
        packet(d).start()
        return carry

    def receive(d, carry):
        arrival(d).wait_recv()
        return carry

    lax.fori_loop(1, ns, send, 0)
    rx[me] = pk[me]
    lax.fori_loop(1, ns, receive, 0)

    def gather(i, carry):
        left = []
        for q in range(4):
            p = rx[i * 4 + q].astype(F32)
            top = iota((his, LANES), 0).astype(F32) == p[own : own + 1]
            left.append(
                jnp.concatenate([jnp.where(top, p[k : k + 1], 0.0) for k in range(own)], axis=0).astype(BF16)
            )
            rgt[:, q * LANES : (q + 1) * LANES] = onehot(
                iota((LANES, LANES), 0).astype(F32) == p[own + 1 : own + 2]
            ).astype(BF16)
        acc2[...] += nt(jnp.concatenate(left, axis=1), rgt[...])
        return carry

    acc2[...] = jnp.zeros_like(acc2)
    lax.fori_loop(0, ns // 4, gather, 0)
    hg[z] = acc2[...].astype(BF16)

    def members_copy(d, slot):
        return pltpu.make_async_remote_copy(
            hg.at[z], hg.at[slot], zs.at[d - 1], zr.at[d - 1], device_id=along(d), device_id_type=MESH)

    for d in range(1, nm):
        members_copy(d, z).start()
    for c in up0 + dn1:
        c.wait_recv()
    for c in up1 + dn0 + fu + fd:
        c.start()
    for d in range(1, nm):
        members_copy(d, lax.rem(z - d + nm, nm)).wait_recv()

    loads[4].wait()
    loads[5].wait()
    hf[...] = hg[...].astype(F32).reshape(members * his, LANES)
    for h in range(his):
        x = hf[pl.ds(h, members, stride=his), :]
        ybar = jnp.sum(x, axis=0, keepdims=True) / members
        dev = x - ybar
        an[:members, h * LANES : (h + 1) * LANES] = dev
        an[members:, h * LANES : (h + 1) * LANES] = jnp.where(
            iota((LANES - members, LANES), 0) == 0, ob[h : h + 1] - ybar, 0.0
        )
        wa[:, h * LANES : (h + 1) * LANES] = dev * va[h : h + 1]
    gr[...] = nt(wa[...], an[...], lax.Precision.HIGHEST).reshape(nown, chunk, LANES)

    mine = me // stride
    owns = jnp.logical_and(lax.rem(me, stride) == 0, mine < nown)

    def to_owner(i):
        return pltpu.make_async_remote_copy(
            gr.at[i], rbuf.at[me], s1.at[i], r1.at[me],
            device_id={"state": i * stride}, device_id_type=MESH)

    def from_peer(d):
        src = lax.rem(me + d, ns)
        return pltpu.make_async_remote_copy(
            gr.at[0], rbuf.at[src], s1.at[0], r1.at[src], device_id=plane(d), device_id_type=MESH)

    def spread_copy(d, i):
        return pltpu.make_async_remote_copy(
            gs.at[i], gs.at[i], s2.at[d], r2.at[i], device_id=plane(d), device_id_type=MESH)

    for i in range(nown):
        @pl.when(me != i * stride)
        def _():
            to_owner(i).start()

    @pl.when(owns)
    def _():
        rbuf[me] = gr[mine]

        def wait_one(d, carry):
            from_peer(d).wait_recv()
            return carry

        lax.fori_loop(1, ns, wait_one, 0)
        gs[mine] = jnp.sum(rbuf[...], axis=0)

        def send_one(d, carry):
            spread_copy(d, mine).start()
            return carry

        lax.fori_loop(1, ns, send_one, 0)

    for i in range(nown):
        @pl.when(me != i * stride)
        def _():
            spread_copy(1, i).wait_recv()

    mixing = transform(gs[...].reshape(members, LANES), members, yref, zref).astype(BF16)

    rows = 32
    pick = onehot(
        jnp.logical_and(
            iota((rows, LANES), 1) == z * own + iota((rows, LANES), 0), iota((rows, LANES), 0) < own
        )
    ).astype(BF16)
    mine_t = nt(pick, mixing).astype(BF16)
    order = [0, nm - 1, 1, 2]
    for r, d in enumerate(order):
        base = lax.rem(z + d, nm) * own
        tab[:LANES, :LANES] = onehot(iota((LANES, LANES), 0) == base + iota((LANES, LANES), 1)).astype(BF16)
        part = jnp.dot(mine_t, tab[:LANES, :LANES], preferred_element_type=F32)
        mix16[r] = part[:own, :16].astype(BF16)
        mix4[r] = part[:own, 16:own].astype(BF16)

    for c in up0 + dn1:
        c.wait_send()
    for c in up1 + dn0 + fu + fd:
        c.wait()

    def drain(d, carry):
        packet(d).wait_send()
        return carry

    lax.fori_loop(1, ns, drain, 0)
    for d in range(1, nm):
        members_copy(d, z).wait_send()
    for i in range(nown):
        @pl.when(me != i * stride)
        def _():
            to_owner(i).wait_send()

    @pl.when(owns)
    def _():
        def drain2(d, carry):
            spread_copy(d, mine).wait_send()
            return carry

        lax.fori_loop(1, ns, drain2, 0)


def final(own, ens, g16, g4, mix16, mix4, out):
    x = ens[...]
    total = jnp.dot(mix16[0], x[:16], preferred_element_type=F32)
    total += jnp.dot(mix4[0], x[16:], preferred_element_type=F32)
    for r in range(3):
        total += jnp.dot(mix16[r + 1], g16[r], preferred_element_type=F32)
        total += jnp.dot(mix4[r + 1], g4[r], preferred_element_type=F32)
    out[...] = total.astype(BF16)


def per_device(ns, nm, ensemble, weights, seg_obs, observed, inv_var):
    own, cells = ensemble.shape
    tiles, slots, _ = weights.shape
    share = observed.shape[0] // ns
    route = tiles * slots // ns
    members = own * nm
    nown = 10 if ns >= 10 else 2
    groups = tiles // GT
    his = share // LANES
    wts = jnp.transpose(weights, (1, 0, 2)).reshape(slots, groups, GT, LANES)
    ids = jnp.transpose(seg_obs)
    obs = observed.reshape(ns, his, LANES)
    var = inv_var.reshape(ns, his, LANES)
    anyspec = pl.BlockSpec(memory_space=pl.ANY)
    vspec = pl.BlockSpec(memory_space=pltpu.VMEM)
    dma = pltpu.SemaphoreType.DMA
    col = GT * GT
    g16, g4, mix16, mix4 = pl.pallas_call(
        functools.partial(kernel, ns, nm, own, tiles, slots, share, route, nown),
        out_shape=(
            jax.ShapeDtypeStruct((3, 16, cells), BF16),
            jax.ShapeDtypeStruct((3, own - 16, cells), BF16),
            jax.ShapeDtypeStruct((nm, own, 16), BF16),
            jax.ShapeDtypeStruct((nm, own, own - 16), BF16),
        ),
        in_specs=[anyspec] * 5,
        out_specs=(anyspec, anyspec, vspec, vspec),
        scratch_shapes=[
            pltpu.VMEM((LANES, LANES), F32),
            pltpu.VMEM((LANES, LANES), F32),
            pltpu.VMEM((col, col), BF16),
            pltpu.VMEM((LANES, 4 * LANES), BF16),
            pltpu.VMEM((16, cells), BF16),
            pltpu.VMEM((own - 16, cells), BF16),
            pltpu.VMEM((slots, groups, GT, LANES), BF16),
            pltpu.VMEM((slots, tiles), I32),
            pltpu.VMEM((his, LANES), F32),
            pltpu.VMEM((his, LANES), F32),
            pltpu.VMEM((32, groups * col), BF16),
            pltpu.VMEM((ns * 32, col), BF16),
            pltpu.VMEM((LANES, groups * col), BF16),
            pltpu.VMEM((ns * 32, LANES), F32),
            pltpu.VMEM((ns, 32, LANES), BF16),
            pltpu.VMEM((ns, 32, LANES), BF16),
            pltpu.VMEM((own * his, LANES), F32),
            pltpu.VMEM((nm, own * his, LANES), BF16),
            pltpu.VMEM((members * his, LANES), F32),
            pltpu.VMEM((LANES, share), F32),
            pltpu.VMEM((members, share), F32),
            pltpu.VMEM((nown, members // nown, LANES), F32),
            pltpu.VMEM((ns, members // nown, LANES), F32),
            pltpu.VMEM((nown, members // nown, LANES), F32),
            dma((6,)), dma((12,)), dma((12,)), dma((ns,)), dma((ns,)),
            dma((nm - 1,)), dma((nm - 1,)), dma((nown,)), dma((ns,)), dma((ns,)), dma((nown,)),
        ],
        compiler_params=pltpu.CompilerParams(collective_id=0, has_side_effects=True),
        name="assimilate",
    )(ensemble, wts, ids, obs, var)
    step = min(4096, cells)
    return pl.pallas_call(
        functools.partial(final, own),
        out_shape=jax.ShapeDtypeStruct((own, cells), BF16),
        grid=(cells // step,),
        in_specs=[
            pl.BlockSpec((own, step), lambda i: (0, i)),
            pl.BlockSpec((3, 16, step), lambda i: (0, 0, i)),
            pl.BlockSpec((3, own - 16, step), lambda i: (0, 0, i)),
            pl.BlockSpec((nm, own, 16), lambda i: (0, 0, 0)),
            pl.BlockSpec((nm, own, own - 16), lambda i: (0, 0, 0)),
        ],
        out_specs=pl.BlockSpec((own, step), lambda i: (0, i)),
        name="update",
    )(ensemble, g16, g4, mix16, mix4)


def solution(mesh):
    return jax.shard_map(
        functools.partial(per_device, mesh.shape["state"], mesh.shape["mem"]),
        mesh=mesh,
        in_specs=(P("mem", "state"), P("state", None, None), P("state", None), P(), P()),
        out_specs=P("mem", "state"),
        check_vma=False,
    )
```

```python
import functools
import math

import jax
import jax.numpy as jnp
from jax import lax
from jax.experimental import pallas as pl
from jax.experimental.pallas import tpu as pltpu
from jax.sharding import PartitionSpec as P

ITERS = 14
F32, BF16, I32 = jnp.float32, jnp.bfloat16, jnp.int32
MESH = pl.DeviceIdType.MESH
GT = 16
START = 10
LANES = 128


def nt(a, b, precision=None):
    return lax.dot_general(
        a, b, (((1,), (1,)), ((), ())), precision=precision, preferred_element_type=F32
    )


def iota(shape, dim):
    return lax.broadcasted_iota(I32, shape, dim)


def onehot(mask):
    return jnp.where(mask, 1.0, 0.0)


def split(x):
    high = x.astype(BF16)
    return high, (x - high.astype(F32)).astype(BF16)


def tall(x):
    high, low = split(x)
    pad = jnp.zeros((LANES - x.shape[0], LANES), BF16)
    return jnp.concatenate([high, pad, high, pad, low, pad], axis=0)


def wide(x):
    high, low = split(x)
    return jnp.concatenate([high, low, high], axis=1)


def product(left, right):
    return jnp.dot(left, right, preferred_element_type=F32)


def transform(total, members, yref, zref):
    shape = (members, LANES)
    down, across = iota(shape, 0), iota(shape, 1)
    identity = onehot(down == across)
    system = (members - 1.0) * identity + jnp.where(across < members, total, 0.0)
    scaling = jnp.sqrt(jnp.sum(jnp.sum(system * system, axis=1, keepdims=True), axis=0, keepdims=True))
    yref[...] = system / scaling
    zref[...] = identity

    def step(_, carry):
        y, z = yref[...], zref[...]
        c = 1.5 * identity - 0.5 * product(wide(z), tall(y))
        yref[...] = product(wide(y), tall(c))
        zref[...] = product(wide(c), tall(z))
        return carry

    lax.fori_loop(0, ITERS, step, 0)
    root = zref[...] / jnp.sqrt(scaling)
    left = wide(root)
    twice = product(left, tall(product(left, tall(total))))
    mixed = twice[:, members : members + 1] + math.sqrt(members - 1.0) * root
    mixed = mixed + (1.0 - jnp.sum(mixed, axis=0, keepdims=True)) / members
    return jnp.where(across < members, mixed, 0.0)


def kernel(
    ns, nm, own, tiles, slots, share, route, nown,
    ens, wts, ids, obs, var,
    g16, g4, mix,
    yref, zref, tab, rgt, e16, e4, wv, idv, ob, va, lhs, sel, acc, pk, rx, acc2, hg, hf, an, wa, gr, rbuf, gs,
    lsem, bs, br, ps, pr, zs, zr, s1, r1, s2, r2,
):
    me = lax.axis_index("state")
    z = lax.axis_index("mem")
    groups = tiles // GT
    cells = tiles * LANES
    half = cells // 2
    his = share // LANES
    members = own * nm
    chunk = members // nown
    stride = ns // nown
    col = GT * GT

    loads = [
        pltpu.make_async_copy(ens.at[pl.ds(0, 16)], e16, lsem.at[0]),
        pltpu.make_async_copy(ens.at[pl.ds(16, own - 16)], e4, lsem.at[1]),
        pltpu.make_async_copy(wts, wv, lsem.at[2]),
        pltpu.make_async_copy(ids, idv, lsem.at[3]),
        pltpu.make_async_copy(obs.at[me], ob, lsem.at[4]),
        pltpu.make_async_copy(var.at[me], va, lsem.at[5]),
    ]
    for c in loads:
        c.start()

    def plane(d):
        return {"state": lax.rem(me + d, ns)}

    def along(d):
        return {"mem": lax.rem(z + d, nm)}

    barrier = pltpu.get_barrier_semaphore()
    for d in range(1, nm):
        pl.semaphore_signal(barrier, inc=1, device_id=along(d), device_id_type=MESH)

    def greet(d, carry):
        pl.semaphore_signal(barrier, inc=1, device_id=plane(d), device_id_type=MESH)
        return carry

    lax.fori_loop(1, ns, greet, 0)

    def bulk(src16, src4, slot, part, d, n):
        cut = pl.ds(part * half, half)
        return [
            pltpu.make_async_remote_copy(
                src16.at[:, cut], g16.at[slot, :, cut], bs.at[2 * n], br.at[2 * n],
                device_id=along(d), device_id_type=MESH),
            pltpu.make_async_remote_copy(
                src4.at[:, cut], g4.at[slot, :, cut], bs.at[2 * n + 1], br.at[2 * n + 1],
                device_id=along(d), device_id_type=MESH),
        ]

    up0 = bulk(e16, e4, 0, 0, 1, 0)
    dn1 = bulk(e16, e4, 1, 1, nm - 1, 1)
    up1 = bulk(e16, e4, 0, 1, 1, 2)
    dn0 = bulk(e16, e4, 1, 0, nm - 1, 3)
    fu = bulk(g16.at[0], g4.at[0], 2, 0, 1, 4)
    fd = bulk(g16.at[1], g4.at[1], 2, 1, nm - 1, 5)

    loads[3].wait()
    raw = jnp.concatenate([idv[...], jnp.zeros((GT - slots, tiles), I32)], axis=0)
    tab[:tiles] = onehot(iota((tiles, col), 0) % GT == iota((tiles, col), 1) % GT).astype(BF16)
    spread = tab[:tiles]

    def regroup(part):
        part = part.astype(F32)
        tall = jnp.concatenate(
            [jnp.where(iota((GT, tiles), 1) // GT == g, part, 0.0) for g in range(groups)], axis=0
        ).astype(BF16)
        out = jnp.dot(tall, spread, preferred_element_type=F32).reshape(groups, GT, col)
        keep = iota((groups, GT, col), 1) == iota((groups, GT, col), 2) // GT
        return jnp.sum(jnp.where(keep, out, 0.0), axis=1)

    ident = (regroup(raw // 256) * 256.0 + regroup(raw % 256)).astype(I32)
    ident = jnp.where(iota((groups, col), 1) < slots * GT, ident, -1)
    owner = ident // share
    owner = jnp.where(ident < 0, -1, owner)
    place = ident % share
    code = jnp.left_shift(1, place // LANES).astype(F32) * (1.0 + (place % LANES).astype(F32) / LANES)

    ones = [onehot(iota((ns, col), 0) == owner[g : g + 1]) for g in range(groups)]
    tab[...] = onehot(iota((col, col), 0) < iota((col, col), 1)).astype(BF16)
    upper = tab[...]
    before = jnp.dot(
        jnp.concatenate([a.astype(BF16) for a in ones], axis=0), upper, preferred_element_type=F32
    )
    run = jnp.zeros((ns, 1), F32)
    ranks = []
    for g in range(groups):
        rank = jnp.sum(ones[g] * (before[g * ns : (g + 1) * ns] + run), axis=0, keepdims=True)
        run = run + jnp.sum(ones[g], axis=1, keepdims=True)
        rank = rank.astype(I32)
        ranks.append(rank)
        sel[:, 2 * g * col : (2 * g + 1) * col] = onehot(iota((LANES, col), 0) == rank).astype(BF16)
        sel[:, (2 * g + 1) * col : (2 * g + 2) * col] = onehot(
            iota((LANES, col), 0) == LANES - 32 + rank % 32
        ).astype(BF16)

    loads[2].wait()
    loads[0].wait()
    loads[1].wait()
    lane = iota((GT, col), 1) % GT
    row = iota((GT, col), 0)
    for g in range(groups):
        w = jnp.concatenate(
            [wv[:, g].reshape(slots * GT, LANES), jnp.zeros((col - slots * GT, LANES), BF16)], axis=0
        )
        a = e16[:, g * GT * LANES : (g + 1) * GT * LANES]
        b = e4[:, g * GT * LANES : (g + 1) * GT * LANES]
        b = jnp.concatenate([b, jnp.zeros((32 - own, GT * LANES), BF16)], axis=0)
        va16 = nt(jnp.concatenate([a[:, t * LANES : (t + 1) * LANES] for t in range(GT)], axis=0), w)
        va4 = nt(jnp.concatenate([b[:, t * LANES : (t + 1) * LANES] for t in range(GT)], axis=0), w)
        first = jnp.zeros((GT, col), F32)
        second = jnp.zeros((GT, col), F32)
        for t in range(GT):
            first = jnp.where(lane == t, va16[t * GT : (t + 1) * GT], first)
            second = jnp.where(lane == t, va4[t * GT : (t + 1) * GT], second)
        extra = [second[r : r + 1] for r in range(own - 16)] + [code[g : g + 1]]
        rest = jnp.zeros((GT, col), F32)
        for r, line in enumerate(extra):
            rest = jnp.where(row // 3 == r, line, rest)
        rest = jnp.where(row % 3 == ranks[g] // 32, rest, 0.0)
        for o in range(ns):
            there = owner[g : g + 1] == o
            lhs[o * GT : (o + 1) * GT, :col] = jnp.where(there, first, 0.0).astype(BF16)
            lhs[o * GT : (o + 1) * GT, col:] = jnp.where(there, rest, 0.0).astype(BF16)
        part = nt(lhs[...], sel[:, 2 * g * col : (2 * g + 2) * col])
        if g == 0:
            acc[...] = part
        else:
            acc[...] += part
        if g == min(START, groups) - 1:
            pl.semaphore_wait(barrier, nm - 1 + ns - 1)
            for c in up0 + dn1:
                c.start()
    for o in range(ns):
        pk[o] = acc[o * GT : (o + 1) * GT, :].astype(BF16)

    def packet(d):
        return pltpu.make_async_remote_copy(
            pk.at[lax.rem(me + d, ns)], rx.at[me], ps.at[d], pr.at[d],
            device_id=plane(d), device_id_type=MESH)

    def arrival(d):
        return pltpu.make_async_remote_copy(
            pk.at[lax.rem(me + d, ns)], rx.at[lax.rem(me - d + ns, ns)], ps.at[d], pr.at[d],
            device_id=plane(d), device_id_type=MESH)

    def send(d, carry):
        packet(d).start()
        return carry

    def receive(d, carry):
        arrival(d).wait_recv()
        return carry

    lax.fori_loop(1, ns, send, 0)
    rx[me] = pk[me]
    lax.fori_loop(1, ns, receive, 0)

    spot = iota((1, LANES), 1)
    power = jnp.left_shift(1, iota((his, LANES), 0)).astype(F32)
    inverse = jnp.left_shift(1, his - 1 - iota((his, LANES), 0)).astype(F32) * (2.0 ** (1 - his))

    def gather(i, carry):
        left = []
        for q in range(4):
            p = rx[i * 4 + q].astype(F32)
            r1x, r2x, r3x = (pltpu.roll(p, 32 * (t + 1), 1) for t in range(3))
            lines = [p[k : k + 1] for k in range(16)]
            for r in range(own - 15):
                line = jnp.where(spot < 96, r3x[3 * r + 2 : 3 * r + 3], 0.0)
                line = jnp.where(spot < 64, r2x[3 * r + 1 : 3 * r + 2], line)
                lines.append(jnp.where(spot < 32, r1x[3 * r : 3 * r + 1], line))
            where = lines.pop()
            top = jnp.logical_and(where >= power, where < 2.0 * power)
            left.append(
                jnp.concatenate([jnp.where(top, v, 0.0) for v in lines], axis=0).astype(BF16)
            )
            low = where * jnp.sum(jnp.where(top, inverse, 0.0), axis=0, keepdims=True) * LANES - LANES
            rgt[:, q * LANES : (q + 1) * LANES] = onehot(iota((LANES, LANES), 0).astype(F32) == low).astype(BF16)
        acc2[...] += nt(jnp.concatenate(left, axis=1), rgt[...])
        return carry

    acc2[...] = jnp.zeros_like(acc2)
    lax.fori_loop(0, ns // 4, gather, 0)
    hg[z] = acc2[...].astype(BF16)

    def members_copy(d, slot):
        return pltpu.make_async_remote_copy(
            hg.at[z], hg.at[slot], zs.at[d - 1], zr.at[d - 1], device_id=along(d), device_id_type=MESH)

    for d in range(1, nm):
        members_copy(d, z).start()
    for c in up0 + dn1:
        c.wait_recv()
    for c in up1 + dn0 + fu + fd:
        c.start()
    for d in range(1, nm):
        members_copy(d, lax.rem(z - d + nm, nm)).wait_recv()

    loads[4].wait()
    loads[5].wait()
    hf[...] = hg[...].astype(F32).reshape(members * his, LANES)
    for h in range(his):
        x = hf[pl.ds(h, members, stride=his), :]
        ybar = jnp.sum(x, axis=0, keepdims=True) / members
        dev = x - ybar
        an[:members, h * LANES : (h + 1) * LANES] = dev
        an[members:, h * LANES : (h + 1) * LANES] = jnp.where(
            iota((LANES - members, LANES), 0) == 0, ob[h : h + 1] - ybar, 0.0
        )
        wa[:, h * LANES : (h + 1) * LANES] = dev * va[h : h + 1]
    gr[...] = nt(wa[...], an[...], lax.Precision.HIGHEST).reshape(nown, chunk, LANES)

    mine = me // stride
    owns = jnp.logical_and(lax.rem(me, stride) == 0, mine < nown)

    def to_owner(i):
        return pltpu.make_async_remote_copy(
            gr.at[i], rbuf.at[me], s1.at[i], r1.at[me],
            device_id={"state": i * stride}, device_id_type=MESH)

    def from_peer(d):
        src = lax.rem(me + d, ns)
        return pltpu.make_async_remote_copy(
            gr.at[0], rbuf.at[src], s1.at[0], r1.at[src], device_id=plane(d), device_id_type=MESH)

    def spread_copy(d, i):
        return pltpu.make_async_remote_copy(
            gs.at[i], gs.at[i], s2.at[d], r2.at[i], device_id=plane(d), device_id_type=MESH)

    for i in range(nown):
        @pl.when(me != i * stride)
        def _():
            to_owner(i).start()

    @pl.when(owns)
    def _():
        rbuf[me] = gr[mine]

        def wait_one(d, carry):
            from_peer(d).wait_recv()
            return carry

        lax.fori_loop(1, ns, wait_one, 0)
        gs[mine] = jnp.sum(rbuf[...], axis=0)

        def send_one(d, carry):
            spread_copy(d, mine).start()
            return carry

        lax.fori_loop(1, ns, send_one, 0)

    for i in range(nown):
        @pl.when(me != i * stride)
        def _():
            spread_copy(1, i).wait_recv()

    mixing = transform(gs[...].reshape(members, LANES), members, yref, zref).astype(BF16)

    rows = 32
    k = iota((rows, LANES), 0)
    pick = onehot(jnp.logical_and(iota((rows, LANES), 1) == z * own + k, k < own)).astype(BF16)
    q = iota((members, LANES), 0)
    slot = jnp.where(q < 16 * nm, q // 16, (q - 16 * nm) // (own - 16))
    inner = jnp.where(q < 16 * nm, q % 16, 16 + (q - 16 * nm) % (own - 16))
    dist = jnp.where(slot == 0, 0, jnp.where(slot == 1, nm - 1, slot - 1))
    tab[:members, :LANES] = onehot(iota((members, LANES), 1) == (z + dist) % nm * own + inner).astype(BF16)
    padded = jnp.concatenate([mixing, jnp.zeros((LANES - members, LANES), BF16)], axis=0)
    mine_t = nt(pick, padded).astype(BF16)
    mix[...] = nt(mine_t, tab[:members, :LANES]).astype(BF16)

    for c in up0 + dn1:
        c.wait_send()
    for c in up1 + dn0 + fu + fd:
        c.wait()

    def drain(d, carry):
        packet(d).wait_send()
        return carry

    lax.fori_loop(1, ns, drain, 0)
    for d in range(1, nm):
        members_copy(d, z).wait_send()
    for i in range(nown):
        @pl.when(me != i * stride)
        def _():
            to_owner(i).wait_send()

    @pl.when(owns)
    def _():
        def drain2(d, carry):
            spread_copy(d, mine).wait_send()
            return carry

        lax.fori_loop(1, ns, drain2, 0)


def final(own, ens, g16, g4, mix, out):
    x = ens[...]
    parts = [x[:16]] + [g16[r] for r in range(3)]
    parts.append(jnp.concatenate([x[16:]] + [g4[r] for r in range(3)], axis=0))
    total = jnp.dot(mix[...], jnp.concatenate(parts, axis=0), preferred_element_type=F32)
    out[...] = total[:own].astype(BF16)


def per_device(ns, nm, ensemble, weights, seg_obs, observed, inv_var):
    own, cells = ensemble.shape
    tiles, slots, _ = weights.shape
    share = observed.shape[0] // ns
    route = tiles * slots // ns
    members = own * nm
    nown = 10 if ns >= 10 else 2
    groups = tiles // GT
    his = share // LANES
    wts = jnp.transpose(weights, (1, 0, 2)).reshape(slots, groups, GT, LANES)
    ids = jnp.transpose(seg_obs)
    obs = observed.reshape(ns, his, LANES)
    var = inv_var.reshape(ns, his, LANES)
    anyspec = pl.BlockSpec(memory_space=pl.ANY)
    vspec = pl.BlockSpec(memory_space=pltpu.VMEM)
    dma = pltpu.SemaphoreType.DMA
    col = GT * GT
    g16, g4, mix = pl.pallas_call(
        functools.partial(kernel, ns, nm, own, tiles, slots, share, route, nown),
        out_shape=(
            jax.ShapeDtypeStruct((3, 16, cells), BF16),
            jax.ShapeDtypeStruct((3, own - 16, cells), BF16),
            jax.ShapeDtypeStruct((32, members), BF16),
        ),
        in_specs=[anyspec] * 5,
        out_specs=(anyspec, anyspec, vspec),
        scratch_shapes=[
            pltpu.VMEM((members, LANES), F32),
            pltpu.VMEM((members, LANES), F32),
            pltpu.VMEM((col, col), BF16),
            pltpu.VMEM((LANES, 4 * LANES), BF16),
            pltpu.VMEM((16, cells), BF16),
            pltpu.VMEM((own - 16, cells), BF16),
            pltpu.VMEM((slots, groups, GT, LANES), BF16),
            pltpu.VMEM((slots, tiles), I32),
            pltpu.VMEM((his, LANES), F32),
            pltpu.VMEM((his, LANES), F32),
            pltpu.VMEM((ns * GT, 2 * col), BF16),
            pltpu.VMEM((LANES, 2 * groups * col), BF16),
            pltpu.VMEM((ns * GT, LANES), F32),
            pltpu.VMEM((ns, GT, LANES), BF16),
            pltpu.VMEM((ns, GT, LANES), BF16),
            pltpu.VMEM((own * his, LANES), F32),
            pltpu.VMEM((nm, own * his, LANES), BF16),
            pltpu.VMEM((members * his, LANES), F32),
            pltpu.VMEM((LANES, share), F32),
            pltpu.VMEM((members, share), F32),
            pltpu.VMEM((nown, members // nown, LANES), F32),
            pltpu.VMEM((ns, members // nown, LANES), F32),
            pltpu.VMEM((nown, members // nown, LANES), F32),
            dma((6,)), dma((12,)), dma((12,)), dma((ns,)), dma((ns,)),
            dma((nm - 1,)), dma((nm - 1,)), dma((nown,)), dma((ns,)), dma((ns,)), dma((nown,)),
        ],
        compiler_params=pltpu.CompilerParams(collective_id=0, has_side_effects=True),
        name="assimilate",
    )(ensemble, wts, ids, obs, var)
    step = min(4096, cells)
    return pl.pallas_call(
        functools.partial(final, own),
        out_shape=jax.ShapeDtypeStruct((own, cells), BF16),
        grid=(cells // step,),
        in_specs=[
            pl.BlockSpec((own, step), lambda i: (0, i)),
            pl.BlockSpec((3, 16, step), lambda i: (0, 0, i)),
            pl.BlockSpec((3, own - 16, step), lambda i: (0, 0, i)),
            pl.BlockSpec((32, members), lambda i: (0, 0)),
        ],
        out_specs=pl.BlockSpec((own, step), lambda i: (0, i)),
        name="update",
    )(ensemble, g16, g4, mix)


def solution(mesh):
    return jax.shard_map(
        functools.partial(per_device, mesh.shape["state"], mesh.shape["mem"]),
        mesh=mesh,
        in_specs=(P("mem", "state"), P("state", None, None), P("state", None), P(), P()),
        out_specs=P("mem", "state"),
        check_vma=False,
    )
```

```python
import functools
import math

import jax
import jax.numpy as jnp
from jax import lax
from jax.experimental import pallas as pl
from jax.experimental.pallas import tpu as pltpu
from jax.sharding import PartitionSpec as P

ITERS = 14
F32, BF16, I32 = jnp.float32, jnp.bfloat16, jnp.int32
MESH = pl.DeviceIdType.MESH
GT = 16
FULL = 8
FSTEPS = 4
START = 10
LANES = 128


def nt(a, b, precision=None):
    return lax.dot_general(
        a, b, (((1,), (1,)), ((), ())), precision=precision, preferred_element_type=F32
    )


def iota(shape, dim):
    return lax.broadcasted_iota(I32, shape, dim)


def onehot(mask):
    return jnp.where(mask, 1.0, 0.0)


def split(x):
    high = x.astype(BF16)
    return high, (x - high.astype(F32)).astype(BF16)


def tall(x):
    high, low = split(x)
    pad = jnp.zeros((LANES - x.shape[0], LANES), BF16)
    return jnp.concatenate([high, pad, high, pad, low, pad], axis=0)


def wide(x):
    high, low = split(x)
    return jnp.concatenate([high, low, high], axis=1)


def product(left, right):
    return jnp.dot(left, right, preferred_element_type=F32)


def transform(total, members, yref, zref):
    shape = (members, LANES)
    down, across = iota(shape, 0), iota(shape, 1)
    identity = onehot(down == across)
    system = (members - 1.0) * identity + jnp.where(across < members, total, 0.0)
    scaling = jnp.sqrt(jnp.sum(jnp.sum(system * system, axis=1, keepdims=True), axis=0, keepdims=True))
    yref[...] = system / scaling
    zref[...] = identity

    def step(_, carry):
        y, z = yref[...], zref[...]
        c = 1.5 * identity - 0.5 * product(wide(z), tall(y))
        yref[...] = product(wide(y), tall(c))
        zref[...] = product(wide(c), tall(z))
        return carry

    lax.fori_loop(0, ITERS, step, 0)
    root = zref[...] / jnp.sqrt(scaling)
    left = wide(root)
    twice = product(left, tall(product(left, tall(total))))
    mixed = twice[:, members : members + 1] + math.sqrt(members - 1.0) * root
    mixed = mixed + (1.0 - jnp.sum(mixed, axis=0, keepdims=True)) / members
    return jnp.where(across < members, mixed, 0.0)


def kernel(
    ns, nm, own, tiles, slots, share, nown, fc,
    ens, wts, ids, obs, var,
    o16, o4,
    f16, f4, q16, q4, t16, t4, x4, w16, w4, v16, v4, u16, u4, mixp,
    yref, zref, tab, rgt, e16, e4, wv, idv, ob, va, lhs, sel, acc, pk, rx, acc2, hg, hf, an, wa, gr, rbuf, gs,
    lsem, bs, br, ps, pr, zs, zr, s1, r1, s2, r2, osem,
):
    me = lax.axis_index("state")
    z = lax.axis_index("mem")
    groups = tiles // GT
    cells = tiles * LANES
    qc = (cells - fc) // nm
    his = share // LANES
    members = own * nm
    chunk = members // nown
    stride = ns // nown
    col = GT * GT

    loads = [
        pltpu.make_async_copy(ens.at[pl.ds(0, 16)], e16, lsem.at[0]),
        pltpu.make_async_copy(ens.at[pl.ds(16, own - 16)], e4, lsem.at[1]),
        pltpu.make_async_copy(wts, wv, lsem.at[2]),
        pltpu.make_async_copy(ids, idv, lsem.at[3]),
        pltpu.make_async_copy(obs.at[me], ob, lsem.at[4]),
        pltpu.make_async_copy(var.at[me], va, lsem.at[5]),
    ]
    for c in loads:
        c.start()

    def plane(d):
        return {"state": lax.rem(me + d, ns)}

    def along(d):
        return {"mem": lax.rem(z + d, nm)}

    barrier = pltpu.get_barrier_semaphore()
    for d in range(1, nm):
        pl.semaphore_signal(barrier, inc=1, device_id=along(d), device_id_type=MESH)

    def greet(d, carry):
        pl.semaphore_signal(barrier, inc=1, device_id=plane(d), device_id_type=MESH)
        return carry

    lax.fori_loop(1, ns, greet, 0)

    count = [0]

    def pair(src16, src4, dst16, dst4, d):
        n = count[0]
        count[0] += 2
        return [
            pltpu.make_async_remote_copy(
                src, dst, bs.at[n + i], br.at[n + i], device_id=along(d), device_id_type=MESH)
            for i, (src, dst) in enumerate(((src16, dst16), (src4, dst4)))
        ]

    up, dn = 1, nm - 1
    fh, qh = fc // 2, qc // 2

    def quarter(d):
        return pl.multiple_of(fc + lax.rem(z + d, nm) * qc, LANES)

    def own_at(at, n):
        return e16.at[:, pl.ds(at, n)], e4.at[:, pl.ds(at, n)]

    def at(pairs, slot, start, n):
        return tuple(ref.at[slot, :, pl.ds(start, n)] for ref in pairs)

    first_up = pair(*own_at(quarter(2), qh), *at((t16, t4), 0, 0, qh), up)
    first_dn = pair(*own_at(quarter(2) + qh, qh), *at((t16, t4), 1, 0, qh), dn)
    near_up = pair(*own_at(quarter(up), qc), *at((q16, q4), 0, 0, qc), up)
    near_dn = pair(*own_at(quarter(dn), qc), *at((q16, q4), 1, 0, qc), dn)
    pass_up = pair(*at((t16, t4), 0, 0, qh), *at((q16, q4), 2, 0, qh), up)
    pass_dn = pair(*at((t16, t4), 1, 0, qh), *at((q16, q4), 2, qh, qh), dn)
    full_up0 = pair(*own_at(0, fh), *at((f16, f4), 0, 0, fh), up)
    full_dn1 = pair(*own_at(fh, fh), *at((f16, f4), 1, fh, fh), dn)
    full_up1 = pair(*own_at(fh, fh), *at((f16, f4), 0, fh, fh), up)
    full_dn0 = pair(*own_at(0, fh), *at((f16, f4), 1, 0, fh), dn)
    over_up = pair(*at((f16, f4), 0, 0, fh), *at((f16, f4), 2, 0, fh), up)
    over_dn = pair(*at((f16, f4), 1, fh, fh), *at((f16, f4), 2, fh, fh), dn)
    wave1 = first_up + first_dn + near_up + near_dn + full_up0 + full_dn1
    wave2 = pass_up + pass_dn
    wave3 = full_up1 + full_dn0 + over_up + over_dn
    mid = pl.multiple_of(fc + z * qc, LANES)
    far = pl.multiple_of(fc + lax.rem(z + 2, nm) * qc, LANES)

    def out_at(start, n):
        return o16.at[:, pl.ds(start, n)], o4.at[:, pl.ds(start, n)]

    back_first_up = pair(*at((w16, w4), 3, 0, qh), *at((v16, v4), 0, 0, qh), up)
    back_first_dn = pair(*at((w16, w4), 3, qh, qh), *at((v16, v4), 1, 0, qh), dn)
    back_near_up = pair(*at((w16, w4), 2, 0, qc), *out_at(mid, qc), up)
    back_near_dn = pair(*at((w16, w4), 1, 0, qc), *out_at(mid, qc), dn)
    before_mid = pl.multiple_of(fc + lax.rem(z + dn, nm) * qc, LANES)
    after_mid = pl.multiple_of(fc + lax.rem(z + up, nm) * qc, LANES)
    back_pass_up = pair(*at((v16, v4), 0, 0, qh), *out_at(before_mid, qh), up)
    back_pass_dn = pair(*at((v16, v4), 1, 0, qh), *out_at(after_mid + qh, qh), dn)
    back1 = back_first_up + back_first_dn + back_near_up + back_near_dn
    back2 = back_pass_up + back_pass_dn

    loads[3].wait()
    raw = jnp.concatenate([idv[...], jnp.zeros((GT - slots, tiles), I32)], axis=0)
    tab[:tiles] = onehot(iota((tiles, col), 0) % GT == iota((tiles, col), 1) % GT).astype(BF16)
    spread = tab[:tiles]

    def regroup(part):
        part = part.astype(F32)
        tall = jnp.concatenate(
            [jnp.where(iota((GT, tiles), 1) // GT == g, part, 0.0) for g in range(groups)], axis=0
        ).astype(BF16)
        out = jnp.dot(tall, spread, preferred_element_type=F32).reshape(groups, GT, col)
        keep = iota((groups, GT, col), 1) == iota((groups, GT, col), 2) // GT
        return jnp.sum(jnp.where(keep, out, 0.0), axis=1)

    ident = (regroup(raw // 256) * 256.0 + regroup(raw % 256)).astype(I32)
    ident = jnp.where(iota((groups, col), 1) < slots * GT, ident, -1)
    owner = ident // share
    owner = jnp.where(ident < 0, -1, owner)
    place = ident % share
    code = jnp.left_shift(1, place // LANES).astype(F32) * (1.0 + (place % LANES).astype(F32) / LANES)

    ones = [onehot(iota((ns, col), 0) == owner[g : g + 1]) for g in range(groups)]
    tab[...] = onehot(iota((col, col), 0) < iota((col, col), 1)).astype(BF16)
    upper = tab[...]
    before = jnp.dot(
        jnp.concatenate([a.astype(BF16) for a in ones], axis=0), upper, preferred_element_type=F32
    )
    run = jnp.zeros((ns, 1), F32)
    ranks = []
    for g in range(groups):
        rank = jnp.sum(ones[g] * (before[g * ns : (g + 1) * ns] + run), axis=0, keepdims=True)
        run = run + jnp.sum(ones[g], axis=1, keepdims=True)
        rank = rank.astype(I32)
        ranks.append(rank)
        sel[:, 2 * g * col : (2 * g + 1) * col] = onehot(iota((LANES, col), 0) == rank).astype(BF16)
        sel[:, (2 * g + 1) * col : (2 * g + 2) * col] = onehot(
            iota((LANES, col), 0) == LANES - 32 + rank % 32
        ).astype(BF16)

    loads[2].wait()
    loads[0].wait()
    loads[1].wait()
    lane = iota((GT, col), 1) % GT
    row = iota((GT, col), 0)
    for g in range(groups):
        w = jnp.concatenate(
            [wv[:, g].reshape(slots * GT, LANES), jnp.zeros((col - slots * GT, LANES), BF16)], axis=0
        )
        a = e16[:, g * GT * LANES : (g + 1) * GT * LANES]
        b = e4[:, g * GT * LANES : (g + 1) * GT * LANES]
        b = jnp.concatenate([b, jnp.zeros((32 - own, GT * LANES), BF16)], axis=0)
        va16 = nt(jnp.concatenate([a[:, t * LANES : (t + 1) * LANES] for t in range(GT)], axis=0), w)
        va4 = nt(jnp.concatenate([b[:, t * LANES : (t + 1) * LANES] for t in range(GT)], axis=0), w)
        first = jnp.zeros((GT, col), F32)
        second = jnp.zeros((GT, col), F32)
        for t in range(GT):
            first = jnp.where(lane == t, va16[t * GT : (t + 1) * GT], first)
            second = jnp.where(lane == t, va4[t * GT : (t + 1) * GT], second)
        extra = [second[r : r + 1] for r in range(own - 16)] + [code[g : g + 1]]
        rest = jnp.zeros((GT, col), F32)
        for r, line in enumerate(extra):
            rest = jnp.where(row // 3 == r, line, rest)
        rest = jnp.where(row % 3 == ranks[g] // 32, rest, 0.0)
        for o in range(ns):
            there = owner[g : g + 1] == o
            lhs[o * GT : (o + 1) * GT, :col] = jnp.where(there, first, 0.0).astype(BF16)
            lhs[o * GT : (o + 1) * GT, col:] = jnp.where(there, rest, 0.0).astype(BF16)
        part = nt(lhs[...], sel[:, 2 * g * col : (2 * g + 2) * col])
        if g == 0:
            acc[...] = part
        else:
            acc[...] += part
        if g == min(START, groups) - 1:
            pl.semaphore_wait(barrier, nm - 1 + ns - 1)
            for c in wave1:
                c.start()
    for o in range(ns):
        pk[o] = acc[o * GT : (o + 1) * GT, :].astype(BF16)

    def send(d, carry):
        pltpu.make_async_remote_copy(
            pk.at[lax.rem(me + d, ns)], rx.at[me], ps.at[0], pr.at[0],
            device_id=plane(d), device_id_type=MESH).start()
        return carry

    packets = pltpu.make_async_remote_copy(
        pk.at[pl.ds(0, ns - 1)], rx.at[pl.ds(0, ns - 1)], ps.at[0], pr.at[0],
        device_id=plane(1), device_id_type=MESH)
    lax.fori_loop(1, ns, send, 0)
    rx[me] = pk[me]
    for c in first_up + first_dn:
        c.wait_recv()
    for c in wave2:
        c.start()
    packets.wait_recv()

    spot = iota((1, LANES), 1)
    power = jnp.left_shift(1, iota((his, LANES), 0)).astype(F32)
    inverse = jnp.left_shift(1, his - 1 - iota((his, LANES), 0)).astype(F32) * (2.0 ** (1 - his))

    def gather(i, carry):
        left = []
        for q in range(4):
            p = rx[i * 4 + q].astype(F32)
            r1x, r2x, r3x = (pltpu.roll(p, 32 * (t + 1), 1) for t in range(3))
            lines = [p[k : k + 1] for k in range(16)]
            for r in range(own - 15):
                line = jnp.where(spot < 96, r3x[3 * r + 2 : 3 * r + 3], 0.0)
                line = jnp.where(spot < 64, r2x[3 * r + 1 : 3 * r + 2], line)
                lines.append(jnp.where(spot < 32, r1x[3 * r : 3 * r + 1], line))
            where = lines.pop()
            top = jnp.logical_and(where >= power, where < 2.0 * power)
            left.append(
                jnp.concatenate([jnp.where(top, v, 0.0) for v in lines], axis=0).astype(BF16)
            )
            low = where * jnp.sum(jnp.where(top, inverse, 0.0), axis=0, keepdims=True) * LANES - LANES
            rgt[:, q * LANES : (q + 1) * LANES] = onehot(iota((LANES, LANES), 0).astype(F32) == low).astype(BF16)
        acc2[...] += nt(jnp.concatenate(left, axis=1), rgt[...])
        return carry

    acc2[...] = jnp.zeros_like(acc2)
    lax.fori_loop(0, ns // 4, gather, 0)
    hg[z] = acc2[...].astype(BF16)

    def members_copy(d, slot):
        return pltpu.make_async_remote_copy(
            hg.at[z], hg.at[slot], zs.at[d - 1], zr.at[d - 1], device_id=along(d), device_id_type=MESH)

    for d in range(1, nm):
        members_copy(d, z).start()
    for c in full_up0 + full_dn1:
        c.wait_recv()
    for c in wave3:
        c.start()
    for d in range(1, nm):
        members_copy(d, lax.rem(z - d + nm, nm)).wait_recv()

    loads[4].wait()
    loads[5].wait()
    hf[...] = hg[...].astype(F32).reshape(members * his, LANES)
    for h in range(his):
        x = hf[pl.ds(h, members, stride=his), :]
        ybar = jnp.sum(x, axis=0, keepdims=True) / members
        dev = x - ybar
        an[:members, h * LANES : (h + 1) * LANES] = dev
        an[members:, h * LANES : (h + 1) * LANES] = jnp.where(
            iota((LANES - members, LANES), 0) == 0, ob[h : h + 1] - ybar, 0.0
        )
        wa[:, h * LANES : (h + 1) * LANES] = dev * va[h : h + 1]
    gr[...] = nt(wa[...], an[...], lax.Precision.HIGHEST).reshape(nown, chunk, LANES)

    mine = me // stride
    owns = jnp.logical_and(lax.rem(me, stride) == 0, mine < nown)

    def to_owner(i):
        return pltpu.make_async_remote_copy(
            gr.at[i], rbuf.at[me], s1.at[0], r1.at[0],
            device_id={"state": i * stride}, device_id_type=MESH)

    def tiles_moved(n, src, dst, ss, rs):
        return pltpu.make_async_remote_copy(
            src.at[pl.ds(0, n)], dst.at[pl.ds(0, n)], ss, rs, device_id=plane(1), device_id_type=MESH)

    for i in range(nown):
        @pl.when(me != i * stride)
        def _():
            to_owner(i).start()

    for c in near_up + near_dn + pass_up + pass_dn:
        c.wait_recv()
    x4[:, :qc] = jnp.concatenate([e4[:, pl.ds(mid, qc)]] + [q4[r] for r in range(3)], axis=0)

    @pl.when(owns)
    def _():
        rbuf[me] = gr[mine]
        tiles_moved(ns - 1, rbuf, rbuf, s1.at[0], r1.at[0]).wait_recv()
        gs[mine] = jnp.sum(rbuf[...], axis=0)

        def send_one(d, carry):
            pltpu.make_async_remote_copy(
                gs.at[mine], gs.at[mine], s2.at[0], r2.at[0],
                device_id=plane(d), device_id_type=MESH).start()
            return carry

        lax.fori_loop(1, ns, send_one, 0)
        tiles_moved(nown - 1, gs, gs, s2.at[0], r2.at[0]).wait_recv()

    @pl.when(jnp.logical_not(owns))
    def _():
        tiles_moved(nown, gs, gs, s2.at[0], r2.at[0]).wait_recv()

    mixing = transform(gs[...].reshape(members, LANES), members, yref, zref).astype(BF16)

    q = iota((members, LANES), 0)
    slot = jnp.where(q < 16 * nm, q // 16, (q - 16 * nm) // (own - 16))
    inner = jnp.where(q < 16 * nm, q % 16, 16 + (q - 16 * nm) % (own - 16))
    dist = jnp.where(slot == 0, 0, jnp.where(slot == 1, nm - 1, slot - 1))
    tab[:members, :LANES] = onehot(iota((members, LANES), 1) == (z + dist) % nm * own + inner).astype(BF16)
    padded = jnp.concatenate([mixing, jnp.zeros((LANES - members, LANES), BF16)], axis=0)
    turned = nt(tab[:members, :LANES], padded).astype(BF16)
    mixp[...] = nt(turned, tab[:members, :LANES]).astype(BF16)

    wide_rows = 16 * nm
    x = jnp.concatenate([e16[:, pl.ds(mid, qc)]] + [q16[r] for r in range(3)] + [x4[:, :qc]], axis=0)
    res = jnp.dot(mixp[...], x, preferred_element_type=F32)
    for t in range(nm):
        w16[t] = res[16 * t : 16 * (t + 1)].astype(BF16)
        w4[t] = res[wide_rows + (own - 16) * t : wide_rows + (own - 16) * (t + 1)].astype(BF16)
    for c in back1:
        c.start()
    local = [
        pltpu.make_async_copy(w16.at[0], out_at(mid, qc)[0], osem.at[0]),
        pltpu.make_async_copy(w4.at[0], out_at(mid, qc)[1], osem.at[1]),
    ]
    for c in local:
        c.start()

    for c in wave3:
        c.wait_recv()
    mine_rows = jnp.concatenate([mixp[:16], mixp[wide_rows:]], axis=0)
    step = fc // FSTEPS
    for i in range(FSTEPS):
        cut = slice(i * step, (i + 1) * step)
        x = jnp.concatenate(
            [e16[:, cut]] + [f16[r, :, cut] for r in range(3)]
            + [e4[:, cut]] + [f4[r, :, cut] for r in range(3)], axis=0)
        res = jnp.dot(mine_rows, x, preferred_element_type=F32)
        u16[:, cut] = res[:16].astype(BF16)
        u4[:, cut] = res[16:own].astype(BF16)
        if i == FSTEPS // 2 - 1:
            for c in back_first_up + back_first_dn:
                c.wait_recv()
            for c in back2:
                c.start()
    more = [
        pltpu.make_async_copy(u16, out_at(0, fc)[0], osem.at[2]),
        pltpu.make_async_copy(u4, out_at(0, fc)[1], osem.at[3]),
    ]
    for c in more:
        c.start()

    for c in back_near_up + back_near_dn + back2:
        c.wait_recv()
    for c in wave1 + wave2 + wave3 + back1 + back2:
        c.wait_send()
    for c in local + more:
        c.wait()
    packets.wait_send()
    for d in range(1, nm):
        members_copy(d, z).wait_send()

    @pl.when(owns)
    def _():
        tiles_moved(nown - 1, gr, rbuf, s1.at[0], r1.at[0]).wait_send()
        tiles_moved(ns - 1, rbuf, rbuf, s2.at[0], r2.at[0]).wait_send()

    @pl.when(jnp.logical_not(owns))
    def _():
        tiles_moved(nown, gr, rbuf, s1.at[0], r1.at[0]).wait_send()


def per_device(ns, nm, ensemble, weights, seg_obs, observed, inv_var):
    own, cells = ensemble.shape
    tiles, slots, _ = weights.shape
    share = observed.shape[0] // ns
    members = own * nm
    nown = 10 if ns >= 10 else 2
    groups = tiles // GT
    his = share // LANES
    wts = jnp.transpose(weights, (1, 0, 2)).reshape(slots, groups, GT, LANES)
    ids = jnp.transpose(seg_obs)
    obs = observed.reshape(ns, his, LANES)
    var = inv_var.reshape(ns, his, LANES)
    anyspec = pl.BlockSpec(memory_space=pl.ANY)
    dma = pltpu.SemaphoreType.DMA
    col = GT * GT
    fc = cells * FULL // 16
    qc = (cells - fc) // nm
    rest = own - 16
    o16, o4 = pl.pallas_call(
        functools.partial(kernel, ns, nm, own, tiles, slots, share, nown, fc),
        out_shape=(
            jax.ShapeDtypeStruct((16, cells), BF16),
            jax.ShapeDtypeStruct((rest, cells), BF16),
        ),
        in_specs=[anyspec] * 5,
        out_specs=(anyspec, anyspec),
        scratch_shapes=[
            pltpu.VMEM((3, 16, fc), BF16),
            pltpu.VMEM((3, rest, fc), BF16),
            pltpu.VMEM((3, 16, qc), BF16),
            pltpu.VMEM((3, rest, qc), BF16),
            pltpu.VMEM((2, 16, qc // 2), BF16),
            pltpu.VMEM((2, rest, qc // 2), BF16),
            pltpu.VMEM((rest * nm, qc), BF16),
            pltpu.VMEM((nm, 16, qc), BF16),
            pltpu.VMEM((nm, rest, qc), BF16),
            pltpu.VMEM((2, 16, qc // 2), BF16),
            pltpu.VMEM((2, rest, qc // 2), BF16),
            pltpu.VMEM((16, fc), BF16),
            pltpu.VMEM((rest, fc), BF16),
            pltpu.VMEM((members, members), BF16),
            pltpu.VMEM((members, LANES), F32),
            pltpu.VMEM((members, LANES), F32),
            pltpu.VMEM((col, col), BF16),
            pltpu.VMEM((LANES, 4 * LANES), BF16),
            pltpu.VMEM((16, cells), BF16),
            pltpu.VMEM((own - 16, cells), BF16),
            pltpu.VMEM((slots, groups, GT, LANES), BF16),
            pltpu.VMEM((slots, tiles), I32),
            pltpu.VMEM((his, LANES), F32),
            pltpu.VMEM((his, LANES), F32),
            pltpu.VMEM((ns * GT, 2 * col), BF16),
            pltpu.VMEM((LANES, 2 * groups * col), BF16),
            pltpu.VMEM((ns * GT, LANES), F32),
            pltpu.VMEM((ns, GT, LANES), BF16),
            pltpu.VMEM((ns, GT, LANES), BF16),
            pltpu.VMEM((own * his, LANES), F32),
            pltpu.VMEM((nm, own * his, LANES), BF16),
            pltpu.VMEM((members * his, LANES), F32),
            pltpu.VMEM((LANES, share), F32),
            pltpu.VMEM((members, share), F32),
            pltpu.VMEM((nown, members // nown, LANES), F32),
            pltpu.VMEM((ns, members // nown, LANES), F32),
            pltpu.VMEM((nown, members // nown, LANES), F32),
            dma((6,)), dma((36,)), dma((36,)), dma((1,)), dma((1,)),
            dma((nm - 1,)), dma((nm - 1,)), dma((1,)), dma((1,)), dma((1,)), dma((1,)), dma((4,)),
        ],
        compiler_params=pltpu.CompilerParams(collective_id=0, has_side_effects=True),
        name="assimilate",
    )(ensemble, wts, ids, obs, var)
    return jnp.concatenate([o16, o4], axis=0)


def solution(mesh):
    return jax.shard_map(
        functools.partial(per_device, mesh.shape["state"], mesh.shape["mem"]),
        mesh=mesh,
        in_specs=(P("mem", "state"), P("state", None, None), P("state", None), P(), P()),
        out_specs=P("mem", "state"),
        check_vma=False,
    )
```

```python
import functools
import math

import jax
import jax.numpy as jnp
from jax import lax
from jax.experimental import pallas as pl
from jax.experimental.pallas import tpu as pltpu
from jax.sharding import PartitionSpec as P

ITERS = 14
F32, BF16, I32 = jnp.float32, jnp.bfloat16, jnp.int32
MESH = pl.DeviceIdType.MESH
GT = 16
FULL = 8
FSTEPS = 4
START = 5
LANES = 128


def nt(a, b, precision=None):
    return lax.dot_general(
        a, b, (((1,), (1,)), ((), ())), precision=precision, preferred_element_type=F32
    )


def iota(shape, dim):
    return lax.broadcasted_iota(I32, shape, dim)


def onehot(mask):
    return jnp.where(mask, 1.0, 0.0)


def split(x):
    high = x.astype(BF16)
    return high, (x - high.astype(F32)).astype(BF16)


def tall(x):
    high, low = split(x)
    pad = jnp.zeros((LANES - x.shape[0], LANES), BF16)
    return jnp.concatenate([high, pad, high, pad, low, pad], axis=0)


def wide(x):
    high, low = split(x)
    return jnp.concatenate([high, low, high], axis=1)


def product(left, right):
    return jnp.dot(left, right, preferred_element_type=F32)


def transform(total, members, yref, zref):
    shape = (members, LANES)
    down, across = iota(shape, 0), iota(shape, 1)
    identity = onehot(down == across)
    system = (members - 1.0) * identity + jnp.where(across < members, total, 0.0)
    scaling = jnp.sqrt(jnp.sum(jnp.sum(system * system, axis=1, keepdims=True), axis=0, keepdims=True))
    yref[...] = system / scaling
    zref[...] = identity

    def step(_, carry):
        y, z = yref[...], zref[...]
        c = 1.5 * identity - 0.5 * product(wide(z), tall(y))
        yref[...] = product(wide(y), tall(c))
        zref[...] = product(wide(c), tall(z))
        return carry

    lax.fori_loop(0, ITERS, step, 0)
    root = zref[...] / jnp.sqrt(scaling)
    left = wide(root)
    twice = product(left, tall(product(left, tall(total))))
    mixed = twice[:, members : members + 1] + math.sqrt(members - 1.0) * root
    mixed = mixed + (1.0 - jnp.sum(mixed, axis=0, keepdims=True)) / members
    return jnp.where(across < members, mixed, 0.0)


def kernel(
    ns, nm, own, tiles, slots, share, nown, fc,
    ens, wts, ids, obs, var,
    o16, o4,
    f16, f4, q16, q4, t16, t4, x4, w16, w4, v16, v4, u16, u4, mixp,
    yref, zref, tab, rgt, e16, e4, wv, idv, ob, va, lhs, sel, acc, pk, rx, acc2, hg, hf, an, wa, gr, rbuf, gs,
    lsem, bs, br, ps, pr, zs, zr, s1, r1, s2, r2, osem,
):
    me = lax.axis_index("state")
    z = lax.axis_index("mem")
    groups = tiles // GT
    cells = tiles * LANES
    qc = (cells - fc) // nm
    his = share // LANES
    members = own * nm
    chunk = members // nown
    stride = ns // nown
    col = GT * GT
    two = 2 * GT * slots
    pairs = groups // 2
    part = (slots - 8) * GT
    hw = ns // 2

    loads = [
        pltpu.make_async_copy(ens.at[pl.ds(0, 16)], e16, lsem.at[0]),
        pltpu.make_async_copy(ens.at[pl.ds(16, own - 16)], e4, lsem.at[1]),
        pltpu.make_async_copy(wts, wv, lsem.at[2]),
        pltpu.make_async_copy(ids, idv, lsem.at[3]),
        pltpu.make_async_copy(obs.at[me], ob, lsem.at[4]),
        pltpu.make_async_copy(var.at[me], va, lsem.at[5]),
    ]
    for c in loads:
        c.start()

    def plane(d):
        return {"state": lax.rem(me + d, ns)}

    def along(d):
        return {"mem": lax.rem(z + d, nm)}

    barrier = pltpu.get_barrier_semaphore()
    for d in range(1, nm):
        pl.semaphore_signal(barrier, inc=1, device_id=along(d), device_id_type=MESH)

    def greet(d, carry):
        pl.semaphore_signal(barrier, inc=1, device_id=plane(d), device_id_type=MESH)
        return carry

    lax.fori_loop(1, ns, greet, 0)

    count = [0]

    def pair(src16, src4, dst16, dst4, d):
        n = count[0]
        count[0] += 2
        return [
            pltpu.make_async_remote_copy(
                src, dst, bs.at[n + i], br.at[n + i], device_id=along(d), device_id_type=MESH)
            for i, (src, dst) in enumerate(((src16, dst16), (src4, dst4)))
        ]

    up, dn = 1, nm - 1
    fh, qh = fc // 2, qc // 2

    def quarter(d):
        return pl.multiple_of(fc + lax.rem(z + d, nm) * qc, LANES)

    def own_at(at, n):
        return e16.at[:, pl.ds(at, n)], e4.at[:, pl.ds(at, n)]

    def at(pairs, slot, start, n):
        return tuple(ref.at[slot, :, pl.ds(start, n)] for ref in pairs)

    first_up = pair(*own_at(quarter(2), qh), *at((t16, t4), 0, 0, qh), up)
    first_dn = pair(*own_at(quarter(2) + qh, qh), *at((t16, t4), 1, 0, qh), dn)
    near_up = pair(*own_at(quarter(up), qc), *at((q16, q4), 0, 0, qc), up)
    near_dn = pair(*own_at(quarter(dn), qc), *at((q16, q4), 1, 0, qc), dn)
    pass_up = pair(*at((t16, t4), 0, 0, qh), *at((q16, q4), 2, 0, qh), up)
    pass_dn = pair(*at((t16, t4), 1, 0, qh), *at((q16, q4), 2, qh, qh), dn)
    full_up0 = pair(*own_at(0, fh), *at((f16, f4), 0, 0, fh), up)
    full_dn1 = pair(*own_at(fh, fh), *at((f16, f4), 1, fh, fh), dn)
    full_up1 = pair(*own_at(fh, fh), *at((f16, f4), 0, fh, fh), up)
    full_dn0 = pair(*own_at(0, fh), *at((f16, f4), 1, 0, fh), dn)
    over_up = pair(*at((f16, f4), 0, 0, fh), *at((f16, f4), 2, 0, fh), up)
    over_dn = pair(*at((f16, f4), 1, fh, fh), *at((f16, f4), 2, fh, fh), dn)
    wave1 = first_up + first_dn + full_up0 + full_dn1
    wave2 = near_up + near_dn + pass_up + pass_dn + over_up + over_dn + full_up1 + full_dn0
    mid = pl.multiple_of(fc + z * qc, LANES)
    far = pl.multiple_of(fc + lax.rem(z + 2, nm) * qc, LANES)

    def out_at(start, n):
        return o16.at[:, pl.ds(start, n)], o4.at[:, pl.ds(start, n)]

    back_first_up = pair(*at((w16, w4), 3, 0, qh), *at((v16, v4), 0, 0, qh), up)
    back_first_dn = pair(*at((w16, w4), 3, qh, qh), *at((v16, v4), 1, 0, qh), dn)
    back_near_up = pair(*at((w16, w4), 2, 0, qc), *out_at(mid, qc), up)
    back_near_dn = pair(*at((w16, w4), 1, 0, qc), *out_at(mid, qc), dn)
    before_mid = pl.multiple_of(fc + lax.rem(z + dn, nm) * qc, LANES)
    after_mid = pl.multiple_of(fc + lax.rem(z + up, nm) * qc, LANES)
    back_pass_up = pair(*at((v16, v4), 0, 0, qh), *out_at(before_mid, qh), up)
    back_pass_dn = pair(*at((v16, v4), 1, 0, qh), *out_at(after_mid + qh, qh), dn)
    back1 = back_first_up + back_first_dn + back_near_up + back_near_dn
    back2 = back_pass_up + back_pass_dn

    loads[3].wait()
    raw = jnp.concatenate([idv[...], jnp.zeros((GT - slots, tiles), I32)], axis=0)
    tab[:tiles, :col] = onehot(iota((tiles, col), 0) % GT == iota((tiles, col), 1) % GT).astype(BF16)
    spread = tab[:tiles, :col]
    order = list(range(0, groups, 2)) + list(range(1, groups, 2))

    def regroup(byte):
        byte = byte.astype(F32)
        high = jnp.concatenate(
            [jnp.where(iota((GT, tiles), 1) // GT == g, byte, 0.0) for g in order], axis=0
        ).astype(BF16)
        out = jnp.dot(high, spread, preferred_element_type=F32).reshape(groups, GT, col)
        at_lane = iota((groups, GT, col), 2)
        shift = jnp.where(jnp.logical_and(iota((groups, GT, col), 0) >= pairs, at_lane >= LANES), part, 0)
        keep = iota((groups, GT, col), 1) == (at_lane - shift) // GT
        return jnp.sum(jnp.where(keep, out, 0.0), axis=1)

    ident = regroup(raw // 256) * 256.0 + regroup(raw % 256)
    beyond = jnp.where(iota((pairs, LANES), 1) < part, ident[:pairs, LANES:], ident[pairs:, LANES:])
    ident = jnp.concatenate([ident[:pairs, :LANES], ident[pairs:, :LANES], beyond], axis=1).astype(I32)
    owner = ident // share
    place = ident % share
    code = jnp.left_shift(1, place // LANES).astype(F32) * (1.0 + (place % LANES).astype(F32) / LANES)

    ones = [onehot(iota((ns, two), 0) == owner[g : g + 1]) for g in range(pairs)]
    tab[...] = onehot(iota((two, two), 0) < iota((two, two), 1)).astype(BF16)
    before = jnp.dot(
        jnp.concatenate([a.astype(BF16) for a in ones], axis=0), tab[...], preferred_element_type=F32
    )
    run = jnp.zeros((ns, 1), F32)
    ranks = []
    for g in range(pairs):
        rank = jnp.sum(ones[g] * (before[g * ns : (g + 1) * ns] + run), axis=0, keepdims=True)
        run = run + jnp.sum(ones[g], axis=1, keepdims=True)
        rank = rank.astype(I32)
        ranks.append(rank)
        side = owner[g : g + 1] // hw * LANES
        sel[:, 2 * g * two : (2 * g + 1) * two] = onehot(
            iota((2 * LANES, two), 0) == rank + side
        ).astype(BF16)
        sel[:, (2 * g + 1) * two : (2 * g + 2) * two] = onehot(
            iota((2 * LANES, two), 0) == LANES - 32 + rank % 32 + side
        ).astype(BF16)

    loads[2].wait()
    loads[0].wait()
    loads[1].wait()
    lane = iota((GT, col), 1) % GT
    lane8 = iota((8, col), 1) % GT - iota((8, col), 0) // 4
    row = iota((GT, two), 0)
    gap = jnp.zeros((col - slots * GT, LANES), BF16)

    def values(g):
        w = wv[:, g].reshape(slots * GT, LANES)
        if g % 2:
            w = jnp.concatenate([w[:LANES], gap, w[LANES:]], axis=0)
        else:
            w = jnp.concatenate([w, gap], axis=0)
        a = e16[:, g * GT * LANES : (g + 1) * GT * LANES]
        b = e4[:, g * GT * LANES : (g + 1) * GT * LANES]
        a = nt(jnp.concatenate([a[:, t * LANES : (t + 1) * LANES] for t in range(GT)], axis=0), w)
        b = nt(jnp.concatenate([b[:, t * LANES : (t + 1) * LANES] for t in range(GT)], axis=0), w)
        first = jnp.zeros((GT, col), F32)
        second = jnp.zeros((8, col), F32)
        for t in range(GT):
            first = jnp.where(lane == t, a[t * GT : (t + 1) * GT], first)
        for t in range(0, GT, 2):
            second = jnp.where(lane8 == t, b[t * 4 : t * 4 + 8], second)
        return first, second[:4] + second[4:]

    def joined(even, odd):
        return jnp.concatenate([even[:, :LANES], odd[:, :LANES], even[:, LANES:] + odd[:, LANES:]], axis=1)

    for g in range(pairs):
        even, odd = values(2 * g), values(2 * g + 1)
        first, second = joined(even[0], odd[0]), joined(even[1], odd[1])
        extra = [second[r : r + 1] for r in range(own - 16)] + [code[g : g + 1]]
        rest = jnp.zeros((GT, two), F32)
        for r, line in enumerate(extra):
            rest = jnp.where(row // 3 == r, line, rest)
        rest = jnp.where(row % 3 == ranks[g] // 32, rest, 0.0)
        for o in range(hw):
            there = owner[g : g + 1] % hw == o
            lhs[o * GT : (o + 1) * GT, :two] = jnp.where(there, first, 0.0).astype(BF16)
            lhs[o * GT : (o + 1) * GT, two:] = jnp.where(there, rest, 0.0).astype(BF16)
        both = nt(lhs[...], sel[:, 2 * g * two : (2 * g + 2) * two])
        if g == 0:
            acc[...] = both
        else:
            acc[...] += both
        if g == min(START, pairs) - 1:
            pl.semaphore_wait(barrier, nm - 1 + ns - 1)
            for c in wave1:
                c.start()
    for o in range(ns):
        pk[o] = acc[o % hw * GT : (o % hw + 1) * GT, o // hw * LANES : (o // hw + 1) * LANES].astype(BF16)

    def send(d, carry):
        pltpu.make_async_remote_copy(
            pk.at[lax.rem(me + d, ns)], rx.at[me], ps.at[0], pr.at[0],
            device_id=plane(d), device_id_type=MESH).start()
        return carry

    packets = pltpu.make_async_remote_copy(
        pk.at[pl.ds(0, ns - 1)], rx.at[pl.ds(0, ns - 1)], ps.at[0], pr.at[0],
        device_id=plane(1), device_id_type=MESH)
    lax.fori_loop(1, ns, send, 0)
    rx[me] = pk[me]
    packets.wait_recv()

    spot = iota((1, LANES), 1)
    power = jnp.left_shift(1, iota((8, LANES), 0)).astype(F32)
    inverse = jnp.left_shift(1, 7 - iota((8, LANES), 0)).astype(F32)
    down = iota((2 * LANES, LANES), 0)
    for i in range(ns // 8):
        left = []
        for q in range(8):
            p = rx[i * 8 + q].astype(F32)
            r1x, r2x, r3x = (pltpu.roll(p, 32 * (t + 1), 1) for t in range(3))
            lines = [p[k : k + 1] for k in range(16)]
            for r in range(own - 15):
                line = jnp.where(spot < 96, r3x[3 * r + 2 : 3 * r + 3], 0.0)
                line = jnp.where(spot < 64, r2x[3 * r + 1 : 3 * r + 2], line)
                lines.append(jnp.where(spot < 32, r1x[3 * r : 3 * r + 1], line))
            where = lines.pop()
            upper = where >= 256.0
            where = jnp.where(upper, where * (1.0 / 256.0), where)
            top = jnp.logical_and(where >= power, where < 2.0 * power)
            left.append(
                jnp.concatenate([jnp.where(top, v, 0.0) for v in lines], axis=0).astype(BF16)
            )
            low = where * jnp.sum(jnp.where(top, inverse, 0.0), axis=0, keepdims=True)
            low = low.astype(I32) - LANES + jnp.where(upper, LANES, 0)
            rgt[:, (i * 8 + q) * LANES : (i * 8 + q + 1) * LANES] = onehot(down == low).astype(BF16)
        both = nt(jnp.concatenate(left, axis=1), rgt[:, i * 8 * LANES : (i + 1) * 8 * LANES])
        if i == 0:
            acc2[...] = both
        else:
            acc2[...] += both
    hg[z] = acc2[...].astype(BF16)

    hrow = own * 8 // 2

    def members_copy(slot, rows, d, n):
        ref = hg.at[slot, pl.ds(rows * hrow, hrow)]
        return pltpu.make_async_remote_copy(
            ref, ref, zs.at[n], zr.at[n], device_id=along(d), device_id_type=MESH)

    before, after = lax.rem(z + dn, nm), lax.rem(z + up, nm)
    direct = [
        members_copy(z, 0, up, 0), members_copy(z, 1, dn, 1),
        members_copy(z, 1, up, 2), members_copy(z, 0, dn, 3),
    ]
    passed = [members_copy(before, 0, up, 4), members_copy(after, 1, dn, 5)]
    for c in direct:
        c.start()
    for c, e in zip(direct[:2], passed):
        c.wait_recv()
        e.start()
    for c in first_up + first_dn + full_up0 + full_dn1:
        c.wait_recv()
    for c in wave2:
        c.start()
    for c in direct[2:] + passed:
        c.wait_recv()

    loads[4].wait()
    loads[5].wait()
    rows = members * 8
    for c in range(2):
        hf[c * rows : (c + 1) * rows] = hg[:, :, c * LANES : (c + 1) * LANES].astype(F32).reshape(rows, LANES)
    for h in range(8):
        x = jnp.concatenate([hf[pl.ds(c * rows + h, members, stride=8), :] for c in range(2)], axis=1)
        seen = jnp.concatenate([ob[h : h + 1], ob[h + 8 : h + 9]], axis=1)
        weight = jnp.concatenate([va[h : h + 1], va[h + 8 : h + 9]], axis=1)
        ybar = jnp.sum(x, axis=0, keepdims=True) / members
        dev = x - ybar
        cut = slice(h * 2 * LANES, (h + 1) * 2 * LANES)
        an[:members, cut] = dev
        an[members:, cut] = jnp.where(
            iota((LANES - members, 2 * LANES), 0) == 0, seen - ybar, 0.0
        )
        wa[:, cut] = dev * weight
    gr[...] = nt(wa[...], an[...], lax.Precision.HIGHEST).reshape(nown, chunk, LANES)

    mine = me // stride
    owns = jnp.logical_and(lax.rem(me, stride) == 0, mine < nown)

    def to_owner(i):
        return pltpu.make_async_remote_copy(
            gr.at[i], rbuf.at[me], s1.at[0], r1.at[0],
            device_id={"state": i * stride}, device_id_type=MESH)

    def tiles_moved(n, src, dst, ss, rs):
        return pltpu.make_async_remote_copy(
            src.at[pl.ds(0, n)], dst.at[pl.ds(0, n)], ss, rs, device_id=plane(1), device_id_type=MESH)

    for i in range(nown):
        @pl.when(me != i * stride)
        def _():
            to_owner(i).start()

    for c in near_up + near_dn + pass_up + pass_dn:
        c.wait_recv()
    x4[:, :qc] = jnp.concatenate([e4[:, pl.ds(mid, qc)]] + [q4[r] for r in range(3)], axis=0)

    @pl.when(owns)
    def _():
        rbuf[me] = gr[mine]
        tiles_moved(ns - 1, rbuf, rbuf, s1.at[0], r1.at[0]).wait_recv()
        gs[mine] = jnp.sum(rbuf[...], axis=0)

        def send_one(d, carry):
            pltpu.make_async_remote_copy(
                gs.at[mine], gs.at[mine], s2.at[0], r2.at[0],
                device_id=plane(d), device_id_type=MESH).start()
            return carry

        lax.fori_loop(1, ns, send_one, 0)
        tiles_moved(nown - 1, gs, gs, s2.at[0], r2.at[0]).wait_recv()

    @pl.when(jnp.logical_not(owns))
    def _():
        tiles_moved(nown, gs, gs, s2.at[0], r2.at[0]).wait_recv()

    mixing = transform(gs[...].reshape(members, LANES), members, yref, zref).astype(BF16)

    q = iota((members, LANES), 0)
    slot = jnp.where(q < 16 * nm, q // 16, (q - 16 * nm) // (own - 16))
    inner = jnp.where(q < 16 * nm, q % 16, 16 + (q - 16 * nm) % (own - 16))
    dist = jnp.where(slot == 0, 0, jnp.where(slot == 1, nm - 1, slot - 1))
    tab[:members, :LANES] = onehot(iota((members, LANES), 1) == (z + dist) % nm * own + inner).astype(BF16)
    padded = jnp.concatenate([mixing, jnp.zeros((LANES - members, LANES), BF16)], axis=0)
    turned = nt(tab[:members, :LANES], padded).astype(BF16)
    mixp[...] = nt(turned, tab[:members, :LANES]).astype(BF16)

    wide_rows = 16 * nm
    x = jnp.concatenate([e16[:, pl.ds(mid, qc)]] + [q16[r] for r in range(3)] + [x4[:, :qc]], axis=0)
    res = jnp.dot(mixp[...], x, preferred_element_type=F32)
    for t in range(nm):
        w16[t] = res[16 * t : 16 * (t + 1)].astype(BF16)
        w4[t] = res[wide_rows + (own - 16) * t : wide_rows + (own - 16) * (t + 1)].astype(BF16)
    for c in back1:
        c.start()
    local = [
        pltpu.make_async_copy(w16.at[0], out_at(mid, qc)[0], osem.at[0]),
        pltpu.make_async_copy(w4.at[0], out_at(mid, qc)[1], osem.at[1]),
    ]
    for c in local:
        c.start()

    for c in over_up + over_dn + full_up1 + full_dn0:
        c.wait_recv()
    mine_rows = jnp.concatenate([mixp[:16], mixp[wide_rows:]], axis=0)
    step = fc // FSTEPS
    for i in range(FSTEPS):
        cut = slice(i * step, (i + 1) * step)
        x = jnp.concatenate(
            [e16[:, cut]] + [f16[r, :, cut] for r in range(3)]
            + [e4[:, cut]] + [f4[r, :, cut] for r in range(3)], axis=0)
        res = jnp.dot(mine_rows, x, preferred_element_type=F32)
        u16[:, cut] = res[:16].astype(BF16)
        u4[:, cut] = res[16:own].astype(BF16)
        if i == FSTEPS // 2 - 1:
            for c in back_first_up + back_first_dn:
                c.wait_recv()
            for c in back2:
                c.start()
    more = [
        pltpu.make_async_copy(u16, out_at(0, fc)[0], osem.at[2]),
        pltpu.make_async_copy(u4, out_at(0, fc)[1], osem.at[3]),
    ]
    for c in more:
        c.start()

    for c in back_near_up + back_near_dn + back2:
        c.wait_recv()
    for c in wave1 + wave2 + back1 + back2 + direct + passed:
        c.wait_send()
    for c in local + more:
        c.wait()
    packets.wait_send()

    @pl.when(owns)
    def _():
        tiles_moved(nown - 1, gr, rbuf, s1.at[0], r1.at[0]).wait_send()
        tiles_moved(ns - 1, rbuf, rbuf, s2.at[0], r2.at[0]).wait_send()

    @pl.when(jnp.logical_not(owns))
    def _():
        tiles_moved(nown, gr, rbuf, s1.at[0], r1.at[0]).wait_send()


def per_device(ns, nm, ensemble, weights, seg_obs, observed, inv_var):
    own, cells = ensemble.shape
    tiles, slots, _ = weights.shape
    share = observed.shape[0] // ns
    members = own * nm
    nown = 10 if ns >= 10 else 2
    groups = tiles // GT
    his = share // LANES
    wts = jnp.transpose(weights, (1, 0, 2)).reshape(slots, groups, GT, LANES)
    ids = jnp.transpose(seg_obs)
    obs = observed.reshape(ns, his, LANES)
    var = inv_var.reshape(ns, his, LANES)
    anyspec = pl.BlockSpec(memory_space=pl.ANY)
    dma = pltpu.SemaphoreType.DMA
    two = 2 * GT * slots
    fc = cells * FULL // 16
    qc = (cells - fc) // nm
    rest = own - 16
    o16, o4 = pl.pallas_call(
        functools.partial(kernel, ns, nm, own, tiles, slots, share, nown, fc),
        out_shape=(
            jax.ShapeDtypeStruct((16, cells), BF16),
            jax.ShapeDtypeStruct((rest, cells), BF16),
        ),
        in_specs=[anyspec] * 5,
        out_specs=(anyspec, anyspec),
        scratch_shapes=[
            pltpu.VMEM((3, 16, fc), BF16),
            pltpu.VMEM((3, rest, fc), BF16),
            pltpu.VMEM((3, 16, qc), BF16),
            pltpu.VMEM((3, rest, qc), BF16),
            pltpu.VMEM((2, 16, qc // 2), BF16),
            pltpu.VMEM((2, rest, qc // 2), BF16),
            pltpu.VMEM((rest * nm, qc), BF16),
            pltpu.VMEM((nm, 16, qc), BF16),
            pltpu.VMEM((nm, rest, qc), BF16),
            pltpu.VMEM((2, 16, qc // 2), BF16),
            pltpu.VMEM((2, rest, qc // 2), BF16),
            pltpu.VMEM((16, fc), BF16),
            pltpu.VMEM((rest, fc), BF16),
            pltpu.VMEM((members, members), BF16),
            pltpu.VMEM((members, LANES), F32),
            pltpu.VMEM((members, LANES), F32),
            pltpu.VMEM((two, two), BF16),
            pltpu.VMEM((2 * LANES, ns * LANES), BF16),
            pltpu.VMEM((16, cells), BF16),
            pltpu.VMEM((own - 16, cells), BF16),
            pltpu.VMEM((slots, groups, GT, LANES), BF16),
            pltpu.VMEM((slots, tiles), I32),
            pltpu.VMEM((his, LANES), F32),
            pltpu.VMEM((his, LANES), F32),
            pltpu.VMEM((ns // 2 * GT, 2 * two), BF16),
            pltpu.VMEM((2 * LANES, groups * two), BF16),
            pltpu.VMEM((ns // 2 * GT, 2 * LANES), F32),
            pltpu.VMEM((ns, GT, LANES), BF16),
            pltpu.VMEM((ns, GT, LANES), BF16),
            pltpu.VMEM((own * 8, 2 * LANES), F32),
            pltpu.VMEM((nm, own * 8, 2 * LANES), BF16),
            pltpu.VMEM((2 * members * 8, LANES), F32),
            pltpu.VMEM((LANES, share), F32),
            pltpu.VMEM((members, share), F32),
            pltpu.VMEM((nown, members // nown, LANES), F32),
            pltpu.VMEM((ns, members // nown, LANES), F32),
            pltpu.VMEM((nown, members // nown, LANES), F32),
            dma((6,)), dma((36,)), dma((36,)), dma((1,)), dma((1,)),
            dma((6,)), dma((6,)), dma((1,)), dma((1,)), dma((1,)), dma((1,)), dma((4,)),
        ],
        compiler_params=pltpu.CompilerParams(collective_id=0, has_side_effects=True),
        name="assimilate",
    )(ensemble, wts, ids, obs, var)
    return jnp.concatenate([o16, o4], axis=0)


def solution(mesh):
    return jax.shard_map(
        functools.partial(per_device, mesh.shape["state"], mesh.shape["mem"]),
        mesh=mesh,
        in_specs=(P("mem", "state"), P("state", None, None), P("state", None), P(), P()),
        out_specs=P("mem", "state"),
        check_vma=False,
    )
```

```python
import functools
import math

import jax
import jax.numpy as jnp
from jax import lax
from jax.experimental import pallas as pl
from jax.experimental.pallas import tpu as pltpu
from jax.sharding import PartitionSpec as P

ITERS = 14
F32, BF16, I32 = jnp.float32, jnp.bfloat16, jnp.int32
MESH = pl.DeviceIdType.MESH
GT = 16
FULL = 8
FSTEPS = 4
START = 5
LANES = 128


def nt(a, b, precision=None):
    return lax.dot_general(
        a, b, (((1,), (1,)), ((), ())), precision=precision, preferred_element_type=F32
    )


def iota(shape, dim):
    return lax.broadcasted_iota(I32, shape, dim)


def onehot(mask):
    return jnp.where(mask, 1.0, 0.0)


def split(x):
    high = x.astype(BF16)
    return high, (x - high.astype(F32)).astype(BF16)


def tall(x):
    high, low = split(x)
    pad = jnp.zeros((LANES - x.shape[0], LANES), BF16)
    return jnp.concatenate([high, pad, high, pad, low, pad], axis=0)


def wide(x):
    high, low = split(x)
    return jnp.concatenate([high, low, high], axis=1)


def product(left, right):
    return jnp.dot(left, right, preferred_element_type=F32)


def transform(total, members, yref, zref):
    shape = (members, LANES)
    down, across = iota(shape, 0), iota(shape, 1)
    identity = onehot(down == across)
    system = (members - 1.0) * identity + jnp.where(across < members, total, 0.0)
    scaling = jnp.sqrt(jnp.sum(jnp.sum(system * system, axis=1, keepdims=True), axis=0, keepdims=True))
    yref[...] = system / scaling
    zref[...] = identity

    def step(_, carry):
        y, z = yref[...], zref[...]
        c = 1.5 * identity - 0.5 * product(wide(z), tall(y))
        yref[...] = product(wide(y), tall(c))
        zref[...] = product(wide(c), tall(z))
        return carry

    lax.fori_loop(0, ITERS, step, 0)
    root = zref[...] / jnp.sqrt(scaling)
    left = wide(root)
    twice = product(left, tall(product(left, tall(total))))
    mixed = twice[:, members : members + 1] + math.sqrt(members - 1.0) * root
    mixed = mixed + (1.0 - jnp.sum(mixed, axis=0, keepdims=True)) / members
    return jnp.where(across < members, mixed, 0.0)


def kernel(
    ns, nm, own, tiles, slots, share, nown, fc,
    ens, wts, ids, obs, var,
    o16, o4,
    f16, f4, q16, q4, t16, t4, x4, w16, w4, v16, v4, mixp,
    yref, zref, tab, rgt, e16, e4, wv, idv, ob, va, lhs, sel, acc, pk, rx, acc2, hg, hf, an, wa, gr, rbuf, gs,
    lsem, bs, br, ps, pr, zs, zr, s1, r1, s2, r2,
):
    me = lax.axis_index("state")
    z = lax.axis_index("mem")
    groups = tiles // GT
    cells = tiles * LANES
    qc = (cells - fc) // nm
    his = share // LANES
    members = own * nm
    chunk = members // nown
    stride = ns // nown
    col = GT * GT
    two = 2 * GT * slots
    pairs = groups // 2
    part = (slots - 8) * GT
    hw = ns // 2

    loads = [
        pltpu.make_async_copy(ens.at[pl.ds(0, 16)], e16, lsem.at[0]),
        pltpu.make_async_copy(ens.at[pl.ds(16, own - 16)], e4, lsem.at[1]),
        pltpu.make_async_copy(wts, wv, lsem.at[2]),
        pltpu.make_async_copy(ids, idv, lsem.at[3]),
        pltpu.make_async_copy(obs.at[me], ob, lsem.at[4]),
        pltpu.make_async_copy(var.at[me], va, lsem.at[5]),
    ]
    for c in loads:
        c.start()

    def plane(d):
        return {"state": lax.rem(me + d, ns)}

    def along(d):
        return {"mem": lax.rem(z + d, nm)}

    barrier = pltpu.get_barrier_semaphore()
    for d in range(1, nm):
        pl.semaphore_signal(barrier, inc=1, device_id=along(d), device_id_type=MESH)

    def greet(d, carry):
        pl.semaphore_signal(barrier, inc=1, device_id=plane(d), device_id_type=MESH)
        return carry

    lax.fori_loop(1, ns, greet, 0)

    count = [0]

    def pair(src16, src4, dst16, dst4, d):
        n = count[0]
        count[0] += 2
        return [
            pltpu.make_async_remote_copy(
                src, dst, bs.at[n + i], br.at[n + i], device_id=along(d), device_id_type=MESH)
            for i, (src, dst) in enumerate(((src16, dst16), (src4, dst4)))
        ]

    up, dn = 1, nm - 1
    fh, qh = fc // 2, qc // 2

    def quarter(d):
        return pl.multiple_of(fc + lax.rem(z + d, nm) * qc, LANES)

    def own_at(at, n):
        return e16.at[:, pl.ds(at, n)], e4.at[:, pl.ds(at, n)]

    def at(pairs, slot, start, n):
        return tuple(ref.at[slot, :, pl.ds(start, n)] for ref in pairs)

    first_up = pair(*own_at(quarter(2), qh), *at((t16, t4), 0, 0, qh), up)
    first_dn = pair(*own_at(quarter(2) + qh, qh), *at((t16, t4), 1, 0, qh), dn)
    near_up = pair(*own_at(quarter(up), qc), *at((q16, q4), 0, 0, qc), up)
    near_dn = pair(*own_at(quarter(dn), qc), *at((q16, q4), 1, 0, qc), dn)
    pass_up = pair(*at((t16, t4), 0, 0, qh), *at((q16, q4), 2, 0, qh), up)
    pass_dn = pair(*at((t16, t4), 1, 0, qh), *at((q16, q4), 2, qh, qh), dn)
    full_up0 = pair(*own_at(0, fh), *at((f16, f4), 0, 0, fh), up)
    full_dn1 = pair(*own_at(fh, fh), *at((f16, f4), 1, fh, fh), dn)
    full_up1 = pair(*own_at(fh, fh), *at((f16, f4), 0, fh, fh), up)
    full_dn0 = pair(*own_at(0, fh), *at((f16, f4), 1, 0, fh), dn)
    over_up = pair(*at((f16, f4), 0, 0, fh), *at((f16, f4), 2, 0, fh), up)
    over_dn = pair(*at((f16, f4), 1, fh, fh), *at((f16, f4), 2, fh, fh), dn)
    wave1 = first_up + first_dn + full_up0 + full_dn1
    wave2 = near_up + near_dn + pass_up + pass_dn + over_up + over_dn + full_up1 + full_dn0
    mid = pl.multiple_of(fc + z * qc, LANES)
    far = pl.multiple_of(fc + lax.rem(z + 2, nm) * qc, LANES)

    def out_at(start, n):
        return o16.at[:, pl.ds(start, n)], o4.at[:, pl.ds(start, n)]

    back_first_up = pair(*at((w16, w4), 3, 0, qh), *at((v16, v4), 0, 0, qh), up)
    back_first_dn = pair(*at((w16, w4), 3, qh, qh), *at((v16, v4), 1, 0, qh), dn)
    back_near_up = pair(*at((w16, w4), 2, 0, qc), *out_at(mid, qc), up)
    back_near_dn = pair(*at((w16, w4), 1, 0, qc), *out_at(mid, qc), dn)
    before_mid = pl.multiple_of(fc + lax.rem(z + dn, nm) * qc, LANES)
    after_mid = pl.multiple_of(fc + lax.rem(z + up, nm) * qc, LANES)
    back_pass_up = pair(*at((v16, v4), 0, 0, qh), *out_at(before_mid, qh), up)
    back_pass_dn = pair(*at((v16, v4), 1, 0, qh), *out_at(after_mid + qh, qh), dn)
    back1 = back_first_up + back_first_dn + back_near_up + back_near_dn
    back2 = back_pass_up + back_pass_dn

    loads[3].wait()
    raw = jnp.concatenate([idv[...], jnp.zeros((GT - slots, tiles), I32)], axis=0)
    tab[:tiles, :col] = onehot(iota((tiles, col), 0) % GT == iota((tiles, col), 1) % GT).astype(BF16)
    spread = tab[:tiles, :col]
    order = list(range(0, groups, 2)) + list(range(1, groups, 2))

    def regroup(byte):
        byte = byte.astype(F32)
        high = jnp.concatenate(
            [jnp.where(iota((GT, tiles), 1) // GT == g, byte, 0.0) for g in order], axis=0
        ).astype(BF16)
        out = jnp.dot(high, spread, preferred_element_type=F32).reshape(groups, GT, col)
        at_lane = iota((groups, GT, col), 2)
        shift = jnp.where(jnp.logical_and(iota((groups, GT, col), 0) >= pairs, at_lane >= LANES), part, 0)
        keep = iota((groups, GT, col), 1) == (at_lane - shift) // GT
        return jnp.sum(jnp.where(keep, out, 0.0), axis=1)

    ident = regroup(raw // 256) * 256.0 + regroup(raw % 256)
    beyond = jnp.where(iota((pairs, LANES), 1) < part, ident[:pairs, LANES:], ident[pairs:, LANES:])
    ident = jnp.concatenate([ident[:pairs, :LANES], ident[pairs:, :LANES], beyond], axis=1).astype(I32)
    owner = ident // share
    place = ident % share
    code = jnp.left_shift(1, place // LANES).astype(F32) * (1.0 + (place % LANES).astype(F32) / LANES)

    ones = [onehot(iota((ns, two), 0) == owner[g : g + 1]) for g in range(pairs)]
    tab[...] = onehot(iota((two, two), 0) < iota((two, two), 1)).astype(BF16)
    before = jnp.dot(
        jnp.concatenate([a.astype(BF16) for a in ones], axis=0), tab[...], preferred_element_type=F32
    )
    run = jnp.zeros((ns, 1), F32)
    ranks = []
    for g in range(pairs):
        rank = jnp.sum(ones[g] * (before[g * ns : (g + 1) * ns] + run), axis=0, keepdims=True)
        run = run + jnp.sum(ones[g], axis=1, keepdims=True)
        rank = rank.astype(I32)
        ranks.append(rank)
        side = owner[g : g + 1] // hw * LANES
        sel[:, 2 * g * two : (2 * g + 1) * two] = onehot(
            iota((2 * LANES, two), 0) == rank + side
        ).astype(BF16)
        sel[:, (2 * g + 1) * two : (2 * g + 2) * two] = onehot(
            iota((2 * LANES, two), 0) == LANES - 32 + rank % 32 + side
        ).astype(BF16)

    loads[2].wait()
    loads[0].wait()
    loads[1].wait()
    lane = iota((GT, col), 1) % GT
    lane8 = iota((8, col), 1) % GT - iota((8, col), 0) // 4
    row = iota((GT, two), 0)
    gap = jnp.zeros((col - slots * GT, LANES), BF16)

    def values(g):
        w = wv[:, g].reshape(slots * GT, LANES)
        if g % 2:
            w = jnp.concatenate([w[:LANES], gap, w[LANES:]], axis=0)
        else:
            w = jnp.concatenate([w, gap], axis=0)
        a = e16[:, g * GT * LANES : (g + 1) * GT * LANES]
        b = e4[:, g * GT * LANES : (g + 1) * GT * LANES]
        a = nt(jnp.concatenate([a[:, t * LANES : (t + 1) * LANES] for t in range(GT)], axis=0), w)
        b = nt(jnp.concatenate([b[:, t * LANES : (t + 1) * LANES] for t in range(GT)], axis=0), w)
        first = jnp.zeros((GT, col), F32)
        second = jnp.zeros((8, col), F32)
        for t in range(GT):
            first = jnp.where(lane == t, a[t * GT : (t + 1) * GT], first)
        for t in range(0, GT, 2):
            second = jnp.where(lane8 == t, b[t * 4 : t * 4 + 8], second)
        return first, second[:4] + second[4:]

    def joined(even, odd):
        return jnp.concatenate([even[:, :LANES], odd[:, :LANES], even[:, LANES:] + odd[:, LANES:]], axis=1)

    for g in range(pairs):
        even, odd = values(2 * g), values(2 * g + 1)
        first, second = joined(even[0], odd[0]), joined(even[1], odd[1])
        extra = [second[r : r + 1] for r in range(own - 16)] + [code[g : g + 1]]
        rest = jnp.zeros((GT, two), F32)
        for r, line in enumerate(extra):
            rest = jnp.where(row // 3 == r, line, rest)
        rest = jnp.where(row % 3 == ranks[g] // 32, rest, 0.0)
        for o in range(hw):
            there = owner[g : g + 1] % hw == o
            lhs[o * GT : (o + 1) * GT, :two] = jnp.where(there, first, 0.0).astype(BF16)
            lhs[o * GT : (o + 1) * GT, two:] = jnp.where(there, rest, 0.0).astype(BF16)
        both = nt(lhs[...], sel[:, 2 * g * two : (2 * g + 2) * two])
        if g == 0:
            acc[...] = both
        else:
            acc[...] += both
        if g == min(START, pairs) - 1:
            pl.semaphore_wait(barrier, nm - 1 + ns - 1)
            for c in wave1:
                c.start()
    for o in range(ns):
        pk[o] = acc[o % hw * GT : (o % hw + 1) * GT, o // hw * LANES : (o // hw + 1) * LANES].astype(BF16)

    def send(d, carry):
        pltpu.make_async_remote_copy(
            pk.at[lax.rem(me + d, ns)], rx.at[me], ps.at[0], pr.at[0],
            device_id=plane(d), device_id_type=MESH).start()
        return carry

    packets = pltpu.make_async_remote_copy(
        pk.at[pl.ds(0, ns - 1)], rx.at[pl.ds(0, ns - 1)], ps.at[0], pr.at[0],
        device_id=plane(1), device_id_type=MESH)
    lax.fori_loop(1, ns, send, 0)
    rx[me] = pk[me]
    packets.wait_recv()

    spot = iota((1, LANES), 1)
    power = jnp.left_shift(1, iota((8, LANES), 0)).astype(F32)
    inverse = jnp.left_shift(1, 7 - iota((8, LANES), 0)).astype(F32)
    down = iota((2 * LANES, LANES), 0)
    for i in range(ns // 8):
        left = []
        for q in range(8):
            p = rx[i * 8 + q].astype(F32)
            r1x, r2x, r3x = (pltpu.roll(p, 32 * (t + 1), 1) for t in range(3))
            lines = [p[k : k + 1] for k in range(16)]
            for r in range(own - 15):
                line = jnp.where(spot < 96, r3x[3 * r + 2 : 3 * r + 3], 0.0)
                line = jnp.where(spot < 64, r2x[3 * r + 1 : 3 * r + 2], line)
                lines.append(jnp.where(spot < 32, r1x[3 * r : 3 * r + 1], line))
            where = lines.pop()
            upper = where >= 256.0
            where = jnp.where(upper, where * (1.0 / 256.0), where)
            top = jnp.logical_and(where >= power, where < 2.0 * power)
            left.append(
                jnp.concatenate([jnp.where(top, v, 0.0) for v in lines], axis=0).astype(BF16)
            )
            low = where * jnp.sum(jnp.where(top, inverse, 0.0), axis=0, keepdims=True)
            low = low.astype(I32) - LANES + jnp.where(upper, LANES, 0)
            rgt[:, (i * 8 + q) * LANES : (i * 8 + q + 1) * LANES] = onehot(down == low).astype(BF16)
        both = nt(jnp.concatenate(left, axis=1), rgt[:, i * 8 * LANES : (i + 1) * 8 * LANES])
        if i == 0:
            acc2[...] = both
        else:
            acc2[...] += both
    hg[z] = acc2[...].astype(BF16)

    hrow = own * 8 // 2

    def members_copy(slot, rows, d, n):
        ref = hg.at[slot, pl.ds(rows * hrow, hrow)]
        return pltpu.make_async_remote_copy(
            ref, ref, zs.at[n], zr.at[n], device_id=along(d), device_id_type=MESH)

    before, after = lax.rem(z + dn, nm), lax.rem(z + up, nm)
    direct = [
        members_copy(z, 0, up, 0), members_copy(z, 1, dn, 1),
        members_copy(z, 1, up, 2), members_copy(z, 0, dn, 3),
    ]
    passed = [members_copy(before, 0, up, 4), members_copy(after, 1, dn, 5)]
    for c in direct:
        c.start()
    for c, e in zip(direct[:2], passed):
        c.wait_recv()
        e.start()
    for c in first_up + first_dn + full_up0 + full_dn1:
        c.wait_recv()
    for c in wave2:
        c.start()
    for c in direct[2:] + passed:
        c.wait_recv()

    loads[4].wait()
    loads[5].wait()
    rows = members * 8
    for c in range(2):
        hf[c * rows : (c + 1) * rows] = hg[:, :, c * LANES : (c + 1) * LANES].astype(F32).reshape(rows, LANES)
    for h in range(8):
        x = jnp.concatenate([hf[pl.ds(c * rows + h, members, stride=8), :] for c in range(2)], axis=1)
        seen = jnp.concatenate([ob[h : h + 1], ob[h + 8 : h + 9]], axis=1)
        weight = jnp.concatenate([va[h : h + 1], va[h + 8 : h + 9]], axis=1)
        ybar = jnp.sum(x, axis=0, keepdims=True) / members
        dev = x - ybar
        cut = slice(h * 2 * LANES, (h + 1) * 2 * LANES)
        an[:members, cut] = dev
        an[members:, cut] = jnp.where(
            iota((LANES - members, 2 * LANES), 0) == 0, seen - ybar, 0.0
        )
        wa[:, cut] = dev * weight
    gr[...] = nt(wa[...], an[...], lax.Precision.HIGHEST).reshape(nown, chunk, LANES)

    mine = me // stride
    owns = jnp.logical_and(lax.rem(me, stride) == 0, mine < nown)

    def to_owner(i):
        return pltpu.make_async_remote_copy(
            gr.at[i], rbuf.at[me], s1.at[0], r1.at[0],
            device_id={"state": i * stride}, device_id_type=MESH)

    def tiles_moved(n, src, dst, ss, rs):
        return pltpu.make_async_remote_copy(
            src.at[pl.ds(0, n)], dst.at[pl.ds(0, n)], ss, rs, device_id=plane(1), device_id_type=MESH)

    for i in range(nown):
        @pl.when(me != i * stride)
        def _():
            to_owner(i).start()

    for c in near_up + near_dn + pass_up + pass_dn:
        c.wait_recv()
    x4[:, :qc] = jnp.concatenate([e4[:, pl.ds(mid, qc)]] + [q4[r] for r in range(3)], axis=0)

    @pl.when(owns)
    def _():
        rbuf[me] = gr[mine]
        tiles_moved(ns - 1, rbuf, rbuf, s1.at[0], r1.at[0]).wait_recv()
        gs[mine] = jnp.sum(rbuf[...], axis=0)

        def send_one(d, carry):
            pltpu.make_async_remote_copy(
                gs.at[mine], gs.at[mine], s2.at[0], r2.at[0],
                device_id=plane(d), device_id_type=MESH).start()
            return carry

        lax.fori_loop(1, ns, send_one, 0)
        tiles_moved(nown - 1, gs, gs, s2.at[0], r2.at[0]).wait_recv()

    @pl.when(jnp.logical_not(owns))
    def _():
        tiles_moved(nown, gs, gs, s2.at[0], r2.at[0]).wait_recv()

    mixing = transform(gs[...].reshape(members, LANES), members, yref, zref).astype(BF16)

    q = iota((members, LANES), 0)
    slot = jnp.where(q < 16 * nm, q // 16, (q - 16 * nm) // (own - 16))
    inner = jnp.where(q < 16 * nm, q % 16, 16 + (q - 16 * nm) % (own - 16))
    dist = jnp.where(slot == 0, 0, jnp.where(slot == 1, nm - 1, slot - 1))
    tab[:members, :LANES] = onehot(iota((members, LANES), 1) == (z + dist) % nm * own + inner).astype(BF16)
    padded = jnp.concatenate([mixing, jnp.zeros((LANES - members, LANES), BF16)], axis=0)
    turned = nt(tab[:members, :LANES], padded).astype(BF16)
    mixp[...] = nt(turned, tab[:members, :LANES]).astype(BF16)

    wide_rows = 16 * nm
    x = jnp.concatenate([e16[:, pl.ds(mid, qc)]] + [q16[r] for r in range(3)] + [x4[:, :qc]], axis=0)
    res = jnp.dot(mixp[...], x, preferred_element_type=F32)
    o16[:, pl.ds(mid, qc)] = res[:16].astype(BF16)
    o4[:, pl.ds(mid, qc)] = res[wide_rows : wide_rows + own - 16].astype(BF16)
    for t in range(1, nm):
        w16[t] = res[16 * t : 16 * (t + 1)].astype(BF16)
        w4[t] = res[wide_rows + (own - 16) * t : wide_rows + (own - 16) * (t + 1)].astype(BF16)
    for c in back1:
        c.start()

    for c in over_up + over_dn + full_up1 + full_dn0:
        c.wait_recv()
    mine_rows = jnp.concatenate([mixp[:16], mixp[wide_rows:]], axis=0)
    step = fc // FSTEPS
    for i in range(FSTEPS):
        cut = slice(i * step, (i + 1) * step)
        x = jnp.concatenate(
            [e16[:, cut]] + [f16[r, :, cut] for r in range(3)]
            + [e4[:, cut]] + [f4[r, :, cut] for r in range(3)], axis=0)
        res = jnp.dot(mine_rows, x, preferred_element_type=F32)
        o16[:, cut] = res[:16].astype(BF16)
        o4[:, cut] = res[16:own].astype(BF16)
        if i == FSTEPS // 2 - 1:
            for c in back_first_up + back_first_dn:
                c.wait_recv()
            for c in back2:
                c.start()
    for c in back_near_up + back_near_dn + back2:
        c.wait_recv()
    for c in wave1 + wave2 + back1 + back2 + direct + passed:
        c.wait_send()
    packets.wait_send()

    @pl.when(owns)
    def _():
        tiles_moved(nown - 1, gr, rbuf, s1.at[0], r1.at[0]).wait_send()
        tiles_moved(ns - 1, rbuf, rbuf, s2.at[0], r2.at[0]).wait_send()

    @pl.when(jnp.logical_not(owns))
    def _():
        tiles_moved(nown, gr, rbuf, s1.at[0], r1.at[0]).wait_send()


def per_device(ns, nm, ensemble, weights, seg_obs, observed, inv_var):
    own, cells = ensemble.shape
    tiles, slots, _ = weights.shape
    share = observed.shape[0] // ns
    members = own * nm
    nown = 10 if ns >= 10 else 2
    groups = tiles // GT
    his = share // LANES
    wts = jnp.transpose(weights, (1, 0, 2)).reshape(slots, groups, GT, LANES)
    ids = jnp.transpose(seg_obs)
    obs = observed.reshape(ns, his, LANES)
    var = inv_var.reshape(ns, his, LANES)
    anyspec = pl.BlockSpec(memory_space=pl.ANY)
    dma = pltpu.SemaphoreType.DMA
    vspec = pl.BlockSpec(memory_space=pltpu.VMEM)
    two = 2 * GT * slots
    fc = cells * FULL // 16
    qc = (cells - fc) // nm
    rest = own - 16
    o16, o4 = pl.pallas_call(
        functools.partial(kernel, ns, nm, own, tiles, slots, share, nown, fc),
        out_shape=(
            pltpu.VMEM((16, cells), BF16),
            pltpu.VMEM((rest, cells), BF16),
        ),
        in_specs=[anyspec] * 5,
        out_specs=(vspec, vspec),
        scratch_shapes=[
            pltpu.VMEM((3, 16, fc), BF16),
            pltpu.VMEM((3, rest, fc), BF16),
            pltpu.VMEM((3, 16, qc), BF16),
            pltpu.VMEM((3, rest, qc), BF16),
            pltpu.VMEM((2, 16, qc // 2), BF16),
            pltpu.VMEM((2, rest, qc // 2), BF16),
            pltpu.VMEM((rest * nm, qc), BF16),
            pltpu.VMEM((nm, 16, qc), BF16),
            pltpu.VMEM((nm, rest, qc), BF16),
            pltpu.VMEM((2, 16, qc // 2), BF16),
            pltpu.VMEM((2, rest, qc // 2), BF16),
            pltpu.VMEM((members, members), BF16),
            pltpu.VMEM((members, LANES), F32),
            pltpu.VMEM((members, LANES), F32),
            pltpu.VMEM((two, two), BF16),
            pltpu.VMEM((2 * LANES, ns * LANES), BF16),
            pltpu.VMEM((16, cells), BF16),
            pltpu.VMEM((own - 16, cells), BF16),
            pltpu.VMEM((slots, groups, GT, LANES), BF16),
            pltpu.VMEM((slots, tiles), I32),
            pltpu.VMEM((his, LANES), F32),
            pltpu.VMEM((his, LANES), F32),
            pltpu.VMEM((ns // 2 * GT, 2 * two), BF16),
            pltpu.VMEM((2 * LANES, groups * two), BF16),
            pltpu.VMEM((ns // 2 * GT, 2 * LANES), F32),
            pltpu.VMEM((ns, GT, LANES), BF16),
            pltpu.VMEM((ns, GT, LANES), BF16),
            pltpu.VMEM((own * 8, 2 * LANES), F32),
            pltpu.VMEM((nm, own * 8, 2 * LANES), BF16),
            pltpu.VMEM((2 * members * 8, LANES), F32),
            pltpu.VMEM((LANES, share), F32),
            pltpu.VMEM((members, share), F32),
            pltpu.VMEM((nown, members // nown, LANES), F32),
            pltpu.VMEM((ns, members // nown, LANES), F32),
            pltpu.VMEM((nown, members // nown, LANES), F32),
            dma((6,)), dma((36,)), dma((36,)), dma((1,)), dma((1,)),
            dma((6,)), dma((6,)), dma((1,)), dma((1,)), dma((1,)), dma((1,)),
        ],
        compiler_params=pltpu.CompilerParams(collective_id=0, has_side_effects=True),
        name="assimilate",
    )(ensemble, wts, ids, obs, var)
    def settle(o16_ref, o4_ref, out, sem):
        moves = [
            pltpu.make_async_copy(o16_ref, out.at[pl.ds(0, 16)], sem.at[0]),
            pltpu.make_async_copy(o4_ref, out.at[pl.ds(16, rest)], sem.at[1]),
        ]
        for c in moves:
            c.start()
        for c in moves:
            c.wait()

    return pl.pallas_call(
        settle,
        out_shape=jax.ShapeDtypeStruct((own, cells), BF16),
        in_specs=[vspec] * 2,
        out_specs=anyspec,
        scratch_shapes=[dma((2,))],
        name="settle",
    )(*(pltpu.with_memory_space_constraint(o, pltpu.VMEM) for o in (o16, o4)))


def solution(mesh):
    return jax.shard_map(
        functools.partial(per_device, mesh.shape["state"], mesh.shape["mem"]),
        mesh=mesh,
        in_specs=(P("mem", "state"), P("state", None, None), P("state", None), P(), P()),
        out_specs=P("mem", "state"),
        check_vma=False,
    )
```

```python
import functools
import math

import jax
import jax.numpy as jnp
from jax import lax
from jax.experimental import pallas as pl
from jax.experimental.pallas import tpu as pltpu
from jax.sharding import PartitionSpec as P

ITERS = 14
F32, BF16, I32 = jnp.float32, jnp.bfloat16, jnp.int32
MESH = pl.DeviceIdType.MESH
GT = 16
FULL = 9
FSTEPS = 4
BATCH = 4
START = 5
LANES = 128


def nt(a, b, precision=None):
    return lax.dot_general(
        a, b, (((1,), (1,)), ((), ())), precision=precision, preferred_element_type=F32
    )


def iota(shape, dim):
    return lax.broadcasted_iota(I32, shape, dim)


def onehot(mask):
    return jnp.where(mask, 1.0, 0.0)


def split(x):
    high = x.astype(BF16)
    return high, (x - high.astype(F32)).astype(BF16)


def tall(x):
    high, low = split(x)
    pad = jnp.zeros((LANES - x.shape[0], LANES), BF16)
    return jnp.concatenate([high, pad, high, pad, low, pad], axis=0)


def wide(x):
    high, low = split(x)
    return jnp.concatenate([high, low, high], axis=1)


def product(left, right):
    return jnp.dot(left, right, preferred_element_type=F32)


def transform(total, members, yref, zref):
    shape = (members, LANES)
    down, across = iota(shape, 0), iota(shape, 1)
    identity = onehot(down == across)
    system = (members - 1.0) * identity + jnp.where(across < members, total, 0.0)
    scaling = jnp.sqrt(jnp.sum(jnp.sum(system * system, axis=1, keepdims=True), axis=0, keepdims=True))
    yref[...] = system / scaling
    zref[...] = identity

    def step(_, carry):
        y, z = yref[...], zref[...]
        c = 1.5 * identity - 0.5 * product(wide(z), tall(y))
        yref[...] = product(wide(y), tall(c))
        zref[...] = product(wide(c), tall(z))
        return carry

    lax.fori_loop(0, ITERS, step, 0)
    root = zref[...] / jnp.sqrt(scaling)
    left = wide(root)
    twice = product(left, tall(product(left, tall(total))))
    mixed = twice[:, members : members + 1] + math.sqrt(members - 1.0) * root
    mixed = mixed + (1.0 - jnp.sum(mixed, axis=0, keepdims=True)) / members
    return jnp.where(across < members, mixed, 0.0)


def kernel(
    ns, nm, own, tiles, slots, share, nown, fc,
    ens, wts, ids, obs, var,
    o16, o4,
    f16, f4, q16, q4, t16, t4, x4, w16, w4, v16, v4, mixp,
    yref, zref, tab, rgt, e16, e4, wv, idv, ob, va, lhs, sel, acc, pk, rx, acc2, hg, hf, an, wa, gr, rbuf, gs,
    lsem, bs, br, ps, pr, zs, zr, s1, r1, s2, r2,
):
    me = lax.axis_index("state")
    z = lax.axis_index("mem")
    groups = tiles // GT
    cells = tiles * LANES
    qc = (cells - fc) // nm
    his = share // LANES
    members = own * nm
    chunk = members // nown
    stride = ns // nown
    col = GT * GT
    two = 2 * GT * slots
    pairs = groups // 2
    part = (slots - 8) * GT
    hw = ns // 2

    loads = [
        pltpu.make_async_copy(ens.at[pl.ds(0, 16)], e16, lsem.at[0]),
        pltpu.make_async_copy(ens.at[pl.ds(16, own - 16)], e4, lsem.at[1]),
        pltpu.make_async_copy(wts, wv, lsem.at[2]),
        pltpu.make_async_copy(ids, idv, lsem.at[3]),
        pltpu.make_async_copy(obs.at[me], ob, lsem.at[4]),
        pltpu.make_async_copy(var.at[me], va, lsem.at[5]),
    ]
    for c in loads:
        c.start()

    def plane(d):
        return {"state": lax.rem(me + d, ns)}

    def along(d):
        return {"mem": lax.rem(z + d, nm)}

    barrier = pltpu.get_barrier_semaphore()
    for d in range(1, nm):
        pl.semaphore_signal(barrier, inc=1, device_id=along(d), device_id_type=MESH)

    def greet(d, carry):
        pl.semaphore_signal(barrier, inc=1, device_id=plane(d), device_id_type=MESH)
        return carry

    lax.fori_loop(1, ns, greet, 0)

    count = [0]

    def pair(src16, src4, dst16, dst4, d):
        n = count[0]
        count[0] += 2
        return [
            pltpu.make_async_remote_copy(
                src, dst, bs.at[n + i], br.at[n + i], device_id=along(d), device_id_type=MESH)
            for i, (src, dst) in enumerate(((src16, dst16), (src4, dst4)))
        ]

    up, dn = 1, nm - 1
    fh, qh = fc // 2, qc // 2

    def quarter(d):
        return pl.multiple_of(fc + lax.rem(z + d, nm) * qc, LANES)

    def own_at(at, n):
        return e16.at[:, pl.ds(at, n)], e4.at[:, pl.ds(at, n)]

    def at(pairs, slot, start, n):
        return tuple(ref.at[slot, :, pl.ds(start, n)] for ref in pairs)

    first_up = pair(*own_at(quarter(2), qh), *at((t16, t4), 0, 0, qh), up)
    first_dn = pair(*own_at(quarter(2) + qh, qh), *at((t16, t4), 1, 0, qh), dn)
    near_up = pair(*own_at(quarter(up), qc), *at((q16, q4), 0, 0, qc), up)
    near_dn = pair(*own_at(quarter(dn), qc), *at((q16, q4), 1, 0, qc), dn)
    pass_up = pair(*at((t16, t4), 0, 0, qh), *at((q16, q4), 2, 0, qh), up)
    pass_dn = pair(*at((t16, t4), 1, 0, qh), *at((q16, q4), 2, qh, qh), dn)
    full_up0 = pair(*own_at(0, fh), *at((f16, f4), 0, 0, fh), up)
    full_dn1 = pair(*own_at(fh, fh), *at((f16, f4), 1, fh, fh), dn)
    full_up1 = pair(*own_at(fh, fh), *at((f16, f4), 0, fh, fh), up)
    full_dn0 = pair(*own_at(0, fh), *at((f16, f4), 1, 0, fh), dn)
    over_up = pair(*at((f16, f4), 0, 0, fh), *at((f16, f4), 2, 0, fh), up)
    over_dn = pair(*at((f16, f4), 1, fh, fh), *at((f16, f4), 2, fh, fh), dn)
    wave1 = first_up + first_dn + full_up0 + full_dn1
    wave2 = near_up + near_dn + pass_up + pass_dn + over_up + over_dn + full_up1 + full_dn0
    mid = pl.multiple_of(fc + z * qc, LANES)
    far = pl.multiple_of(fc + lax.rem(z + 2, nm) * qc, LANES)

    def out_at(start, n):
        return o16.at[:, pl.ds(start, n)], o4.at[:, pl.ds(start, n)]

    back_first_up = pair(*at((w16, w4), 3, 0, qh), *at((v16, v4), 0, 0, qh), up)
    back_first_dn = pair(*at((w16, w4), 3, qh, qh), *at((v16, v4), 1, 0, qh), dn)
    back_near_up = pair(*at((w16, w4), 2, 0, qc), *out_at(mid, qc), up)
    back_near_dn = pair(*at((w16, w4), 1, 0, qc), *out_at(mid, qc), dn)
    before_mid = pl.multiple_of(fc + lax.rem(z + dn, nm) * qc, LANES)
    after_mid = pl.multiple_of(fc + lax.rem(z + up, nm) * qc, LANES)
    back_pass_up = pair(*at((v16, v4), 0, 0, qh), *out_at(before_mid, qh), up)
    back_pass_dn = pair(*at((v16, v4), 1, 0, qh), *out_at(after_mid + qh, qh), dn)
    back1 = back_first_up + back_first_dn + back_near_up + back_near_dn
    back2 = back_pass_up + back_pass_dn

    loads[3].wait()
    raw = jnp.concatenate([idv[...], jnp.zeros((GT - slots, tiles), I32)], axis=0)
    tab[:tiles, :col] = onehot(iota((tiles, col), 0) % GT == iota((tiles, col), 1) % GT).astype(BF16)
    spread = tab[:tiles, :col]
    order = list(range(0, groups, 2)) + list(range(1, groups, 2))

    def regroup(byte):
        byte = byte.astype(F32)
        high = jnp.concatenate(
            [jnp.where(iota((GT, tiles), 1) // GT == g, byte, 0.0) for g in order], axis=0
        ).astype(BF16)
        out = jnp.dot(high, spread, preferred_element_type=F32).reshape(groups, GT, col)
        at_lane = iota((groups, GT, col), 2)
        shift = jnp.where(jnp.logical_and(iota((groups, GT, col), 0) >= pairs, at_lane >= LANES), part, 0)
        keep = iota((groups, GT, col), 1) == (at_lane - shift) // GT
        return jnp.sum(jnp.where(keep, out, 0.0), axis=1)

    ident = regroup(raw // 256) * 256.0 + regroup(raw % 256)
    beyond = jnp.where(iota((pairs, LANES), 1) < part, ident[:pairs, LANES:], ident[pairs:, LANES:])
    ident = jnp.concatenate([ident[:pairs, :LANES], ident[pairs:, :LANES], beyond], axis=1).astype(I32)
    owner = ident // share
    place = ident % share
    code = jnp.left_shift(1, place // LANES).astype(F32) * (1.0 + (place % LANES).astype(F32) / LANES)

    ones = [onehot(iota((ns, two), 0) == owner[g : g + 1]) for g in range(pairs)]
    tab[...] = onehot(iota((two, two), 0) < iota((two, two), 1)).astype(BF16)
    before = jnp.dot(
        jnp.concatenate([a.astype(BF16) for a in ones], axis=0), tab[...], preferred_element_type=F32
    )
    run = jnp.zeros((ns, 1), F32)
    for g in range(pairs):
        rank = jnp.sum(ones[g] * (before[g * ns : (g + 1) * ns] + run), axis=0, keepdims=True)
        run = run + jnp.sum(ones[g], axis=1, keepdims=True)
        rank = rank.astype(I32)
        side = owner[g : g + 1] // hw * LANES
        sel[:, g * two : (g + 1) * two] = onehot(iota((2 * LANES, two), 0) == rank + side).astype(BF16)

    loads[2].wait()
    loads[0].wait()
    loads[1].wait()
    lane = iota((GT, col), 1) % GT
    lane8 = iota((8, col), 1) % GT - iota((8, col), 0) // 4
    row = iota((8, two), 0)
    split_at = hw * GT
    gap = jnp.zeros((col - slots * GT, LANES), BF16)

    def values(g):
        w = wv[:, g].reshape(slots * GT, LANES)
        if g % 2:
            w = jnp.concatenate([w[:LANES], gap, w[LANES:]], axis=0)
        else:
            w = jnp.concatenate([w, gap], axis=0)
        a = e16[:, g * GT * LANES : (g + 1) * GT * LANES]
        b = e4[:, g * GT * LANES : (g + 1) * GT * LANES]
        a = nt(jnp.concatenate([a[:, t * LANES : (t + 1) * LANES] for t in range(GT)], axis=0), w)
        b = nt(jnp.concatenate([b[:, t * LANES : (t + 1) * LANES] for t in range(GT)], axis=0), w)
        first = jnp.zeros((GT, col), F32)
        second = jnp.zeros((8, col), F32)
        for t in range(GT):
            first = jnp.where(lane == t, a[t * GT : (t + 1) * GT], first)
        for t in range(0, GT, 2):
            second = jnp.where(lane8 == t, b[t * 4 : t * 4 + 8], second)
        return first, second[:4] + second[4:]

    def joined(even, odd):
        return jnp.concatenate([even[:, :LANES], odd[:, :LANES], even[:, LANES:] + odd[:, LANES:]], axis=1)

    for g in range(pairs):
        even, odd = values(2 * g), values(2 * g + 1)
        first, second = joined(even[0], odd[0]), joined(even[1], odd[1])
        rest = jnp.concatenate([second, jnp.zeros((20 - own + 4, two), F32)], axis=0)
        rest = jnp.where(row == own - 16, code[g : g + 1], rest)
        here = slice(g * two, (g + 1) * two)
        for o in range(hw):
            there = owner[g : g + 1] % hw == o
            lhs[o * GT : (o + 1) * GT, here] = jnp.where(there, first, 0.0).astype(BF16)
        for o in range(0, hw, 2):
            low = jnp.where(owner[g : g + 1] % hw == o, rest, 0.0)
            high = jnp.where(owner[g : g + 1] % hw == o + 1, rest, 0.0)
            lhs[split_at + o * 8 : split_at + o * 8 + 16, here] = jnp.concatenate(
                [low, high], axis=0
            ).astype(BF16)
        if g % BATCH == BATCH - 1:
            cut = slice((g + 1 - BATCH) * two, (g + 1) * two)
            both = nt(lhs[:, cut], sel[:, cut])
            if g == BATCH - 1:
                acc[...] = both
            else:
                acc[...] += both
        if g == min(START, pairs) - 1:
            pl.semaphore_wait(barrier, nm - 1 + ns - 1)
            for c in wave1:
                c.start()
    eight = iota((8, LANES), 0)
    spot = iota((1, LANES), 1)
    for o in range(ns):
        across = slice(o // hw * LANES, (o // hw + 1) * LANES)
        main = acc[o % hw * GT : (o % hw + 1) * GT, across]
        rest = acc[split_at + o % hw * 8 : split_at + (o % hw + 1) * 8, across]
        p0, p1, p2 = (pltpu.roll(rest, 96 - 32 * t, 1) for t in range(3))
        head = jnp.where(eight < 5, p0, pltpu.roll(p2, 5, 0))
        tail = jnp.where(eight < 5, p1, pltpu.roll(p2, 2, 0))
        pk[o] = jnp.where(spot < 96, main, jnp.concatenate([head, tail], axis=0)).astype(BF16)

    def send(d, carry):
        pltpu.make_async_remote_copy(
            pk.at[lax.rem(me + d, ns)], rx.at[me], ps.at[0], pr.at[0],
            device_id=plane(d), device_id_type=MESH).start()
        return carry

    packets = pltpu.make_async_remote_copy(
        pk.at[pl.ds(0, ns - 1)], rx.at[pl.ds(0, ns - 1)], ps.at[0], pr.at[0],
        device_id=plane(1), device_id_type=MESH)
    lax.fori_loop(1, ns, send, 0)
    rx[me] = pk[me]
    packets.wait_recv()

    spot = iota((1, LANES), 1)
    power = jnp.left_shift(1, iota((8, LANES), 0)).astype(F32)
    inverse = jnp.left_shift(1, 7 - iota((8, LANES), 0)).astype(F32)
    down = iota((2 * LANES, LANES), 0)
    for i in range(ns // 8):
        left = []
        for q in range(8):
            p = rx[i * 8 + q].astype(F32)
            r1x, r2x, r3x = (pltpu.roll(p, 32 * (t + 1), 1) for t in range(3))
            lines = [p[k : k + 1] for k in range(16)]
            for r in range(own - 15):
                third = 5 + r if r < 3 else 10 + r
                line = jnp.where(spot < 96, r3x[third : third + 1], 0.0)
                line = jnp.where(spot < 64, r2x[8 + r : 9 + r], line)
                lines.append(jnp.where(spot < 32, r1x[r : r + 1], line))
            where = lines.pop()
            upper = where >= 256.0
            where = jnp.where(upper, where * (1.0 / 256.0), where)
            top = jnp.logical_and(where >= power, where < 2.0 * power)
            left.append(
                jnp.concatenate([jnp.where(top, v, 0.0) for v in lines], axis=0).astype(BF16)
            )
            low = where * jnp.sum(jnp.where(top, inverse, 0.0), axis=0, keepdims=True)
            low = low.astype(I32) - LANES + jnp.where(upper, LANES, 0)
            rgt[:, (i * 8 + q) * LANES : (i * 8 + q + 1) * LANES] = onehot(down == low).astype(BF16)
        both = nt(jnp.concatenate(left, axis=1), rgt[:, i * 8 * LANES : (i + 1) * 8 * LANES])
        if i == 0:
            acc2[...] = both
        else:
            acc2[...] += both
    hg[z] = acc2[...].astype(BF16)

    hrow = own * 8 // 2

    def members_copy(slot, rows, d, n):
        ref = hg.at[slot, pl.ds(rows * hrow, hrow)]
        return pltpu.make_async_remote_copy(
            ref, ref, zs.at[n], zr.at[n], device_id=along(d), device_id_type=MESH)

    before, after = lax.rem(z + dn, nm), lax.rem(z + up, nm)
    direct = [
        members_copy(z, 0, up, 0), members_copy(z, 1, dn, 1),
        members_copy(z, 1, up, 2), members_copy(z, 0, dn, 3),
    ]
    passed = [members_copy(before, 0, up, 4), members_copy(after, 1, dn, 5)]
    for c in direct:
        c.start()
    for c, e in zip(direct[:2], passed):
        c.wait_recv()
        e.start()
    for c in first_up + first_dn + full_up0 + full_dn1:
        c.wait_recv()
    for c in wave2:
        c.start()
    for c in direct[2:] + passed:
        c.wait_recv()

    loads[4].wait()
    loads[5].wait()
    rows = members * 8
    for c in range(2):
        hf[c * rows : (c + 1) * rows] = hg[:, :, c * LANES : (c + 1) * LANES].astype(F32).reshape(rows, LANES)
    for h in range(8):
        x = jnp.concatenate([hf[pl.ds(c * rows + h, members, stride=8), :] for c in range(2)], axis=1)
        seen = jnp.concatenate([ob[h : h + 1], ob[h + 8 : h + 9]], axis=1)
        weight = jnp.concatenate([va[h : h + 1], va[h + 8 : h + 9]], axis=1)
        ybar = jnp.sum(x, axis=0, keepdims=True) / members
        dev = x - ybar
        cut = slice(h * 2 * LANES, (h + 1) * 2 * LANES)
        an[:members, cut] = dev
        an[members:, cut] = jnp.where(
            iota((LANES - members, 2 * LANES), 0) == 0, seen - ybar, 0.0
        )
        wa[:, cut] = dev * weight
    gr[...] = nt(wa[...], an[...], lax.Precision.HIGHEST).reshape(nown, chunk, LANES)

    mine = me // stride
    owns = jnp.logical_and(lax.rem(me, stride) == 0, mine < nown)

    def to_owner(i):
        return pltpu.make_async_remote_copy(
            gr.at[i], rbuf.at[me], s1.at[0], r1.at[0],
            device_id={"state": i * stride}, device_id_type=MESH)

    def tiles_moved(n, src, dst, ss, rs):
        return pltpu.make_async_remote_copy(
            src.at[pl.ds(0, n)], dst.at[pl.ds(0, n)], ss, rs, device_id=plane(1), device_id_type=MESH)

    for i in range(nown):
        @pl.when(me != i * stride)
        def _():
            to_owner(i).start()

    for c in near_up + near_dn + pass_up + pass_dn:
        c.wait_recv()
    x4[:, :qc] = jnp.concatenate([e4[:, pl.ds(mid, qc)]] + [q4[r] for r in range(3)], axis=0)

    @pl.when(owns)
    def _():
        rbuf[me] = gr[mine]
        tiles_moved(ns - 1, rbuf, rbuf, s1.at[0], r1.at[0]).wait_recv()
        gs[mine] = jnp.sum(rbuf[...], axis=0)

        def send_one(d, carry):
            pltpu.make_async_remote_copy(
                gs.at[mine], gs.at[mine], s2.at[0], r2.at[0],
                device_id=plane(d), device_id_type=MESH).start()
            return carry

        lax.fori_loop(1, ns, send_one, 0)
        tiles_moved(nown - 1, gs, gs, s2.at[0], r2.at[0]).wait_recv()

    @pl.when(jnp.logical_not(owns))
    def _():
        tiles_moved(nown, gs, gs, s2.at[0], r2.at[0]).wait_recv()

    mixing = transform(gs[...].reshape(members, LANES), members, yref, zref).astype(BF16)

    q = iota((members, LANES), 0)
    slot = jnp.where(q < 16 * nm, q // 16, (q - 16 * nm) // (own - 16))
    inner = jnp.where(q < 16 * nm, q % 16, 16 + (q - 16 * nm) % (own - 16))
    dist = jnp.where(slot == 0, 0, jnp.where(slot == 1, nm - 1, slot - 1))
    tab[:members, :LANES] = onehot(iota((members, LANES), 1) == (z + dist) % nm * own + inner).astype(BF16)
    padded = jnp.concatenate([mixing, jnp.zeros((LANES - members, LANES), BF16)], axis=0)
    turned = nt(tab[:members, :LANES], padded).astype(BF16)
    mixp[...] = nt(turned, tab[:members, :LANES]).astype(BF16)

    wide_rows = 16 * nm
    x = jnp.concatenate([e16[:, pl.ds(mid, qc)]] + [q16[r] for r in range(3)] + [x4[:, :qc]], axis=0)
    res = jnp.dot(mixp[...], x, preferred_element_type=F32)
    o16[:, pl.ds(mid, qc)] = res[:16].astype(BF16)
    o4[:, pl.ds(mid, qc)] = res[wide_rows : wide_rows + own - 16].astype(BF16)
    for t in range(1, nm):
        w16[t] = res[16 * t : 16 * (t + 1)].astype(BF16)
        w4[t] = res[wide_rows + (own - 16) * t : wide_rows + (own - 16) * (t + 1)].astype(BF16)
    for c in back1:
        c.start()

    for c in over_up + over_dn + full_up1 + full_dn0:
        c.wait_recv()
    mine_rows = jnp.concatenate([mixp[:16], mixp[wide_rows:]], axis=0)
    step = fc // FSTEPS
    for i in range(FSTEPS):
        cut = slice(i * step, (i + 1) * step)
        x = jnp.concatenate(
            [e16[:, cut]] + [f16[r, :, cut] for r in range(3)]
            + [e4[:, cut]] + [f4[r, :, cut] for r in range(3)], axis=0)
        res = jnp.dot(mine_rows, x, preferred_element_type=F32)
        o16[:, cut] = res[:16].astype(BF16)
        o4[:, cut] = res[16:own].astype(BF16)
        if i == FSTEPS // 2 - 1:
            for c in back_first_up + back_first_dn:
                c.wait_recv()
            for c in back2:
                c.start()
    for c in back_near_up + back_near_dn + back2:
        c.wait_recv()
    for c in wave1 + wave2 + back1 + back2 + direct + passed:
        c.wait_send()
    packets.wait_send()

    @pl.when(owns)
    def _():
        tiles_moved(nown - 1, gr, rbuf, s1.at[0], r1.at[0]).wait_send()
        tiles_moved(ns - 1, rbuf, rbuf, s2.at[0], r2.at[0]).wait_send()

    @pl.when(jnp.logical_not(owns))
    def _():
        tiles_moved(nown, gr, rbuf, s1.at[0], r1.at[0]).wait_send()


def per_device(ns, nm, ensemble, weights, seg_obs, observed, inv_var):
    own, cells = ensemble.shape
    tiles, slots, _ = weights.shape
    share = observed.shape[0] // ns
    members = own * nm
    nown = 10 if ns >= 10 else 2
    groups = tiles // GT
    his = share // LANES
    wts = jnp.transpose(weights, (1, 0, 2)).reshape(slots, groups, GT, LANES)
    ids = jnp.transpose(seg_obs)
    obs = observed.reshape(ns, his, LANES)
    var = inv_var.reshape(ns, his, LANES)
    anyspec = pl.BlockSpec(memory_space=pl.ANY)
    dma = pltpu.SemaphoreType.DMA
    vspec = pl.BlockSpec(memory_space=pltpu.VMEM)
    two = 2 * GT * slots
    fc = cells * FULL // 16
    qc = (cells - fc) // nm
    rest = own - 16
    o16, o4 = pl.pallas_call(
        functools.partial(kernel, ns, nm, own, tiles, slots, share, nown, fc),
        out_shape=(
            pltpu.VMEM((16, cells), BF16),
            pltpu.VMEM((rest, cells), BF16),
        ),
        in_specs=[anyspec] * 5,
        out_specs=(vspec, vspec),
        scratch_shapes=[
            pltpu.VMEM((3, 16, fc), BF16),
            pltpu.VMEM((3, rest, fc), BF16),
            pltpu.VMEM((3, 16, qc), BF16),
            pltpu.VMEM((3, rest, qc), BF16),
            pltpu.VMEM((2, 16, qc // 2), BF16),
            pltpu.VMEM((2, rest, qc // 2), BF16),
            pltpu.VMEM((rest * nm, qc), BF16),
            pltpu.VMEM((nm, 16, qc), BF16),
            pltpu.VMEM((nm, rest, qc), BF16),
            pltpu.VMEM((2, 16, qc // 2), BF16),
            pltpu.VMEM((2, rest, qc // 2), BF16),
            pltpu.VMEM((members, members), BF16),
            pltpu.VMEM((members, LANES), F32),
            pltpu.VMEM((members, LANES), F32),
            pltpu.VMEM((two, two), BF16),
            pltpu.VMEM((2 * LANES, ns * LANES), BF16),
            pltpu.VMEM((16, cells), BF16),
            pltpu.VMEM((own - 16, cells), BF16),
            pltpu.VMEM((slots, groups, GT, LANES), BF16),
            pltpu.VMEM((slots, tiles), I32),
            pltpu.VMEM((his, LANES), F32),
            pltpu.VMEM((his, LANES), F32),
            pltpu.VMEM((ns // 2 * (GT + 8), groups // 2 * two), BF16),
            pltpu.VMEM((2 * LANES, groups // 2 * two), BF16),
            pltpu.VMEM((ns // 2 * (GT + 8), 2 * LANES), F32),
            pltpu.VMEM((ns, GT, LANES), BF16),
            pltpu.VMEM((ns, GT, LANES), BF16),
            pltpu.VMEM((own * 8, 2 * LANES), F32),
            pltpu.VMEM((nm, own * 8, 2 * LANES), BF16),
            pltpu.VMEM((2 * members * 8, LANES), F32),
            pltpu.VMEM((LANES, share), F32),
            pltpu.VMEM((members, share), F32),
            pltpu.VMEM((nown, members // nown, LANES), F32),
            pltpu.VMEM((ns, members // nown, LANES), F32),
            pltpu.VMEM((nown, members // nown, LANES), F32),
            dma((6,)), dma((36,)), dma((36,)), dma((1,)), dma((1,)),
            dma((6,)), dma((6,)), dma((1,)), dma((1,)), dma((1,)), dma((1,)),
        ],
        compiler_params=pltpu.CompilerParams(collective_id=0, has_side_effects=True),
        name="assimilate",
    )(ensemble, wts, ids, obs, var)
    def settle(o16_ref, o4_ref, out, sem):
        moves = [
            pltpu.make_async_copy(o16_ref, out.at[pl.ds(0, 16)], sem.at[0]),
            pltpu.make_async_copy(o4_ref, out.at[pl.ds(16, rest)], sem.at[1]),
        ]
        for c in moves:
            c.start()
        for c in moves:
            c.wait()

    return pl.pallas_call(
        settle,
        out_shape=jax.ShapeDtypeStruct((own, cells), BF16),
        in_specs=[vspec] * 2,
        out_specs=anyspec,
        scratch_shapes=[dma((2,))],
        name="settle",
    )(*(pltpu.with_memory_space_constraint(o, pltpu.VMEM) for o in (o16, o4)))


def solution(mesh):
    return jax.shard_map(
        functools.partial(per_device, mesh.shape["state"], mesh.shape["mem"]),
        mesh=mesh,
        in_specs=(P("mem", "state"), P("state", None, None), P("state", None), P(), P()),
        out_specs=P("mem", "state"),
        check_vma=False,
    )
```

```python
import functools
import math

import jax
import jax.numpy as jnp
from jax import lax
from jax.experimental import pallas as pl
from jax.experimental.pallas import tpu as pltpu
from jax.sharding import PartitionSpec as P

ITERS = 14
F32, BF16, I32 = jnp.float32, jnp.bfloat16, jnp.int32
MESH = pl.DeviceIdType.MESH
GT = 16
FULL = 7
FSTEPS = 4
BATCH = 4
START = 5
LANES = 128


def nt(a, b, precision=None):
    return lax.dot_general(
        a, b, (((1,), (1,)), ((), ())), precision=precision, preferred_element_type=F32
    )


def iota(shape, dim):
    return lax.broadcasted_iota(I32, shape, dim)


def onehot(mask):
    return jnp.where(mask, 1.0, 0.0)


def split(x):
    high = x.astype(BF16)
    return high, (x - high.astype(F32)).astype(BF16)


def tall(x):
    high, low = split(x)
    pad = jnp.zeros((LANES - x.shape[0], LANES), BF16)
    return jnp.concatenate([high, pad, high, pad, low, pad], axis=0)


def wide(x):
    high, low = split(x)
    return jnp.concatenate([high, low, high], axis=1)


def product(left, right):
    return jnp.dot(left, right, preferred_element_type=F32)


def transform(total, members, yref, zref):
    shape = (members, LANES)
    down, across = iota(shape, 0), iota(shape, 1)
    identity = onehot(down == across)
    system = (members - 1.0) * identity + jnp.where(across < members, total, 0.0)
    scaling = jnp.sqrt(jnp.sum(jnp.sum(system * system, axis=1, keepdims=True), axis=0, keepdims=True))
    y = system / scaling
    c = 1.5 * identity - 0.5 * y
    yref[...] = product(wide(y), tall(c))
    zref[...] = c

    def step(_, carry):
        y, z = yref[...], zref[...]
        c = 1.5 * identity - 0.5 * product(wide(z), tall(y))
        yref[...] = product(wide(y), tall(c))
        zref[...] = product(wide(c), tall(z))
        return carry

    lax.fori_loop(1, ITERS, step, 0)
    root = zref[...] / jnp.sqrt(scaling)
    left = wide(root)
    twice = product(left, tall(product(left, tall(total))))
    mixed = twice[:, members : members + 1] + math.sqrt(members - 1.0) * root
    mixed = mixed + (1.0 - jnp.sum(mixed, axis=0, keepdims=True)) / members
    return jnp.where(across < members, mixed, 0.0)


def kernel(
    ns, nm, own, tiles, slots, share, nown, fc,
    ens, wts, ids, obs, var,
    o16, o4,
    f16, f4, q16, q4, t16, t4, x4, w16, w4, mixp,
    yref, zref, tab, rgt, e16, e4, wv, idv, ob, va, lhs, sel, acc, pk, rx, acc2, hg, hf, an, wa, gr, rbuf, gs,
    lsem, bs, br, ps, pr, zs, zr, s1, r1, s2, r2,
):
    me = lax.axis_index("state")
    z = lax.axis_index("mem")
    groups = tiles // GT
    cells = tiles * LANES
    qc = (cells - fc) // nm
    his = share // LANES
    members = own * nm
    chunk = members // nown
    stride = ns // nown
    col = GT * GT
    two = 2 * GT * slots
    pairs = groups // 2
    part = (slots - 8) * GT
    hw = ns // 2

    loads = [
        pltpu.make_async_copy(ens.at[pl.ds(0, 16)], e16, lsem.at[0]),
        pltpu.make_async_copy(ens.at[pl.ds(16, own - 16)], e4, lsem.at[1]),
        pltpu.make_async_copy(wts, wv, lsem.at[2]),
        pltpu.make_async_copy(ids, idv, lsem.at[3]),
        pltpu.make_async_copy(obs.at[me], ob, lsem.at[4]),
        pltpu.make_async_copy(var.at[me], va, lsem.at[5]),
    ]
    for c in loads:
        c.start()

    def plane(d):
        return {"state": lax.rem(me + d, ns)}

    def along(d):
        return {"mem": lax.rem(z + d, nm)}

    barrier = pltpu.get_barrier_semaphore()
    for d in range(1, nm):
        pl.semaphore_signal(barrier, inc=1, device_id=along(d), device_id_type=MESH)

    def greet(d, carry):
        pl.semaphore_signal(barrier, inc=1, device_id=plane(d), device_id_type=MESH)
        return carry

    lax.fori_loop(1, ns, greet, 0)

    count = [0]

    def pair(src16, src4, dst16, dst4, d):
        n = count[0]
        count[0] += 2
        return [
            pltpu.make_async_remote_copy(
                src, dst, bs.at[n + i], br.at[n + i], device_id=along(d), device_id_type=MESH)
            for i, (src, dst) in enumerate(((src16, dst16), (src4, dst4)))
        ]

    up, dn = 1, nm - 1
    fh, qh = fc // 2, qc // 2

    def quarter(d):
        return pl.multiple_of(fc + lax.rem(z + d, nm) * qc, LANES)

    def own_at(at, n):
        return e16.at[:, pl.ds(at, n)], e4.at[:, pl.ds(at, n)]

    def at(pairs, slot, start, n):
        return tuple(ref.at[slot, :, pl.ds(start, n)] for ref in pairs)

    first_up = pair(*own_at(quarter(2), qh), *at((t16, t4), 0, 0, qh), up)
    first_dn = pair(*own_at(quarter(2) + qh, qh), *at((t16, t4), 1, 0, qh), dn)
    near_up = pair(*own_at(quarter(up), qc), *at((q16, q4), 0, 0, qc), up)
    near_dn = pair(*own_at(quarter(dn), qc), *at((q16, q4), 1, 0, qc), dn)
    pass_up = pair(*at((t16, t4), 0, 0, qh), *at((q16, q4), 2, 0, qh), up)
    pass_dn = pair(*at((t16, t4), 1, 0, qh), *at((q16, q4), 2, qh, qh), dn)
    full_up0 = pair(*own_at(0, fh), *at((f16, f4), 0, 0, fh), up)
    full_dn1 = pair(*own_at(fh, fh), *at((f16, f4), 1, fh, fh), dn)
    full_up1 = pair(*own_at(fh, fh), *at((f16, f4), 0, fh, fh), up)
    full_dn0 = pair(*own_at(0, fh), *at((f16, f4), 1, 0, fh), dn)
    over_up = pair(*at((f16, f4), 0, 0, fh), *at((f16, f4), 2, 0, fh), up)
    over_dn = pair(*at((f16, f4), 1, fh, fh), *at((f16, f4), 2, fh, fh), dn)
    wave1 = first_up + first_dn + full_up0 + full_dn1
    wave2 = near_up + near_dn + pass_up + pass_dn + full_up1 + full_dn0
    wave3 = over_up + over_dn
    mid = pl.multiple_of(fc + z * qc, LANES)
    far = pl.multiple_of(fc + lax.rem(z + 2, nm) * qc, LANES)

    def out_at(start, n):
        return o16.at[:, pl.ds(start, n)], o4.at[:, pl.ds(start, n)]

    back_far = pair(*at((w16, w4), 3, 0, qc), *out_at(mid, qc), 2)
    back_near_up = pair(*at((w16, w4), 2, 0, qc), *out_at(mid, qc), up)
    back_near_dn = pair(*at((w16, w4), 1, 0, qc), *out_at(mid, qc), dn)
    back1 = back_far + back_near_up + back_near_dn

    loads[3].wait()
    raw = jnp.concatenate([idv[...], jnp.zeros((GT - slots, tiles), I32)], axis=0)
    tab[:tiles, :col] = onehot(iota((tiles, col), 0) % GT == iota((tiles, col), 1) % GT).astype(BF16)
    spread = tab[:tiles, :col]
    order = list(range(0, groups, 2)) + list(range(1, groups, 2))

    def regroup(byte):
        byte = byte.astype(F32)
        high = jnp.concatenate(
            [jnp.where(iota((GT, tiles), 1) // GT == g, byte, 0.0) for g in order], axis=0
        ).astype(BF16)
        out = jnp.dot(high, spread, preferred_element_type=F32).reshape(groups, GT, col)
        at_lane = iota((groups, GT, col), 2)
        shift = jnp.where(jnp.logical_and(iota((groups, GT, col), 0) >= pairs, at_lane >= LANES), part, 0)
        keep = iota((groups, GT, col), 1) == (at_lane - shift) // GT
        return jnp.sum(jnp.where(keep, out, 0.0), axis=1)

    ident = regroup(raw // 256) * 256.0 + regroup(raw % 256)
    beyond = jnp.where(iota((pairs, LANES), 1) < part, ident[:pairs, LANES:], ident[pairs:, LANES:])
    ident = jnp.concatenate([ident[:pairs, :LANES], ident[pairs:, :LANES], beyond], axis=1).astype(I32)
    owner = ident // share
    place = ident % share
    code = jnp.left_shift(1, place // LANES).astype(F32) * (1.0 + (place % LANES).astype(F32) / LANES)

    ones = [onehot(iota((ns, two), 0) == owner[g : g + 1]) for g in range(pairs)]
    tab[...] = onehot(iota((two, two), 0) < iota((two, two), 1)).astype(BF16)
    before = jnp.dot(
        jnp.concatenate([a.astype(BF16) for a in ones], axis=0), tab[...], preferred_element_type=F32
    )
    run = jnp.zeros((ns, 1), F32)
    for g in range(pairs):
        rank = jnp.sum(ones[g] * (before[g * ns : (g + 1) * ns] + run), axis=0, keepdims=True)
        run = run + jnp.sum(ones[g], axis=1, keepdims=True)
        rank = rank.astype(I32)
        side = owner[g : g + 1] // hw * LANES
        sel[:, g * two : (g + 1) * two] = onehot(iota((2 * LANES, two), 0) == rank + side).astype(BF16)

    loads[2].wait()
    loads[0].wait()
    loads[1].wait()
    lane = iota((GT, col), 1) % GT
    lane8 = iota((8, col), 1) % GT - iota((8, col), 0) // 4
    row = iota((8, two), 0)
    split_at = hw * GT
    gap = jnp.zeros((col - slots * GT, LANES), BF16)

    def values(g):
        w = wv[:, g].reshape(slots * GT, LANES)
        if g % 2:
            w = jnp.concatenate([w[:LANES], gap, w[LANES:]], axis=0)
        else:
            w = jnp.concatenate([w, gap], axis=0)
        a = e16[:, g * GT * LANES : (g + 1) * GT * LANES]
        b = e4[:, g * GT * LANES : (g + 1) * GT * LANES]
        a = nt(jnp.concatenate([a[:, t * LANES : (t + 1) * LANES] for t in range(GT)], axis=0), w)
        b = nt(jnp.concatenate([b[:, t * LANES : (t + 1) * LANES] for t in range(GT)], axis=0), w)
        first = jnp.zeros((GT, col), F32)
        second = jnp.zeros((8, col), F32)
        for t in range(GT):
            first = jnp.where(lane == t, a[t * GT : (t + 1) * GT], first)
        for t in range(0, GT, 2):
            second = jnp.where(lane8 == t, b[t * 4 : t * 4 + 8], second)
        return first, second[:4] + second[4:]

    def joined(even, odd):
        return jnp.concatenate([even[:, :LANES], odd[:, :LANES], even[:, LANES:] + odd[:, LANES:]], axis=1)

    for g in range(pairs):
        even, odd = values(2 * g), values(2 * g + 1)
        first, second = joined(even[0], odd[0]), joined(even[1], odd[1])
        rest = jnp.concatenate([second, jnp.zeros((20 - own + 4, two), F32)], axis=0)
        rest = jnp.where(row == own - 16, code[g : g + 1], rest)
        here = slice(g * two, (g + 1) * two)
        for o in range(hw):
            there = owner[g : g + 1] % hw == o
            lhs[o * GT : (o + 1) * GT, here] = jnp.where(there, first, 0.0).astype(BF16)
        for o in range(0, hw, 2):
            low = jnp.where(owner[g : g + 1] % hw == o, rest, 0.0)
            high = jnp.where(owner[g : g + 1] % hw == o + 1, rest, 0.0)
            lhs[split_at + o * 8 : split_at + o * 8 + 16, here] = jnp.concatenate(
                [low, high], axis=0
            ).astype(BF16)
        if g % BATCH == BATCH - 1:
            cut = slice((g + 1 - BATCH) * two, (g + 1) * two)
            both = nt(lhs[:, cut], sel[:, cut])
            if g == BATCH - 1:
                acc[...] = both
            else:
                acc[...] += both
        if g == min(START, pairs) - 1:
            pl.semaphore_wait(barrier, nm - 1 + ns - 1)
            for c in wave1:
                c.start()
    eight = iota((8, LANES), 0)
    spot = iota((1, LANES), 1)
    for o in range(ns):
        across = slice(o // hw * LANES, (o // hw + 1) * LANES)
        main = acc[o % hw * GT : (o % hw + 1) * GT, across]
        rest = acc[split_at + o % hw * 8 : split_at + (o % hw + 1) * 8, across]
        p0, p1, p2 = (pltpu.roll(rest, 96 - 32 * t, 1) for t in range(3))
        head = jnp.where(eight < 5, p0, pltpu.roll(p2, 5, 0))
        tail = jnp.where(eight < 5, p1, pltpu.roll(p2, 2, 0))
        pk[o] = jnp.where(spot < 96, main, jnp.concatenate([head, tail], axis=0)).astype(BF16)

    def send(d, carry):
        pltpu.make_async_remote_copy(
            pk.at[lax.rem(me + d, ns)], rx.at[me], ps.at[0], pr.at[0],
            device_id=plane(d), device_id_type=MESH).start()
        return carry

    packets = pltpu.make_async_remote_copy(
        pk.at[pl.ds(0, ns - 1)], rx.at[pl.ds(0, ns - 1)], ps.at[0], pr.at[0],
        device_id=plane(1), device_id_type=MESH)
    lax.fori_loop(1, ns, send, 0)
    rx[me] = pk[me]
    packets.wait_recv()

    spot = iota((1, LANES), 1)
    power = jnp.left_shift(1, iota((8, LANES), 0)).astype(F32)
    inverse = jnp.left_shift(1, 7 - iota((8, LANES), 0)).astype(F32)
    down = iota((2 * LANES, LANES), 0)
    for i in range(ns // 8):
        left = []
        for q in range(8):
            p = rx[i * 8 + q].astype(F32)
            r1x, r2x, r3x = (pltpu.roll(p, 32 * (t + 1), 1) for t in range(3))
            lines = [p[k : k + 1] for k in range(16)]
            for r in range(own - 15):
                third = 5 + r if r < 3 else 10 + r
                line = jnp.where(spot < 96, r3x[third : third + 1], 0.0)
                line = jnp.where(spot < 64, r2x[8 + r : 9 + r], line)
                lines.append(jnp.where(spot < 32, r1x[r : r + 1], line))
            where = lines.pop()
            upper = where >= 256.0
            where = jnp.where(upper, where * (1.0 / 256.0), where)
            top = jnp.logical_and(where >= power, where < 2.0 * power)
            left.append(
                jnp.concatenate([jnp.where(top, v, 0.0) for v in lines], axis=0).astype(BF16)
            )
            low = where * jnp.sum(jnp.where(top, inverse, 0.0), axis=0, keepdims=True)
            low = low.astype(I32) - LANES + jnp.where(upper, LANES, 0)
            rgt[:, (i * 8 + q) * LANES : (i * 8 + q + 1) * LANES] = onehot(down == low).astype(BF16)
        both = nt(jnp.concatenate(left, axis=1), rgt[:, i * 8 * LANES : (i + 1) * 8 * LANES])
        if i == 0:
            acc2[...] = both
        else:
            acc2[...] += both
    hg[z] = acc2[...].astype(BF16)

    def members_copy(d, n):
        ref = hg.at[z]
        return pltpu.make_async_remote_copy(
            ref, ref, zs.at[n], zr.at[n], device_id=along(d), device_id_type=MESH)

    direct = [members_copy(2, 0), members_copy(up, 1), members_copy(dn, 2)]
    for c in direct:
        c.start()
    for c in first_up + first_dn:
        c.wait_recv()
    for c in wave2:
        c.start()
    for c in direct:
        c.wait_recv()

    loads[4].wait()
    loads[5].wait()
    rows = members * 8
    for c in range(2):
        hf[c * rows : (c + 1) * rows] = hg[:, :, c * LANES : (c + 1) * LANES].astype(F32).reshape(rows, LANES)
    for h in range(8):
        x = jnp.concatenate([hf[pl.ds(c * rows + h, members, stride=8), :] for c in range(2)], axis=1)
        seen = jnp.concatenate([ob[h : h + 1], ob[h + 8 : h + 9]], axis=1)
        weight = jnp.concatenate([va[h : h + 1], va[h + 8 : h + 9]], axis=1)
        ybar = jnp.sum(x, axis=0, keepdims=True) / members
        dev = x - ybar
        cut = slice(h * 2 * LANES, (h + 1) * 2 * LANES)
        an[:members, cut] = dev
        an[members:, cut] = jnp.where(
            iota((LANES - members, 2 * LANES), 0) == 0, seen - ybar, 0.0
        )
        wa[:, cut] = dev * weight
    gr[...] = nt(wa[...], an[...], lax.Precision.HIGHEST).reshape(nown, chunk, LANES)

    mine = me // stride
    owns = jnp.logical_and(lax.rem(me, stride) == 0, mine < nown)

    def to_owner(i):
        return pltpu.make_async_remote_copy(
            gr.at[i], rbuf.at[me], s1.at[0], r1.at[0],
            device_id={"state": i * stride}, device_id_type=MESH)

    def tiles_moved(n, src, dst, ss, rs):
        return pltpu.make_async_remote_copy(
            src.at[pl.ds(0, n)], dst.at[pl.ds(0, n)], ss, rs, device_id=plane(1), device_id_type=MESH)

    for i in range(nown):
        @pl.when(me != i * stride)
        def _():
            to_owner(i).start()

    for c in full_up0 + full_dn1:
        c.wait_recv()
    for c in wave3:
        c.start()
    for c in near_up + near_dn + pass_up + pass_dn:
        c.wait_recv()
    x4[:, :qc] = jnp.concatenate([e4[:, pl.ds(mid, qc)]] + [q4[r] for r in range(3)], axis=0)

    @pl.when(owns)
    def _():
        rbuf[me] = gr[mine]
        tiles_moved(ns - 1, rbuf, rbuf, s1.at[0], r1.at[0]).wait_recv()
        gs[mine] = jnp.sum(rbuf[...], axis=0)

        def send_one(d, carry):
            pltpu.make_async_remote_copy(
                gs.at[mine], gs.at[mine], s2.at[0], r2.at[0],
                device_id=plane(d), device_id_type=MESH).start()
            return carry

        lax.fori_loop(1, ns, send_one, 0)
        tiles_moved(nown - 1, gs, gs, s2.at[0], r2.at[0]).wait_recv()

    @pl.when(jnp.logical_not(owns))
    def _():
        tiles_moved(nown, gs, gs, s2.at[0], r2.at[0]).wait_recv()

    mixing = transform(gs[...].reshape(members, LANES), members, yref, zref).astype(BF16)

    q = iota((members, LANES), 0)
    slot = jnp.where(q < 16 * nm, q // 16, (q - 16 * nm) // (own - 16))
    inner = jnp.where(q < 16 * nm, q % 16, 16 + (q - 16 * nm) % (own - 16))
    dist = jnp.where(slot == 0, 0, jnp.where(slot == 1, nm - 1, slot - 1))
    tab[:members, :LANES] = onehot(iota((members, LANES), 1) == (z + dist) % nm * own + inner).astype(BF16)
    padded = jnp.concatenate([mixing, jnp.zeros((LANES - members, LANES), BF16)], axis=0)
    turned = nt(tab[:members, :LANES], padded).astype(BF16)
    mixp[...] = nt(turned, tab[:members, :LANES]).astype(BF16)

    wide_rows = 16 * nm
    for part in range(2):
        here = slice(part * qh, (part + 1) * qh)
        at_mid = pl.ds(pl.multiple_of(mid + part * qh, LANES), qh)
        x = jnp.concatenate([e16[:, at_mid]] + [q16[r, :, here] for r in range(3)] + [x4[:, here]], axis=0)
        res = jnp.dot(mixp[...], x, preferred_element_type=F32)
        for t in range(nm - 1, 0, -1):
            w16[t, :, here] = res[16 * t : 16 * (t + 1)].astype(BF16)
            w4[t, :, here] = res[wide_rows + (own - 16) * t : wide_rows + (own - 16) * (t + 1)].astype(BF16)
        o16[:, at_mid] = res[:16].astype(BF16)
        o4[:, at_mid] = res[wide_rows : wide_rows + own - 16].astype(BF16)
    for c in back1:
        c.start()

    for c in over_up + over_dn + full_up1 + full_dn0:
        c.wait_recv()
    mine_rows = jnp.concatenate([mixp[:16], mixp[wide_rows:]], axis=0)
    step = fc // FSTEPS
    for i in range(FSTEPS):
        cut = slice(i * step, (i + 1) * step)
        x = jnp.concatenate(
            [e16[:, cut]] + [f16[r, :, cut] for r in range(3)]
            + [e4[:, cut]] + [f4[r, :, cut] for r in range(3)], axis=0)
        res = jnp.dot(mine_rows, x, preferred_element_type=F32)
        o16[:, cut] = res[:16].astype(BF16)
        o4[:, cut] = res[16:own].astype(BF16)

    for c in back1:
        c.wait_recv()
    for c in wave1 + wave2 + wave3 + back1 + direct:
        c.wait_send()
    packets.wait_send()

    @pl.when(owns)
    def _():
        tiles_moved(nown - 1, gr, rbuf, s1.at[0], r1.at[0]).wait_send()
        tiles_moved(ns - 1, rbuf, rbuf, s2.at[0], r2.at[0]).wait_send()

    @pl.when(jnp.logical_not(owns))
    def _():
        tiles_moved(nown, gr, rbuf, s1.at[0], r1.at[0]).wait_send()


def per_device(ns, nm, ensemble, weights, seg_obs, observed, inv_var):
    own, cells = ensemble.shape
    tiles, slots, _ = weights.shape
    share = observed.shape[0] // ns
    members = own * nm
    nown = 10 if ns >= 10 else 2
    groups = tiles // GT
    his = share // LANES
    wts = jnp.transpose(weights, (1, 0, 2)).reshape(slots, groups, GT, LANES)
    ids = jnp.transpose(seg_obs)
    obs = observed.reshape(ns, his, LANES)
    var = inv_var.reshape(ns, his, LANES)
    anyspec = pl.BlockSpec(memory_space=pl.ANY)
    dma = pltpu.SemaphoreType.DMA
    vspec = pl.BlockSpec(memory_space=pltpu.VMEM)
    two = 2 * GT * slots
    fc = cells * FULL // 16
    qc = (cells - fc) // nm
    rest = own - 16
    o16, o4 = pl.pallas_call(
        functools.partial(kernel, ns, nm, own, tiles, slots, share, nown, fc),
        out_shape=(
            pltpu.VMEM((16, cells), BF16),
            pltpu.VMEM((rest, cells), BF16),
        ),
        in_specs=[anyspec] * 5,
        out_specs=(vspec, vspec),
        scratch_shapes=[
            pltpu.VMEM((3, 16, fc), BF16),
            pltpu.VMEM((3, rest, fc), BF16),
            pltpu.VMEM((3, 16, qc), BF16),
            pltpu.VMEM((3, rest, qc), BF16),
            pltpu.VMEM((2, 16, qc // 2), BF16),
            pltpu.VMEM((2, rest, qc // 2), BF16),
            pltpu.VMEM((rest * nm, qc), BF16),
            pltpu.VMEM((nm, 16, qc), BF16),
            pltpu.VMEM((nm, rest, qc), BF16),
            pltpu.VMEM((members, members), BF16),
            pltpu.VMEM((members, LANES), F32),
            pltpu.VMEM((members, LANES), F32),
            pltpu.VMEM((two, two), BF16),
            pltpu.VMEM((2 * LANES, ns * LANES), BF16),
            pltpu.VMEM((16, cells), BF16),
            pltpu.VMEM((own - 16, cells), BF16),
            pltpu.VMEM((slots, groups, GT, LANES), BF16),
            pltpu.VMEM((slots, tiles), I32),
            pltpu.VMEM((his, LANES), F32),
            pltpu.VMEM((his, LANES), F32),
            pltpu.VMEM((ns // 2 * (GT + 8), groups // 2 * two), BF16),
            pltpu.VMEM((2 * LANES, groups // 2 * two), BF16),
            pltpu.VMEM((ns // 2 * (GT + 8), 2 * LANES), F32),
            pltpu.VMEM((ns, GT, LANES), BF16),
            pltpu.VMEM((ns, GT, LANES), BF16),
            pltpu.VMEM((own * 8, 2 * LANES), F32),
            pltpu.VMEM((nm, own * 8, 2 * LANES), BF16),
            pltpu.VMEM((2 * members * 8, LANES), F32),
            pltpu.VMEM((LANES, share), F32),
            pltpu.VMEM((members, share), F32),
            pltpu.VMEM((nown, members // nown, LANES), F32),
            pltpu.VMEM((ns, members // nown, LANES), F32),
            pltpu.VMEM((nown, members // nown, LANES), F32),
            dma((6,)), dma((36,)), dma((36,)), dma((1,)), dma((1,)),
            dma((3,)), dma((3,)), dma((1,)), dma((1,)), dma((1,)), dma((1,)),
        ],
        compiler_params=pltpu.CompilerParams(collective_id=0, has_side_effects=True),
        name="assimilate",
    )(ensemble, wts, ids, obs, var)
    def settle(o16_ref, o4_ref, out, sem):
        moves = [
            pltpu.make_async_copy(o16_ref, out.at[pl.ds(0, 16)], sem.at[0]),
            pltpu.make_async_copy(o4_ref, out.at[pl.ds(16, rest)], sem.at[1]),
        ]
        for c in moves:
            c.start()
        for c in moves:
            c.wait()

    return pl.pallas_call(
        settle,
        out_shape=jax.ShapeDtypeStruct((own, cells), BF16),
        in_specs=[vspec] * 2,
        out_specs=anyspec,
        scratch_shapes=[dma((2,))],
        name="settle",
    )(*(pltpu.with_memory_space_constraint(o, pltpu.VMEM) for o in (o16, o4)))


def solution(mesh):
    return jax.shard_map(
        functools.partial(per_device, mesh.shape["state"], mesh.shape["mem"]),
        mesh=mesh,
        in_specs=(P("mem", "state"), P("state", None, None), P("state", None), P(), P()),
        out_specs=P("mem", "state"),
        check_vma=False,
    )
```

```python
import functools
import math

import jax
import jax.numpy as jnp
from jax import lax
from jax.experimental import pallas as pl
from jax.experimental.pallas import tpu as pltpu
from jax.sharding import PartitionSpec as P

ITERS = 14
F32, BF16, I32 = jnp.float32, jnp.bfloat16, jnp.int32
MESH = pl.DeviceIdType.MESH
GT = 16
FULL = 7
FSTEPS = 4
BATCH = 4
START = 5
LANES = 128


def nt(a, b, precision=None):
    return lax.dot_general(
        a, b, (((1,), (1,)), ((), ())), precision=precision, preferred_element_type=F32
    )


def iota(shape, dim):
    return lax.broadcasted_iota(I32, shape, dim)


def onehot(mask):
    return jnp.where(mask, 1.0, 0.0)


def split(x):
    high = x.astype(BF16)
    return high, (x - high.astype(F32)).astype(BF16)


def tall(x):
    high, low = split(x)
    pad = jnp.zeros((LANES - x.shape[0], LANES), BF16)
    return jnp.concatenate([high, pad, high, pad, low, pad], axis=0)


def wide(x):
    high, low = split(x)
    return jnp.concatenate([high, low, high], axis=1)


def product(left, right):
    return jnp.dot(left, right, preferred_element_type=F32)


def transform(total, members, yref, zref):
    shape = (members, LANES)
    down, across = iota(shape, 0), iota(shape, 1)
    identity = onehot(down == across)
    system = (members - 1.0) * identity + jnp.where(across < members, total, 0.0)
    scaling = jnp.sqrt(jnp.sum(jnp.sum(system * system, axis=1, keepdims=True), axis=0, keepdims=True))
    y = system / scaling
    c = 1.5 * identity - 0.5 * y
    yref[...] = product(wide(y), tall(c))
    zref[...] = c

    def step(_, carry):
        y, z = yref[...], zref[...]
        c = 1.5 * identity - 0.5 * product(wide(z), tall(y))
        yref[...] = product(wide(y), tall(c))
        zref[...] = product(wide(c), tall(z))
        return carry

    lax.fori_loop(1, ITERS, step, 0)
    root = zref[...] / jnp.sqrt(scaling)
    left = wide(root)
    twice = product(left, tall(product(left, tall(total))))
    mixed = twice[:, members : members + 1] + math.sqrt(members - 1.0) * root
    mixed = mixed + (1.0 - jnp.sum(mixed, axis=0, keepdims=True)) / members
    return jnp.where(across < members, mixed, 0.0)


def kernel(
    ns, nm, own, tiles, slots, share, nown, fc,
    ens, wts, ids, obs, var,
    o16, o4,
    f16, f4, q16, q4, t16, t4, x4, w16, w4, mixp,
    yref, zref, tab, rgt, e16, e4, wv, idv, ob, va, lhs, sel, acc, pk, rx, acc2, hg, hf, an, wa, gr, rbuf, gs,
    lsem, bs, br, ps, pr, zs, zr, s1, r1, s2, r2,
):
    me = lax.axis_index("state")
    z = lax.axis_index("mem")
    groups = tiles // GT
    cells = tiles * LANES
    qc = (cells - fc) // nm
    his = share // LANES
    members = own * nm
    chunk = members // nown
    stride = ns // nown
    col = GT * GT
    two = 2 * GT * slots
    pairs = groups // 2
    part = (slots - 8) * GT
    hw = ns // 2

    loads = [
        pltpu.make_async_copy(ens.at[pl.ds(0, 16)], e16, lsem.at[0]),
        pltpu.make_async_copy(ens.at[pl.ds(16, own - 16)], e4, lsem.at[1]),
        pltpu.make_async_copy(wts, wv, lsem.at[2]),
        pltpu.make_async_copy(ids, idv, lsem.at[3]),
        pltpu.make_async_copy(obs.at[me], ob, lsem.at[4]),
        pltpu.make_async_copy(var.at[me], va, lsem.at[5]),
    ]
    for c in loads:
        c.start()

    def plane(d):
        return {"state": lax.rem(me + d, ns)}

    def along(d):
        return {"mem": lax.rem(z + d, nm)}

    barrier = pltpu.get_barrier_semaphore()
    for d in range(1, nm):
        pl.semaphore_signal(barrier, inc=1, device_id=along(d), device_id_type=MESH)

    def greet(n, carry):
        d = 1 + lax.rem(n + 8, ns - 1)
        pl.semaphore_signal(barrier, inc=1, device_id=plane(d), device_id_type=MESH)
        return carry

    lax.fori_loop(1, ns, greet, 0)

    count = [0]

    def pair(src16, src4, dst16, dst4, d):
        n = count[0]
        count[0] += 2
        return [
            pltpu.make_async_remote_copy(
                src, dst, bs.at[n + i], br.at[n + i], device_id=along(d), device_id_type=MESH)
            for i, (src, dst) in enumerate(((src16, dst16), (src4, dst4)))
        ]

    up, dn = 1, nm - 1
    fh, qh = fc // 2, qc // 2

    def quarter(d):
        return pl.multiple_of(fc + lax.rem(z + d, nm) * qc, LANES)

    def own_at(at, n):
        return e16.at[:, pl.ds(at, n)], e4.at[:, pl.ds(at, n)]

    def at(pairs, slot, start, n):
        return tuple(ref.at[slot, :, pl.ds(start, n)] for ref in pairs)

    first_up = pair(*own_at(quarter(2), qh), *at((t16, t4), 0, 0, qh), up)
    first_dn = pair(*own_at(quarter(2) + qh, qh), *at((t16, t4), 1, 0, qh), dn)
    near_up = pair(*own_at(quarter(up), qc), *at((q16, q4), 0, 0, qc), up)
    near_dn = pair(*own_at(quarter(dn), qc), *at((q16, q4), 1, 0, qc), dn)
    pass_up = pair(*at((t16, t4), 0, 0, qh), *at((q16, q4), 2, 0, qh), up)
    pass_dn = pair(*at((t16, t4), 1, 0, qh), *at((q16, q4), 2, qh, qh), dn)
    full_up0 = pair(*own_at(0, fh), *at((f16, f4), 0, 0, fh), up)
    full_dn1 = pair(*own_at(fh, fh), *at((f16, f4), 1, fh, fh), dn)
    full_up1 = pair(*own_at(fh, fh), *at((f16, f4), 0, fh, fh), up)
    full_dn0 = pair(*own_at(0, fh), *at((f16, f4), 1, 0, fh), dn)
    over_up = pair(*at((f16, f4), 0, 0, fh), *at((f16, f4), 2, 0, fh), up)
    over_dn = pair(*at((f16, f4), 1, fh, fh), *at((f16, f4), 2, fh, fh), dn)
    wave1 = first_up + first_dn + full_up0 + full_dn1
    wave2 = near_up + near_dn + pass_up + pass_dn + full_up1 + full_dn0
    wave3 = over_up + over_dn
    mid = pl.multiple_of(fc + z * qc, LANES)
    far = pl.multiple_of(fc + lax.rem(z + 2, nm) * qc, LANES)

    def out_at(start, n):
        return o16.at[:, pl.ds(start, n)], o4.at[:, pl.ds(start, n)]

    back_far = pair(*at((w16, w4), 3, 0, qc), *out_at(mid, qc), 2)
    back_near_up = pair(*at((w16, w4), 2, 0, qc), *out_at(mid, qc), up)
    back_near_dn = pair(*at((w16, w4), 1, 0, qc), *out_at(mid, qc), dn)
    back1 = back_far + back_near_up + back_near_dn

    loads[3].wait()
    raw = jnp.concatenate([idv[...], jnp.zeros((GT - slots, tiles), I32)], axis=0)
    tab[:tiles, :col] = onehot(iota((tiles, col), 0) % GT == iota((tiles, col), 1) % GT).astype(BF16)
    spread = tab[:tiles, :col]
    order = list(range(0, groups, 2)) + list(range(1, groups, 2))

    def regroup(byte):
        byte = byte.astype(F32)
        high = jnp.concatenate(
            [jnp.where(iota((GT, tiles), 1) // GT == g, byte, 0.0) for g in order], axis=0
        ).astype(BF16)
        out = jnp.dot(high, spread, preferred_element_type=F32).reshape(groups, GT, col)
        at_lane = iota((groups, GT, col), 2)
        shift = jnp.where(jnp.logical_and(iota((groups, GT, col), 0) >= pairs, at_lane >= LANES), part, 0)
        keep = iota((groups, GT, col), 1) == (at_lane - shift) // GT
        return jnp.sum(jnp.where(keep, out, 0.0), axis=1)

    ident = regroup(raw // 256) * 256.0 + regroup(raw % 256)
    beyond = jnp.where(iota((pairs, LANES), 1) < part, ident[:pairs, LANES:], ident[pairs:, LANES:])
    ident = jnp.concatenate([ident[:pairs, :LANES], ident[pairs:, :LANES], beyond], axis=1).astype(I32)
    owner = ident // share
    place = ident % share
    code = jnp.left_shift(1, place // LANES).astype(F32) * (1.0 + (place % LANES).astype(F32) / LANES)

    ones = [onehot(iota((ns, two), 0) == owner[g : g + 1]) for g in range(pairs)]
    tab[...] = onehot(iota((two, two), 0) < iota((two, two), 1)).astype(BF16)
    before = jnp.dot(
        jnp.concatenate([a.astype(BF16) for a in ones], axis=0), tab[...], preferred_element_type=F32
    )
    run = jnp.zeros((ns, 1), F32)
    for g in range(pairs):
        rank = jnp.sum(ones[g] * (before[g * ns : (g + 1) * ns] + run), axis=0, keepdims=True)
        run = run + jnp.sum(ones[g], axis=1, keepdims=True)
        rank = rank.astype(I32)
        side = owner[g : g + 1] // hw * LANES
        sel[:, g * two : (g + 1) * two] = onehot(iota((2 * LANES, two), 0) == rank + side).astype(BF16)

    loads[2].wait()
    loads[0].wait()
    loads[1].wait()
    lane = iota((GT, col), 1) % GT
    lane8 = iota((8, col), 1) % GT - iota((8, col), 0) // 4
    row = iota((8, two), 0)
    split_at = hw * GT
    gap = jnp.zeros((col - slots * GT, LANES), BF16)

    def values(g):
        w = wv[:, g].reshape(slots * GT, LANES)
        if g % 2:
            w = jnp.concatenate([w[:LANES], gap, w[LANES:]], axis=0)
        else:
            w = jnp.concatenate([w, gap], axis=0)
        a = e16[:, g * GT * LANES : (g + 1) * GT * LANES]
        b = e4[:, g * GT * LANES : (g + 1) * GT * LANES]
        a = nt(jnp.concatenate([a[:, t * LANES : (t + 1) * LANES] for t in range(GT)], axis=0), w)
        b = nt(jnp.concatenate([b[:, t * LANES : (t + 1) * LANES] for t in range(GT)], axis=0), w)
        first = jnp.zeros((GT, col), F32)
        second = jnp.zeros((8, col), F32)
        for t in range(GT):
            first = jnp.where(lane == t, a[t * GT : (t + 1) * GT], first)
        for t in range(0, GT, 2):
            second = jnp.where(lane8 == t, b[t * 4 : t * 4 + 8], second)
        return first, second[:4] + second[4:]

    def joined(even, odd):
        return jnp.concatenate([even[:, :LANES], odd[:, :LANES], even[:, LANES:] + odd[:, LANES:]], axis=1)

    for g in range(pairs):
        even, odd = values(2 * g), values(2 * g + 1)
        first, second = joined(even[0], odd[0]), joined(even[1], odd[1])
        rest = jnp.concatenate([second, jnp.zeros((20 - own + 4, two), F32)], axis=0)
        rest = jnp.where(row == own - 16, code[g : g + 1], rest)
        here = slice(g * two, (g + 1) * two)
        for o in range(hw):
            there = owner[g : g + 1] % hw == o
            lhs[o * GT : (o + 1) * GT, here] = jnp.where(there, first, 0.0).astype(BF16)
        for o in range(0, hw, 2):
            low = jnp.where(owner[g : g + 1] % hw == o, rest, 0.0)
            high = jnp.where(owner[g : g + 1] % hw == o + 1, rest, 0.0)
            lhs[split_at + o * 8 : split_at + o * 8 + 16, here] = jnp.concatenate(
                [low, high], axis=0
            ).astype(BF16)
        if g % BATCH == BATCH - 1:
            cut = slice((g + 1 - BATCH) * two, (g + 1) * two)
            both = nt(lhs[:, cut], sel[:, cut])
            if g == BATCH - 1:
                acc[...] = both
            else:
                acc[...] += both
        if g == min(START, pairs) - 1:
            pl.semaphore_wait(barrier, nm - 1 + ns - 1)
            for c in wave1:
                c.start()
    eight = iota((8, LANES), 0)
    spot = iota((1, LANES), 1)
    for o in range(ns):
        across = slice(o // hw * LANES, (o // hw + 1) * LANES)
        main = acc[o % hw * GT : (o % hw + 1) * GT, across]
        rest = acc[split_at + o % hw * 8 : split_at + (o % hw + 1) * 8, across]
        p0, p1, p2 = (pltpu.roll(rest, 96 - 32 * t, 1) for t in range(3))
        head = jnp.where(eight < 5, p0, pltpu.roll(p2, 5, 0))
        tail = jnp.where(eight < 5, p1, pltpu.roll(p2, 2, 0))
        pk[o] = jnp.where(spot < 96, main, jnp.concatenate([head, tail], axis=0)).astype(BF16)

    def send(n, carry):
        d = 1 + lax.rem(n + 8, ns - 1)
        pltpu.make_async_remote_copy(
            pk.at[lax.rem(me + d, ns)], rx.at[me], ps.at[0], pr.at[0],
            device_id=plane(d), device_id_type=MESH).start()
        return carry

    packets = pltpu.make_async_remote_copy(
        pk.at[pl.ds(0, ns - 1)], rx.at[pl.ds(0, ns - 1)], ps.at[0], pr.at[0],
        device_id=plane(1), device_id_type=MESH)
    lax.fori_loop(1, ns, send, 0)
    rx[me] = pk[me]
    packets.wait_recv()

    spot = iota((1, LANES), 1)
    power = jnp.left_shift(1, iota((8, LANES), 0)).astype(F32)
    inverse = jnp.left_shift(1, 7 - iota((8, LANES), 0)).astype(F32)
    down = iota((2 * LANES, LANES), 0)
    for i in range(ns // 8):
        left = []
        for q in range(8):
            p = rx[i * 8 + q].astype(F32)
            r1x, r2x, r3x = (pltpu.roll(p, 32 * (t + 1), 1) for t in range(3))
            lines = [p[k : k + 1] for k in range(16)]
            for r in range(own - 15):
                third = 5 + r if r < 3 else 10 + r
                line = jnp.where(spot < 96, r3x[third : third + 1], 0.0)
                line = jnp.where(spot < 64, r2x[8 + r : 9 + r], line)
                lines.append(jnp.where(spot < 32, r1x[r : r + 1], line))
            where = lines.pop()
            upper = where >= 256.0
            where = jnp.where(upper, where * (1.0 / 256.0), where)
            top = jnp.logical_and(where >= power, where < 2.0 * power)
            left.append(
                jnp.concatenate([jnp.where(top, v, 0.0) for v in lines], axis=0).astype(BF16)
            )
            low = where * jnp.sum(jnp.where(top, inverse, 0.0), axis=0, keepdims=True)
            low = low.astype(I32) - LANES + jnp.where(upper, LANES, 0)
            rgt[:, (i * 8 + q) * LANES : (i * 8 + q + 1) * LANES] = onehot(down == low).astype(BF16)
        both = nt(jnp.concatenate(left, axis=1), rgt[:, i * 8 * LANES : (i + 1) * 8 * LANES])
        if i == 0:
            acc2[...] = both
        else:
            acc2[...] += both
    hg[z] = acc2[...].astype(BF16)

    def members_copy(d, n):
        ref = hg.at[z]
        return pltpu.make_async_remote_copy(
            ref, ref, zs.at[n], zr.at[n], device_id=along(d), device_id_type=MESH)

    direct = [members_copy(2, 0), members_copy(up, 1), members_copy(dn, 2)]
    for c in direct:
        c.start()
    for c in first_up + first_dn:
        c.wait_recv()
    for c in wave2:
        c.start()
    for c in direct:
        c.wait_recv()

    loads[4].wait()
    loads[5].wait()
    rows = members * 8
    for c in range(2):
        hf[c * rows : (c + 1) * rows] = hg[:, :, c * LANES : (c + 1) * LANES].astype(F32).reshape(rows, LANES)
    for h in range(8):
        x = jnp.concatenate([hf[pl.ds(c * rows + h, members, stride=8), :] for c in range(2)], axis=1)
        seen = jnp.concatenate([ob[h : h + 1], ob[h + 8 : h + 9]], axis=1)
        weight = jnp.concatenate([va[h : h + 1], va[h + 8 : h + 9]], axis=1)
        ybar = jnp.sum(x, axis=0, keepdims=True) / members
        dev = x - ybar
        cut = [slice((t * 8 + h) * 2 * LANES, (t * 8 + h + 1) * 2 * LANES) for t in range(3)]
        last = jnp.where(iota((LANES - members, 2 * LANES), 0) == 0, seen - ybar, 0.0)
        high, low = split(jnp.concatenate([dev, last], axis=0))
        an[:, cut[0]], an[:, cut[1]], an[:, cut[2]] = high, high, low
        high, low = split(dev * weight)
        wa[:, cut[0]], wa[:, cut[1]], wa[:, cut[2]] = high, low, high
    gr[...] = nt(wa[...], an[...]).reshape(nown, chunk, LANES)

    mine = me // stride
    owns = jnp.logical_and(lax.rem(me, stride) == 0, mine < nown)

    def to_owner(i):
        return pltpu.make_async_remote_copy(
            gr.at[i], rbuf.at[me], s1.at[0], r1.at[0],
            device_id={"state": i * stride}, device_id_type=MESH)

    def tiles_moved(n, src, dst, ss, rs):
        return pltpu.make_async_remote_copy(
            src.at[pl.ds(0, n)], dst.at[pl.ds(0, n)], ss, rs, device_id=plane(1), device_id_type=MESH)

    for i in range(nown):
        @pl.when(me != i * stride)
        def _():
            to_owner(i).start()

    q = iota((members, LANES), 0)
    slot = jnp.where(q < 16 * nm, q // 16, (q - 16 * nm) // (own - 16))
    inner = jnp.where(q < 16 * nm, q % 16, 16 + (q - 16 * nm) % (own - 16))
    dist = jnp.where(slot == 0, 0, jnp.where(slot == 1, nm - 1, slot - 1))
    tab[:members, :LANES] = onehot(iota((members, LANES), 1) == (z + dist) % nm * own + inner).astype(BF16)

    for c in full_up0 + full_dn1:
        c.wait_recv()
    for c in wave3:
        c.start()
    @pl.when(owns)
    def _():
        rbuf[me] = gr[mine]
        tiles_moved(ns - 1, rbuf, rbuf, s1.at[0], r1.at[0]).wait_recv()
        gs[mine] = jnp.sum(rbuf[...], axis=0)

        def send_one(d, carry):
            pltpu.make_async_remote_copy(
                gs.at[mine], gs.at[mine], s2.at[0], r2.at[0],
                device_id=plane(d), device_id_type=MESH).start()
            return carry

        lax.fori_loop(1, ns, send_one, 0)

    for c in near_up + near_dn + pass_up + pass_dn:
        c.wait_recv()
    x4[:, :qc] = jnp.concatenate([e4[:, pl.ds(mid, qc)]] + [q4[r] for r in range(3)], axis=0)

    @pl.when(owns)
    def _():
        tiles_moved(nown - 1, gs, gs, s2.at[0], r2.at[0]).wait_recv()

    @pl.when(jnp.logical_not(owns))
    def _():
        tiles_moved(nown, gs, gs, s2.at[0], r2.at[0]).wait_recv()

    mixing = transform(gs[...].reshape(members, LANES), members, yref, zref).astype(BF16)

    padded = jnp.concatenate([mixing, jnp.zeros((LANES - members, LANES), BF16)], axis=0)
    turned = nt(tab[:members, :LANES], padded).astype(BF16)
    mixp[...] = nt(turned, tab[:members, :LANES]).astype(BF16)

    wide_rows = 16 * nm
    for part in range(2):
        here = slice(part * qh, (part + 1) * qh)
        at_mid = pl.ds(pl.multiple_of(mid + part * qh, LANES), qh)
        x = jnp.concatenate([e16[:, at_mid]] + [q16[r, :, here] for r in range(3)] + [x4[:, here]], axis=0)
        res = jnp.dot(mixp[...], x, preferred_element_type=F32)
        for t in range(nm - 1, 0, -1):
            w16[t, :, here] = res[16 * t : 16 * (t + 1)].astype(BF16)
            w4[t, :, here] = res[wide_rows + (own - 16) * t : wide_rows + (own - 16) * (t + 1)].astype(BF16)
        o16[:, at_mid] = res[:16].astype(BF16)
        o4[:, at_mid] = res[wide_rows : wide_rows + own - 16].astype(BF16)
    for c in back1:
        c.start()

    for c in over_up + over_dn + full_up1 + full_dn0:
        c.wait_recv()
    mine_rows = jnp.concatenate([mixp[:16], mixp[wide_rows:]], axis=0)
    step = fc // FSTEPS
    for i in range(FSTEPS):
        cut = slice(i * step, (i + 1) * step)
        x = jnp.concatenate(
            [e16[:, cut]] + [f16[r, :, cut] for r in range(3)]
            + [e4[:, cut]] + [f4[r, :, cut] for r in range(3)], axis=0)
        res = jnp.dot(mine_rows, x, preferred_element_type=F32)
        o16[:, cut] = res[:16].astype(BF16)
        o4[:, cut] = res[16:own].astype(BF16)

    for c in back1:
        c.wait_recv()
    for c in wave1 + wave2 + wave3 + back1 + direct:
        c.wait_send()
    packets.wait_send()

    @pl.when(owns)
    def _():
        tiles_moved(nown - 1, gr, rbuf, s1.at[0], r1.at[0]).wait_send()
        tiles_moved(ns - 1, rbuf, rbuf, s2.at[0], r2.at[0]).wait_send()

    @pl.when(jnp.logical_not(owns))
    def _():
        tiles_moved(nown, gr, rbuf, s1.at[0], r1.at[0]).wait_send()


def per_device(ns, nm, ensemble, weights, seg_obs, observed, inv_var):
    own, cells = ensemble.shape
    tiles, slots, _ = weights.shape
    share = observed.shape[0] // ns
    members = own * nm
    nown = 10 if ns >= 10 else 2
    groups = tiles // GT
    his = share // LANES
    wts = jnp.transpose(weights, (1, 0, 2)).reshape(slots, groups, GT, LANES)
    ids = jnp.transpose(seg_obs)
    obs = observed.reshape(ns, his, LANES)
    var = inv_var.reshape(ns, his, LANES)
    anyspec = pl.BlockSpec(memory_space=pl.ANY)
    dma = pltpu.SemaphoreType.DMA
    vspec = pl.BlockSpec(memory_space=pltpu.VMEM)
    two = 2 * GT * slots
    fc = cells * FULL // 16
    qc = (cells - fc) // nm
    rest = own - 16
    o16, o4 = pl.pallas_call(
        functools.partial(kernel, ns, nm, own, tiles, slots, share, nown, fc),
        out_shape=(
            pltpu.VMEM((16, cells), BF16),
            pltpu.VMEM((rest, cells), BF16),
        ),
        in_specs=[anyspec] * 5,
        out_specs=(vspec, vspec),
        scratch_shapes=[
            pltpu.VMEM((3, 16, fc), BF16),
            pltpu.VMEM((3, rest, fc), BF16),
            pltpu.VMEM((3, 16, qc), BF16),
            pltpu.VMEM((3, rest, qc), BF16),
            pltpu.VMEM((2, 16, qc // 2), BF16),
            pltpu.VMEM((2, rest, qc // 2), BF16),
            pltpu.VMEM((rest * nm, qc), BF16),
            pltpu.VMEM((nm, 16, qc), BF16),
            pltpu.VMEM((nm, rest, qc), BF16),
            pltpu.VMEM((members, members), BF16),
            pltpu.VMEM((members, LANES), F32),
            pltpu.VMEM((members, LANES), F32),
            pltpu.VMEM((two, two), BF16),
            pltpu.VMEM((2 * LANES, ns * LANES), BF16),
            pltpu.VMEM((16, cells), BF16),
            pltpu.VMEM((own - 16, cells), BF16),
            pltpu.VMEM((slots, groups, GT, LANES), BF16),
            pltpu.VMEM((slots, tiles), I32),
            pltpu.VMEM((his, LANES), F32),
            pltpu.VMEM((his, LANES), F32),
            pltpu.VMEM((ns // 2 * (GT + 8), groups // 2 * two), BF16),
            pltpu.VMEM((2 * LANES, groups // 2 * two), BF16),
            pltpu.VMEM((ns // 2 * (GT + 8), 2 * LANES), F32),
            pltpu.VMEM((ns, GT, LANES), BF16),
            pltpu.VMEM((ns, GT, LANES), BF16),
            pltpu.VMEM((own * 8, 2 * LANES), F32),
            pltpu.VMEM((nm, own * 8, 2 * LANES), BF16),
            pltpu.VMEM((2 * members * 8, LANES), F32),
            pltpu.VMEM((LANES, 3 * share), BF16),
            pltpu.VMEM((members, 3 * share), BF16),
            pltpu.VMEM((nown, members // nown, LANES), F32),
            pltpu.VMEM((ns, members // nown, LANES), F32),
            pltpu.VMEM((nown, members // nown, LANES), F32),
            dma((6,)), dma((36,)), dma((36,)), dma((1,)), dma((1,)),
            dma((3,)), dma((3,)), dma((1,)), dma((1,)), dma((1,)), dma((1,)),
        ],
        compiler_params=pltpu.CompilerParams(collective_id=0, has_side_effects=True),
        name="assimilate",
    )(ensemble, wts, ids, obs, var)
    def settle(o16_ref, o4_ref, out, sem):
        moves = [
            pltpu.make_async_copy(o16_ref, out.at[pl.ds(0, 16)], sem.at[0]),
            pltpu.make_async_copy(o4_ref, out.at[pl.ds(16, rest)], sem.at[1]),
        ]
        for c in moves:
            c.start()
        for c in moves:
            c.wait()

    return pl.pallas_call(
        settle,
        out_shape=jax.ShapeDtypeStruct((own, cells), BF16),
        in_specs=[vspec] * 2,
        out_specs=anyspec,
        scratch_shapes=[dma((2,))],
        name="settle",
    )(*(pltpu.with_memory_space_constraint(o, pltpu.VMEM) for o in (o16, o4)))


def solution(mesh):
    return jax.shard_map(
        functools.partial(per_device, mesh.shape["state"], mesh.shape["mem"]),
        mesh=mesh,
        in_specs=(P("mem", "state"), P("state", None, None), P("state", None), P(), P()),
        out_specs=P("mem", "state"),
        check_vma=False,
    )
```
